32 devices in a mesh: grp: 2 (over y), seq: 4 (over z), zero: 4 (over x, core).
Axes of the slice: x: 2, y: 2, z: 4, core: 2. Of those that a mesh axis runs over, the one named last changes fastest.
Arguments:
- hidden: bfloat16 [8, 512, 1280], P(('grp', 'zero'), 'seq'), parts along dimension 0, may hold values from -6 to 6
- grad_out: bfloat16 [8, 512, 1280], P(('grp', 'zero'), 'seq'), parts along dimension 0, may hold values from -6 to 6
- w_proj: bfloat16 [1280, 148], P('zero'), may hold values from -0.15625 to 0.15625
- conv_w: bfloat16 [4, 1408], P(None, 'zero'), may hold values from -3 to 3
- a_log: float32 [20], replicated, may hold values from -8 to 1, as said below
- dt_bias: float32 [20], replicated, may hold values from -4.5 to -3
Outputs:
- output: bfloat16 [8, 512, 1280], P(('grp', 'zero'), 'seq'), parts along dimension 0
- grad_hidden: bfloat16 [8, 512, 1280], P(('grp', 'zero'), 'seq'), parts along dimension 0
- grad_proj: float32 [2560, 148], P(('grp', 'zero')), parts along dimension 0
- grad_conv: float32 [8, 1408], P('grp', 'zero'), parts along dimension 0
- grad_heads: float32 [4, 20], P('grp'), parts along dimension 0
The draws below stay inside these ranges and needn't reach their ends.
There are 2 independent parts, one for each index of `grp`. The reference program is written for one: setup_inputs(seed, part) draws one part's arguments, and reference() takes and returns one part's arrays. A program takes and returns all parts, laid end to end along the dimension named above; an argument that names none is the same for every part. Nothing has to cross between parts.
Inputs may be any that keep to these rules, and one draw needn't show every extreme that they name: `a_log`: the logarithms of the heads' decay rates.
All inputs are finite; a program needn't handle non-finite values.
Results may differ from the reference program's by a relative error of at most 0.017.
Values may be sent and summed in bfloat16 or wider, within the bound.
A program may use at most 192 MiB of HBM per device.

```python
import math
import jax
import jax.numpy as jnp
from jax import lax

WIDTH = 1280
STATE = 64
HEAD_DIM = 64
SPAN = 128
KERNEL = 4
HEADS = 20
SEQ_LEN = 512
SEQS = 4


def draw_a_log(key, part):
    picked = jax.random.uniform(jax.random.fold_in(key, 11), (HEADS,))
    slow_rates = jax.random.uniform(jax.random.fold_in(key, 12), (HEADS,), minval=math.log(10.0 / SEQ_LEN), maxval=math.log(40.0 / SEQ_LEN))
    fast_rates = jax.random.uniform(jax.random.fold_in(key, 13), (HEADS,), minval=math.log(0.6), maxval=math.log(2.0))
    share = 0.5
    return jnp.where(picked < share, slow_rates, fast_rates).astype(jnp.float32)


def spiked(values, key, source, target, blocks, factor):
    owner, partner = [(jnp.arange(values.shape[dim]) // (values.shape[dim] // blocks)).reshape([-1 if axis == dim else 1 for axis in range(values.ndim)]) for dim in (source, target)]
    chosen = jax.random.permutation(key, blocks)[partner]
    strong = (owner == chosen) | (owner == (partner + blocks // 2) % blocks)
    return jnp.where(strong, factor * values, values)


def block_levels(own_key, dims, shards, low, top_value):
    def one(axis_at, parts):
        draws = jax.random.uniform(jax.random.fold_in(jax.random.fold_in(own_key, 6), axis_at), (parts,), jnp.float32, low / len(shards), top_value / len(shards))
        return jnp.repeat(jnp.exp(draws), dims[axis_at] // parts).reshape((-1,) + (1,) * (len(dims) - axis_at - 1))

    factor_of = one(*shards[0])
    for cut in shards[1:]:
        factor_of = factor_of * one(*cut)
    return factor_of


def centred(own_key, shape, scale, most, cuts=(), dtype=jnp.bfloat16):
    array = scale * jax.random.normal(own_key, shape, jnp.float32)
    if cuts:
        array = array * block_levels(own_key, shape, cuts, -0.22, 0.18)
    return jnp.clip(array, -most, most).astype(dtype)


def bell_draw_with(own_key, extent, scale, bound, split, heavy, held_as=jnp.bfloat16):
    entries = scale * jax.random.normal(own_key, extent, jnp.float32)
    if split:
        entries = entries * block_levels(own_key, extent, split, -0.22, 0.18)
    return jnp.clip(spiked(entries, jax.random.fold_in(own_key, 3), *heavy), -bound, bound).astype(held_as)


def setup_inputs(seed: int = 0, part: int = 0) -> dict:
    key_of = jax.random.split(jax.random.key(seed), 7)
    part_keys = jax.random.split(jax.random.fold_in(key_of[6], part), 7)
    return {
        "hidden": bell_draw_with(part_keys[0], (SEQS, SEQ_LEN, WIDTH), 1.0, 6.0, ((0, 4), (1, 4)), (0, 2, 4, 2.0)),
        "grad_out": centred(part_keys[1], (SEQS, SEQ_LEN, WIDTH), 1.0, 6.0, ((0, 4), (1, 4))),
        "w_proj": centred(key_of[2], (WIDTH, 2 * STATE + HEADS), WIDTH ** -0.5, 0.15625, ((0, 4),)),
        "conv_w": centred(key_of[3], (KERNEL, WIDTH + 2 * STATE), KERNEL ** -0.5, 3.0, ((1, 4),)),
        "a_log": draw_a_log(jax.random.fold_in(key_of[6], 71), part),
        "dt_bias": jnp.clip(jax.random.uniform(key_of[5], (HEADS,), jnp.float32, -4.5, -3.0), -4.5, -3.0),
    }


def conv_core(ahead_in, dt_raw, filters, a_log, dt_bias):
    length = dt_raw.shape[0]
    head_count = dt_raw.shape[1]
    blocks = length // SPAN
    mixed_sum = filters[0] * ahead_in[KERNEL - 1:KERNEL - 1 + length]
    for step_back in range(1, KERNEL):
        mixed_sum = mixed_sum + filters[step_back] * ahead_in[KERNEL - 1 - step_back:KERNEL - 1 - step_back + length]
    active = jax.nn.silu(mixed_sum)
    values = active[:, :WIDTH].astype(jnp.bfloat16).reshape(blocks, SPAN, head_count, HEAD_DIM)
    b_mat = active[:, WIDTH:WIDTH + STATE].astype(jnp.bfloat16).reshape(blocks, SPAN, STATE)
    c_mat = active[:, WIDTH + STATE:].astype(jnp.bfloat16)
    c_blocks = c_mat.reshape(blocks, SPAN, STATE)
    steps_dt = jax.nn.softplus(dt_raw + dt_bias)
    log_decay = -jnp.exp(a_log) * steps_dt
    within = jnp.cumsum(log_decay.reshape(blocks, SPAN, head_count), axis=1).transpose(0, 2, 1)
    dt_blocks = steps_dt.reshape(blocks, SPAN, head_count).transpose(0, 2, 1)
    scores = jnp.einsum('kin,kjn->kij', c_blocks.astype(jnp.float32), b_mat.astype(jnp.float32))
    causal = jnp.arange(SPAN)[:, None] >= jnp.arange(SPAN)[None, :]
    gap_log = within[:, :, :, None] - within[:, :, None, :]
    decays = jnp.exp(jnp.where(causal, gap_log, -jnp.inf))
    weights = (scores[:, None] * decays * dt_blocks[:, :, None, :]).astype(jnp.bfloat16)
    y_intra = jnp.einsum('khij,kjhp->kihp', weights.astype(jnp.float32), values.astype(jnp.float32))
    to_end = jnp.exp(within[:, :, -1:] - within) * dt_blocks
    b_weighted = (to_end[..., None] * b_mat[:, None, :, :].astype(jnp.float32)).astype(jnp.bfloat16)
    states = jnp.einsum('khjn,kjhp->khnp', b_weighted.astype(jnp.float32), values.astype(jnp.float32))
    totals = within[:, :, -1]

    def advance(carried, current):
        return (jnp.exp(current[0])[:, None, None] * carried + current[1], carried)
    last_state, entering = lax.scan(advance, jnp.zeros(states.shape[1:], jnp.float32), (totals, states))
    y_inter = jnp.einsum('kin,khnp->kihp', c_blocks.astype(jnp.float32), entering, precision=lax.Precision.HIGHEST)
    y_inter = y_inter * jnp.exp(within).transpose(0, 2, 1)[..., None]
    return (y_intra + y_inter).reshape(length, WIDTH)

def strand(tokens, cotangent, w_proj, filters, a_log, dt_bias):
    projected = jnp.dot(tokens, w_proj, preferred_element_type=jnp.float32)
    inner_act = jnp.concatenate([tokens, projected[:, :2 * STATE].astype(jnp.bfloat16)], axis=1)
    dt_raw = projected[:, 2 * STATE:]
    margin = KERNEL - 1

    def both_ways(inner_f32, dt_vals, filt, decay_log, bias):
        ahead_in = jnp.pad(inner_f32, ((margin, 0), (0, 0)))
        behind = jnp.pad(jnp.flip(inner_f32, axis=0), ((margin, 0), (0, 0)))
        y_ahead = conv_core(ahead_in, dt_vals, filt, decay_log, bias)
        y_behind = conv_core(behind, jnp.flip(dt_vals, axis=0), filt, decay_log, bias)
        return y_ahead + jnp.flip(y_behind, axis=0)
    total, pullback = jax.vjp(both_ways, inner_act.astype(jnp.float32), dt_raw, filters, a_log, dt_bias)
    result = total.astype(jnp.bfloat16)
    grad_inner32, grad_dt, grad_filt, grad_alog, grad_bias = pullback(cotangent.astype(jnp.float32))
    grad_inner = grad_inner32.astype(jnp.bfloat16)
    grad_projected = jnp.concatenate([grad_inner[:, WIDTH:], grad_dt.astype(jnp.bfloat16)], axis=1)
    grad_weight = jnp.dot(tokens.T, grad_projected, preferred_element_type=jnp.float32)
    grad_tokens = (grad_inner[:, :WIDTH].astype(jnp.float32) + jnp.dot(grad_projected, w_proj.T, preferred_element_type=jnp.float32)).astype(jnp.bfloat16)
    return (result, grad_tokens, grad_weight, grad_filt, jnp.stack([grad_alog, grad_bias]))

def reference(hidden, grad_out, w_proj, conv_w, a_log, dt_bias):
    filters = conv_w.astype(jnp.float32)

    def one_sequence(pieces):
        tokens, cotangent = pieces
        first = strand(tokens, cotangent, w_proj, filters, a_log, dt_bias)
        second = strand(jnp.flip(tokens, axis=1), jnp.flip(cotangent, axis=1), w_proj, filters, a_log, dt_bias)
        merged = (first[0].astype(jnp.float32) + jnp.flip(second[0], axis=1).astype(jnp.float32)).astype(jnp.bfloat16)
        grad_tok = (first[1].astype(jnp.float32) + jnp.flip(second[1], axis=1).astype(jnp.float32)).astype(jnp.bfloat16)
        return (merged, grad_tok, first[2] + second[2], first[3] + second[3], first[4] + second[4])
    outs = lax.map(one_sequence, (hidden, grad_out))
    return (outs[0], outs[1], lax.optimization_barrier(jnp.sum(outs[2], axis=0)), lax.optimization_barrier(jnp.sum(outs[3], axis=0)), lax.optimization_barrier(jnp.sum(outs[4], axis=0)))
```

```python
import functools
import jax
import jax.numpy as jnp
from jax import lax
from jax.experimental import pallas as pl
from jax.experimental.pallas import tpu as pltpu
from jax.sharding import PartitionSpec as P

WIDTH = 1280
STATE = 64
HEAD_DIM = 64
SPAN = 128
KERNEL = 4
HEADS = 20
PAIRS = WIDTH // 128
CHANNELS = WIDTH + 2 * STATE
EDGE = 8
EXT = SPAN + 2 * EDGE
F32 = jnp.float32
BF16 = jnp.bfloat16
LOW = -1e30
COMBOS = ((0, 0), (0, 1), (1, 0), (1, 1))


def mm(a, b):
    return jnp.dot(a, b, preferred_element_type=F32)


def mm_nt(a, b):
    return lax.dot_general(a, b, (((1,), (1,)), ((), ())), preferred_element_type=F32)


def mm_tn(a, b):
    return lax.dot_general(a, b, (((0,), (0,)), ((), ())), preferred_element_type=F32)


def exact(a, b):
    return jnp.dot(a, b, preferred_element_type=F32, precision=lax.Precision.HIGHEST)


def iota(dim, shape=(128, 128)):
    return lax.broadcasted_iota(jnp.int32, shape, dim)


def mirror(dtype=BF16):
    return jnp.where(iota(0) + iota(1) == 127, 1.0, 0.0).astype(dtype)


def col(x, h):
    return jnp.sum(jnp.where(iota(1) == h, x, 0.0), axis=1, keepdims=True)


def softplus(x):
    return jnp.maximum(x, 0.0) + jnp.log1p(jnp.exp(-jnp.abs(x)))


def sigmoid(x):
    return 1.0 / (1.0 + jnp.exp(-x))


def head_of(strand, pair, r):
    return 2 * pair + r if strand == 0 else HEADS - 1 - 2 * pair - r


def shifted(x):
    back = [x[EDGE : EDGE + SPAN]]
    fore = [back[0]]
    for k in range(1, KERNEL):
        back.append(pltpu.roll(x, k, 0)[EDGE : EDGE + SPAN])
        fore.append(pltpu.roll(x, EXT - k, 0)[EDGE : EDGE + SPAN])
    return back, fore


def conv(taps, rows):
    out = taps[0:1] * rows[0]
    for k in range(1, KERNEL):
        out = out + taps[k : k + 1] * rows[k]
    return out


def conv_back(taps, dm, direction):
    zero = jnp.zeros((EDGE, 128), F32)
    wide = jnp.concatenate([zero, dm, zero], axis=0)
    out = taps[0:1] * wide
    for k in range(1, KERNEL):
        out = out + taps[k : k + 1] * pltpu.roll(wide, EXT - k if direction == 0 else k, 0)
    return out


def tap_grads(dm, rows):
    parts = [jnp.sum(dm * rows[k], axis=0, keepdims=True) for k in range(KERNEL)]
    return jnp.concatenate(parts + [jnp.zeros((8 - KERNEL, 128), F32)], axis=0)


def last_row(x, direction):
    return x[SPAN - 1 : SPAN] if direction == 0 else x[0:1]


def lanes(i):
    return pl.ds(pl.multiple_of(i * 128, 128), 128)


def first_kernel(
    x_ref, go_ref, w_ref, f_ref, alog_ref, bias_ref,
    up_ref, down_ref, dup_ref, ddown_ref, wr_ref, bcx_ref, dtx_ref, within_ref,
    tow_t, e_col, bc_t,
):
    flip = mirror()
    for b in range(PAIRS):
        wr_ref[b * 128 : (b + 1) * 128] = mm(
            flip, w_ref[(PAIRS - 1 - b) * 128 : (PAIRS - b) * 128]
        ).astype(BF16)
    x_all = x_ref[...]
    rate = jnp.exp(alog_ref[...])
    for s in range(2):
        proj = mm(x_all, w_ref[...] if s == 0 else wr_ref[...])
        bcx = proj[:, :128].astype(BF16).astype(F32)
        bcx_ref[s] = bcx
        dtx = proj[EDGE : EDGE + SPAN, 128:] + bias_ref[...]
        dtx_ref[s] = dtx
        delta = softplus(dtx)
        rows = shifted(bcx)
        for d in range(2):
            c = 2 * s + d
            tri = iota(0) >= iota(1) if d == 0 else iota(0) <= iota(1)
            within = exact(jnp.where(tri, 1.0, 0.0), -rate * delta)
            within_ref[c] = within
            mixed = conv(f_ref[:, WIDTH:], rows[d])
            act = (mixed * sigmoid(mixed)).astype(BF16).astype(F32)
            bc_t[c] = act.T
            tow_t[c] = (jnp.exp(last_row(within, d) - within) * delta).T
            e_col[c] = jnp.exp(within)

    own_refs = (up_ref, down_ref)
    dec_refs = (dup_ref, ddown_ref)

    def pair_step(i, carry):
        x = x_ref[:, lanes(i)].astype(F32)
        g = go_ref[:, lanes(i)].astype(F32)
        rows = shifted(x)
        taps = (
            f_ref[:, lanes(i)],
            mm(f_ref[:, lanes(PAIRS - 1 - i)].astype(BF16), flip),
        )
        low = iota(1) < HEAD_DIM
        low_half = iota(1, (STATE, 128)) < HEAD_DIM
        for s, d in COMBOS:
            c = 2 * s + d
            mixed = conv(taps[s], rows[d])
            values = (mixed * sigmoid(mixed)).astype(BF16)
            heads = [head_of(s, i, r) for r in range(2)]
            b_t = bc_t[c, 0:STATE]
            bw = jnp.concatenate(
                [b_t * tow_t[c, pl.ds(h, 1), :] for h in heads], axis=0
            ).astype(BF16)
            st = mm(bw, values)
            own_refs[d][i, s] = jnp.where(low_half, st[:STATE], st[STATE:])
            e = e_col[c]
            e0, e1 = [col(e, h) for h in heads]
            e_pair = jnp.where(low, e0, e1)
            own_refs[1 - d][i, 2 + s] = mm(
                bc_t[c, STATE:128].astype(BF16), (e_pair * g).astype(BF16)
            )
            decay = jnp.broadcast_to(last_row(e_pair, d), (8, 128))
            dec_refs[d][i, s] = decay
            dec_refs[1 - d][i, 2 + s] = decay
        return carry

    lax.fori_loop(0, PAIRS, pair_step, 0)


def main_kernel(
    x_ref, go_ref, f_ref, alog_ref, bcx_ref, dtx_ref, within_ref, up_ref, down_ref,
    out_ref, gi_ref, gf_ref, ddt_ref, heads_ref,
    e_col, f_col, tow, within_t, delta_t, score, d_score, d_b, d_c, d_l, d_lt, d_dc, d_dt, bc_act,
):
    flip = mirror()
    rate = jnp.exp(alog_ref[...])
    for s in range(2):
        delta = softplus(dtx_ref[s])
        delta_t[s] = delta.T
        rows = shifted(bcx_ref[s])
        d_dc[s] = jnp.zeros((128, 128), F32)
        d_dt[s] = jnp.zeros((128, 128), F32)
        for d in range(2):
            c = 2 * s + d
            within = within_ref[c]
            within_t[c] = within.T
            e_col[c] = jnp.exp(within)
            f = jnp.exp(last_row(within, d) - within)
            f_col[c] = f
            tow[c] = f * delta
            mixed = conv(f_ref[:, WIDTH:], rows[d])
            act = (mixed * sigmoid(mixed)).astype(BF16)
            bc_act[c, 0] = act[:, :STATE].astype(F32)
            bc_act[c, 1] = act[:, STATE:].astype(F32)
            score[c] = mm_nt(act[:, STATE:], act[:, :STATE])
            d_score[c] = jnp.zeros((128, 128), F32)
            d_l[c] = jnp.zeros((128, 128), F32)
            d_lt[c] = jnp.zeros((128, 128), F32)
            d_b[c] = jnp.zeros((128, STATE), F32)
            d_c[c] = jnp.zeros((128, STATE), F32)

    def pair_step(i, carry):
        x = x_ref[:, lanes(i)].astype(F32)
        go = go_ref[:, lanes(i)]
        g = go.astype(F32)
        rows = shifted(x)
        taps = (
            f_ref[:, lanes(i)],
            mm(f_ref[:, lanes(PAIRS - 1 - i)].astype(BF16), flip),
        )
        lane = iota(1)
        low = lane < HEAD_DIM
        low_half = iota(1, (STATE, 128)) < HEAD_DIM
        none = jnp.zeros((128, 128), BF16)
        g_two = jnp.concatenate([jnp.where(low, go, none), jnp.where(low, none, go)], axis=0)
        strands = []
        for s in range(2):
            y = jnp.zeros((128, 128), F32)
            gi = jnp.zeros((EXT, 128), F32)
            gf = jnp.zeros((8, 128), F32)
            heads = [head_of(s, i, r) for r in range(2)]
            delta_r = [delta_t[s, pl.ds(h, 1), :] for h in heads]
            for d in range(2):
                c = 2 * s + d
                end = SPAN - 1 if d == 0 else 0
                keep = iota(0) >= lane if d == 0 else iota(0) <= lane
                mixed = conv(taps[s], rows[d])
                sig = sigmoid(mixed)
                values = (mixed * sig).astype(BF16)
                b_mat, c_mat = bc_act[c, 0], bc_act[c, 1]
                within = within_ref[c]
                e_all, f_all, tow_all = e_col[c], f_col[c], tow[c]
                sc = score[c]
                decays, sds, ws, tows, fs, es = [], [], [], [], [], []
                for r, h in enumerate(heads):
                    gap = jnp.where(keep, col(within, h) - within_t[c, pl.ds(h, 1), :], LOW)
                    decay = jnp.exp(gap)
                    decays.append(decay)
                    sds.append(sc * decay)
                    ws.append((sds[r] * delta_r[r]).astype(BF16))
                    tows.append(col(tow_all, h))
                    fs.append(col(f_all, h))
                    es.append(col(e_all, h))
                e_pair = jnp.where(low, es[0], es[1])
                ge = (e_pair * g).astype(BF16)
                ahead, behind = (up_ref, down_ref) if d == 0 else (down_ref, up_ref)
                s_in, g_in = ahead[i, s], behind[i, 2 + s]
                y_two = mm(jnp.concatenate(ws, axis=0), values)
                inter = mm(c_mat.astype(BF16), s_in) * e_pair
                y = y + jnp.where(low, y_two[:128], y_two[128:]) + inter
                d_w = mm_nt(g_two, values)
                bws = jnp.concatenate([(t * b_mat).astype(BF16) for t in tows], axis=0)
                dv_state = mm(bws, g_in)
                dv = jnp.where(
                    low,
                    mm_tn(ws[0], go) + dv_state[:128],
                    mm_tn(ws[1], go) + dv_state[128:],
                )
                v_two = jnp.concatenate(
                    [jnp.where(low, values, none), jnp.where(low, none, values)], axis=0
                )
                d_bw = mm_nt(v_two, g_in)
                d_c[c] += mm_nt(ge, s_in)
                q = g * inter
                both = jnp.sum(g_in.astype(F32) * s_in.astype(F32), axis=0, keepdims=True)
                ends = both * last_row(e_pair, d)
                low_row = iota(1, (1, 128)) < HEAD_DIM
                ds = d_score[c]
                db = d_b[c]
                dl = d_l[c]
                dd = d_dc[s]
                for r, h in enumerate(heads):
                    mine = low if r == 0 else ~low
                    mine_row = low_row if r == 0 else ~low_row
                    dw = d_w[128 * r : 128 * r + 128]
                    rr = dw * sds[r]
                    rows_sum = jnp.sum(rr * delta_r[r], axis=1, keepdims=True)
                    cols_sum = jnp.sum(rr, axis=0, keepdims=True)
                    d_dt[s, pl.ds(h, 1), :] += cols_sum
                    d_lt[c, pl.ds(h, 1), :] -= cols_sum * delta_r[r]
                    ds = ds + dw * decays[r] * delta_r[r]
                    dbw = d_bw[128 * r : 128 * r + 128]
                    d_tow = jnp.sum(dbw * b_mat, axis=1, keepdims=True)
                    db = db + tows[r] * dbw
                    dd = dd + jnp.where(lane == h, d_tow * fs[r], 0.0)
                    t = d_tow * tows[r]
                    total = jnp.sum(t, axis=0, keepdims=True) + jnp.sum(
                        jnp.where(mine_row, ends, 0.0), axis=1, keepdims=True
                    )
                    q_sum = jnp.sum(jnp.where(mine, q, 0.0), axis=1, keepdims=True)
                    at_end = jnp.where(iota(0, (128, 1)) == end, total, 0.0)
                    dl = dl + jnp.where(lane == h, rows_sum - t + q_sum + at_end, 0.0)
                d_score[c] = ds
                d_b[c] = db
                d_l[c] = dl
                d_dc[s] = dd
                dact = dv.astype(BF16).astype(F32)
                dm = dact * (sig * (1.0 + mixed * (1.0 - sig)))
                gf = gf + tap_grads(dm, rows[d])
                gi = gi + conv_back(taps[s], dm, d)
            strands.append(y.astype(BF16).astype(F32))
            gi_ref[s, :, lanes(i)] = gi
            gf_ref[s, :, lanes(i)] = gf
        out_ref[:, lanes(i)] = (strands[0] + strands[1]).astype(BF16)
        return carry

    lax.fori_loop(0, PAIRS, pair_step, 0)

    d_alog = jnp.zeros((1, 128), F32)
    d_bias = jnp.zeros((1, 128), F32)
    for s in range(2):
        rows = shifted(bcx_ref[s])
        dtx = dtx_ref[s]
        log_decay = -rate * softplus(dtx)
        d_delta = d_dc[s] + d_dt[s].T
        gi = jnp.zeros((EXT, 128), F32)
        gf = jnp.zeros((8, 128), F32)
        taps = f_ref[:, WIDTH:]
        for d in range(2):
            c = 2 * s + d
            tri = iota(0) <= iota(1) if d == 0 else iota(0) >= iota(1)
            d_log = exact(jnp.where(tri, 1.0, 0.0), d_l[c] + d_lt[c].T)
            d_delta = d_delta - rate * d_log
            d_alog = d_alog + jnp.sum(d_log * log_decay, axis=0, keepdims=True)
            ds = d_score[c].astype(BF16)
            dc = d_c[c] + mm(ds, bc_act[c, 0].astype(BF16))
            db = d_b[c] + mm_tn(ds, bc_act[c, 1].astype(BF16))
            dact = jnp.concatenate([db, dc], axis=1).astype(BF16).astype(F32)
            mixed = conv(taps, rows[d])
            sig = sigmoid(mixed)
            dm = dact * (sig * (1.0 + mixed * (1.0 - sig)))
            gf = gf + tap_grads(dm, rows[d])
            gi = gi + conv_back(taps, dm, d)
        d_raw = d_delta * sigmoid(dtx)
        ddt_ref[s] = d_raw.astype(BF16)
        d_bias = d_bias + jnp.sum(d_raw, axis=0, keepdims=True)
        gi_ref[s, :, WIDTH:] = gi
        gf_ref[s, :, WIDTH:] = gf
    heads_ref[...] = jnp.concatenate([d_alog, d_bias, jnp.zeros((6, 128), F32)], axis=0)


MESH = pl.DeviceIdType.MESH


def greet_all(sizes):
    barrier = pltpu.get_barrier_semaphore()
    for axis, size in sizes:
        me = lax.axis_index(axis)
        for k in range(1, size):
            pl.semaphore_signal(
                barrier, inc=1, device_id={axis: lax.rem(me + k, size)}, device_id_type=MESH
            )
    pl.semaphore_wait(barrier, sum(size - 1 for _, size in sizes))


def push(src, dst, send, recv, axis, peer):
    return pltpu.make_async_remote_copy(
        src_ref=src,
        dst_ref=dst,
        send_sem=send,
        recv_sem=recv,
        device_id={axis: peer},
        device_id_type=MESH,
    )


def greet_sides(me, count, more=0):
    barrier = pltpu.get_barrier_semaphore()
    for k in (1, count - 1):
        pl.semaphore_signal(
            barrier, inc=1, device_id={"seq": lax.rem(me + k, count)}, device_id_type=MESH
        )
    pl.semaphore_wait(barrier, 2 + more)


def gather_kernel(
    shards, count, hid_ref, w_ref, c_ref, x_ref, w_out, f_out,
    w_slots, c_own, c_slots, before, after, send, recv, sides,
):
    seq, zero = lax.axis_index("seq"), lax.axis_index("zero")
    barrier = pltpu.get_barrier_semaphore()
    for k in range(1, shards):
        pl.semaphore_signal(
            barrier, inc=1, device_id={"zero": lax.rem(zero + k, shards)}, device_id_type=MESH
        )
    greet_sides(seq, count, shards - 1)
    up = push(
        hid_ref.at[pl.ds(SPAN - 2 * EDGE, 2 * EDGE)], before, sides.at[0], sides.at[1], "seq",
        lax.rem(seq + 1, count),
    )
    down = push(
        hid_ref.at[pl.ds(0, 2 * EDGE)], after, sides.at[2], sides.at[3], "seq",
        lax.rem(seq + count - 1, count),
    )

    @pl.when(seq < count - 1)
    def _():
        up.start()

    @pl.when(seq > 0)
    def _():
        down.start()

    c_own[...] = jnp.zeros_like(c_own)
    c_own[:KERNEL] = c_ref[...].astype(F32)
    copies = []
    for k in range(1, shards):
        peer = lax.rem(zero + k, shards)
        copies.append(push(w_ref, w_slots.at[zero], send.at[k, 0], recv.at[k, 0], "zero", peer))
        copies.append(push(c_own, c_slots.at[zero], send.at[k, 1], recv.at[k, 1], "zero", peer))
    for copy in copies:
        copy.start()
    w_slots[zero] = w_ref[...]
    c_slots[zero] = c_own[...]
    w_out[:, 128:] = jnp.zeros((WIDTH, 128), BF16)
    x_ref[EDGE : EDGE + SPAN] = hid_ref[...]

    @pl.when(seq == 0)
    def _():
        x_ref[:EDGE] = jnp.zeros((EDGE, WIDTH), BF16)

    @pl.when(seq > 0)
    def _():
        up.wait_recv()
        x_ref[:EDGE] = before[EDGE:]

    @pl.when(seq == count - 1)
    def _():
        x_ref[EDGE + SPAN :] = jnp.zeros((EDGE, WIDTH), BF16)

    @pl.when(seq < count - 1)
    def _():
        down.wait_recv()
        x_ref[EDGE + SPAN :] = after[:EDGE]

    for copy in copies:
        copy.wait()
    rows, columns = w_ref.shape
    part = c_ref.shape[1]
    for z in range(shards):
        w_out[z * rows : (z + 1) * rows, :columns] = w_slots[z]
        f_out[:, z * part : (z + 1) * part] = c_slots[z]

    @pl.when(seq < count - 1)
    def _():
        up.wait_send()

    @pl.when(seq > 0)
    def _():
        down.wait_send()


def exchange_kernel(
    count, own_up, own_down, dec_up, dec_down, up_ref, down_ref,
    in_slots, out_slots, send, recv,
):
    seq = lax.axis_index("seq")
    greet_sides(seq, count)

    chains = (
        (0, seq, seq + 1, own_up, dec_up, up_ref),
        (1, count - 1 - seq, seq - 1, own_down, dec_down, down_ref),
    )

    def copy_of(d, i, peer):
        return push(
            out_slots.at[d, i], in_slots.at[d, i], send.at[d, i], recv.at[d, i], "seq", peer
        )

    def step(t, carry):
        for d, place, peer, own, dec, _ in chains:
            i = t - place

            @pl.when((i >= 0) & (i < PAIRS))
            def _():
                @pl.when(place == 0)
                def _():
                    out_slots[d, i] = own[i].astype(BF16)

                @pl.when(place > 0)
                def _():
                    copy_of(d, i, seq).wait_recv()

                @pl.when((place > 0) & (place < count - 1))
                def _():
                    out_slots[d, i] = (
                        own[i] + dec[i, :, :1] * in_slots[d, i].astype(F32)
                    ).astype(BF16)

                @pl.when(place < count - 1)
                def _():
                    copy_of(d, i, peer).start()

        return carry

    lax.fori_loop(0, PAIRS + count - 1, step, 0)
    for d, place, peer, _, _, ref in chains:
        @pl.when(place == 0)
        def _():
            ref[...] = jnp.zeros_like(ref)

        @pl.when(place > 0)
        def _():
            ref[...] = in_slots[d]

        @pl.when(place < count - 1)
        def _():
            for i in range(PAIRS):
                copy_of(d, i, peer).wait_send()


def last_kernel(
    shards, count, fold,
    hid_ref, w_ref, wr_ref, gi_ref, ddt_ref, gf_ref, heads_ref,
    gh_ref, gw_ref, gc_ref, gd_ref,
    before, after, parts, part_in, mine, chunk_in, full, total, small, small_in, small2, small2_in,
    taps, sides, zs, zr, ss, sr,
):
    seq, zero = lax.axis_index("seq"), lax.axis_index("zero")
    rows = WIDTH // shards
    fold_rows = rows // fold
    chunk = mine.shape[0] // count
    greet_all((("zero", shards), ("seq", count)))
    up = push(
        gi_ref.at[:, pl.ds(EDGE + SPAN, EDGE)], before, sides.at[0], sides.at[1], "seq",
        lax.rem(seq + 1, count),
    )
    down = push(
        gi_ref.at[:, pl.ds(0, EDGE)], after, sides.at[2], sides.at[3], "seq",
        lax.rem(seq + count - 1, count),
    )

    @pl.when(seq < count - 1)
    def _():
        up.start()

    @pl.when(seq > 0)
    def _():
        down.start()

    @pl.when(seq == 0)
    def _():
        before[...] = jnp.zeros_like(before)

    @pl.when(seq == count - 1)
    def _():
        after[...] = jnp.zeros_like(after)

    flip = mirror()
    small[...] = jnp.zeros_like(small)
    for i in range(PAIRS):
        at = slice(i * 128, i * 128 + 128)
        other = slice((PAIRS - 1 - i) * 128, (PAIRS - i) * 128)
        block = gf_ref[0, :, at] + exact(gf_ref[1, :, other], mirror(F32))
        small[KERNEL * i : KERNEL * i + KERNEL] = block[:KERNEL]
    block = gf_ref[0, :, WIDTH:] + gf_ref[1, :, WIDTH:]
    small[KERNEL * PAIRS : KERNEL * PAIRS + KERNEL] = block[:KERNEL]
    small[KERNEL * PAIRS + KERNEL : KERNEL * PAIRS + KERNEL + 2] = heads_ref[:2]
    first = []
    for k in range(1, shards):
        peer = lax.rem(zero + k, shards)
        copy = push(small, small_in.at[zero], zs.at[1, k], zr.at[1, k], "zero", peer)
        copy.start()
        first.append(copy)
    small_in[zero] = small[...]

    @pl.when(seq > 0)
    def _():
        up.wait_recv()

    @pl.when(seq < count - 1)
    def _():
        down.wait_recv()

    def own(s, at):
        top = gi_ref[s, EDGE : 2 * EDGE, at] + before[s, :, at]
        low = gi_ref[s, SPAN : SPAN + EDGE, at] + after[s, :, at]
        return jnp.concatenate([top, gi_ref[s, 2 * EDGE : SPAN, at], low], axis=0).astype(BF16)

    gps = [
        jnp.concatenate([own(s, slice(WIDTH, CHANNELS)), ddt_ref[s]], axis=1) for s in range(2)
    ]
    for i in range(PAIRS):
        at = slice(i * 128, i * 128 + 128)
        other = slice((PAIRS - 1 - i) * 128, (PAIRS - i) * 128)
        hid_flip = mm(hid_ref[:, other], flip).astype(BF16)
        total[at] = mm_tn(hid_ref[:, at], gps[0]) + mm_tn(hid_flip, gps[1])
    for z in range(shards):
        parts[z, :rows] = total[z * rows : (z + 1) * rows, :128].astype(BF16)
        folded = jnp.zeros((fold_rows, 128), F32)
        for q in range(fold):
            start = z * rows + q * fold_rows
            piece = total[start : start + fold_rows, 128:]
            folded = folded + (pltpu.roll(piece, 32 * q, 1) if q else piece)
        parts[z, rows : rows + fold_rows] = folded.astype(BF16)
        spare = parts.shape[1] - rows - fold_rows
        if spare:
            parts[z, rows + fold_rows :] = jnp.zeros((spare, 128), BF16)
    scatter = []
    for k in range(1, shards):
        peer = lax.rem(zero + k, shards)
        copy = push(parts.at[peer], part_in.at[k], zs.at[0, k], zr.at[0, k], "zero", peer)
        copy.start()
        scatter.append(copy)
    for copy in first:
        copy.wait()
    small2[...] = small_in[0]
    for z in range(1, shards):
        small2[...] += small_in[z]
    second = []
    for k in range(1, count):
        peer = lax.rem(seq + k, count)
        copy = push(small2, small2_in.at[seq], ss.at[0, k], sr.at[0, k], "seq", peer)
        copy.start()
        second.append(copy)
    small2_in[seq] = small2[...]
    for i in range(PAIRS):
        at = slice(i * 128, i * 128 + 128)
        a = (own(0, at).astype(F32) + mm_nt(gps[0], w_ref[at])).astype(BF16)
        b = (own(1, at).astype(F32) + mm_nt(gps[1], wr_ref[at])).astype(BF16)
        gh_ref[:, at] = (a.astype(F32) + b.astype(F32)).astype(BF16)
    for copy in scatter:
        copy.wait()
    summed = parts[zero].astype(F32)
    for k in range(1, shards):
        summed = summed + part_in[k].astype(F32)
    mine[...] = summed.astype(BF16)
    third = []
    for k in range(1, count):
        peer = lax.rem(seq + k, count)
        src = mine.at[pl.ds(pl.multiple_of(peer * chunk, 16), chunk)]
        copy = push(src, chunk_in.at[k], ss.at[1, k], sr.at[1, k], "seq", peer)
        copy.start()
        third.append(copy)
    for copy in third:
        copy.wait()
    here = pl.ds(pl.multiple_of(seq * chunk, 16), chunk)
    summed = mine[here].astype(F32)
    for k in range(1, count):
        summed = summed + chunk_in[k].astype(F32)
    full[here] = summed.astype(BF16)
    third = []
    for k in range(1, count):
        peer = lax.rem(seq + k, count)
        copy = push(full.at[here], full.at[here], ss.at[2, k], sr.at[2, k], "seq", peer)
        copy.start()
        third.append(copy)
    for copy in second:
        copy.wait()
    summed = small2_in[0]
    for z in range(1, count):
        summed = summed + small2_in[z]
    gd_ref[...] = summed[KERNEL * PAIRS + KERNEL : KERNEL * PAIRS + KERNEL + 2, :HEADS]
    for i in range(PAIRS + 1):
        taps[:, i * 128 : i * 128 + 128] = summed[KERNEL * i : KERNEL * i + KERNEL]
    width = gc_ref.shape[1]
    for z in range(shards):

        @pl.when(zero == z)
        def _():
            gc_ref[...] = taps[:, z * width : (z + 1) * width]

    for copy in third:
        copy.wait()

    @pl.when(seq < count - 1)
    def _():
        up.wait_send()

    @pl.when(seq > 0)
    def _():
        down.wait_send()

    gw_ref[:, :128] = full[:rows].astype(F32)
    tail = full[rows : rows + fold_rows].astype(F32)
    for q in range(fold):
        gw_ref[q * fold_rows : (q + 1) * fold_rows, 128:] = tail[:, 32 * q : 32 * q + HEADS]


def call(body, outs, scratch=(), sems=(), number=None):
    return pl.pallas_call(
        body,
        out_shape=[jax.ShapeDtypeStruct(s, t) for s, t in outs],
        scratch_shapes=[pltpu.VMEM(s, t) for s, t in scratch]
        + [pltpu.SemaphoreType.DMA(s) for s in sems],
        compiler_params=pltpu.CompilerParams(
            vmem_limit_bytes=48 * 1024 * 1024,
            collective_id=number,
            has_side_effects=number is not None,
        ),
    )


SQ4 = (4, 128, 128)
SQ2 = (2, 128, 128)


def per_device(hidden, grad_out, w_proj, conv_w, a_log, dt_bias):
    hid, go = hidden[0], grad_out[0]
    assert hidden.shape[:2] == (1, SPAN)
    count, shards = lax.axis_size("seq"), lax.axis_size("zero")
    rows = WIDTH // shards
    part = CHANNELS // shards
    alog = jnp.pad(a_log, (0, 128 - HEADS))[None]
    bias = jnp.pad(dt_bias, (0, 128 - HEADS))[None]
    x_ext, w_full, filters = call(
        functools.partial(gather_kernel, shards, count),
        [((EXT, WIDTH), BF16), ((WIDTH, 256), BF16), ((8, CHANNELS), F32)],
        [
            ((shards,) + w_proj.shape, BF16), ((8, part), F32), ((shards, 8, part), F32),
            ((2 * EDGE, WIDTH), BF16), ((2 * EDGE, WIDTH), BF16),
        ],
        [(shards, 2), (shards, 2), (4,)],
        0,
    )(hid, w_proj, conv_w)
    pieces = (PAIRS, 4, STATE, 128)
    own_up, own_down, dec_up, dec_down, w_rev, bcx, dtx, within = call(
        first_kernel,
        [
            (pieces, F32), (pieces, F32), ((PAIRS, 4, 8, 128), F32), ((PAIRS, 4, 8, 128), F32),
            ((WIDTH, 256), BF16), ((2, EXT, 128), F32), (SQ2, F32), (SQ4, F32),
        ],
        [(SQ4, F32)] * 3,
    )(x_ext, go, w_full, filters, alog, bias)
    in_up, in_down = call(
        functools.partial(exchange_kernel, count),
        [(pieces, BF16), (pieces, BF16)],
        [((2,) + pieces, BF16), ((2,) + pieces, BF16)],
        [(2, PAIRS), (2, PAIRS)],
        1,
    )(own_up, own_down, dec_up, dec_down)
    output, gi, gf, ddt, heads = call(
        main_kernel,
        [
            ((SPAN, WIDTH), BF16), ((2, EXT, CHANNELS), F32), ((2, 8, CHANNELS), F32),
            (SQ2, BF16), ((8, 128), F32),
        ],
        [
            (s, F32)
            for s in (
                SQ4, SQ4, SQ4, SQ4, SQ2, SQ4, SQ4, (4, 128, STATE), (4, 128, STATE), SQ4, SQ4,
                SQ2, SQ2, (4, 2, 128, STATE),
            )
        ],
    )(x_ext, go, filters, alog, bcx, dtx, within, in_up, in_down)
    fold = 4 if rows % 64 == 0 else 1
    step = 16 * count
    padded = -(-(rows + rows // fold) // step) * step
    lines = 48
    grad_hidden, share_w, share_c, grad_heads = call(
        functools.partial(last_kernel, shards, count, fold),
        [
            ((SPAN, WIDTH), BF16), (w_proj.shape, F32), ((KERNEL, part), F32), ((2, HEADS), F32),
        ],
        [
            ((2, EDGE, CHANNELS), F32), ((2, EDGE, CHANNELS), F32),
            ((shards, padded, 128), BF16), ((shards, padded, 128), BF16),
            ((padded, 128), BF16), ((count, padded // count, 128), BF16), ((padded, 128), BF16),
            ((WIDTH, 256), F32),
            ((lines, 128), F32), ((shards, lines, 128), F32),
            ((lines, 128), F32), ((count, lines, 128), F32), ((KERNEL, CHANNELS), F32),
        ],
        [(4,), (2, shards), (2, shards), (3, count), (3, count)],
        2,
    )(hid, w_full, w_rev, gi, ddt, gf, heads)
    return (output[None], grad_hidden[None], share_w, share_c, grad_heads)


def solution(mesh):
    return jax.shard_map(
        per_device,
        mesh=mesh,
        in_specs=(
            P(("grp", "zero"), "seq", None),
            P(("grp", "zero"), "seq", None),
            P("zero", None),
            P(None, "zero"),
            P(),
            P(),
        ),
        out_specs=(
            P(("grp", "zero"), "seq", None),
            P(("grp", "zero"), "seq", None),
            P(("grp", "zero"), None),
            P("grp", "zero"),
            P("grp", None),
        ),
        check_vma=False,
    )
```

```python
import functools
import jax
import jax.numpy as jnp
from jax import lax
from jax.experimental import pallas as pl
from jax.experimental.pallas import tpu as pltpu
from jax.sharding import PartitionSpec as P

WIDTH = 1280
STATE = 64
HEAD_DIM = 64
SPAN = 128
KERNEL = 4
HEADS = 20
PAIRS = WIDTH // 128
CHANNELS = WIDTH + 2 * STATE
EDGE = 8
EXT = SPAN + 2 * EDGE
F32 = jnp.float32
BF16 = jnp.bfloat16
UNITS = 2 * PAIRS
LAG = 3


def mm(a, b):
    return jnp.dot(a, b, preferred_element_type=F32)


def mm_nt(a, b):
    return lax.dot_general(a, b, (((1,), (1,)), ((), ())), preferred_element_type=F32)


def mm_tn(a, b):
    return lax.dot_general(a, b, (((0,), (0,)), ((), ())), preferred_element_type=F32)


def exact(a, b):
    return jnp.dot(a, b, preferred_element_type=F32, precision=lax.Precision.HIGHEST)


def iota(dim, shape=(128, 128)):
    return lax.broadcasted_iota(jnp.int32, shape, dim)


def mirror(dtype=BF16):
    return jnp.where(iota(0) + iota(1) == 127, 1.0, 0.0).astype(dtype)


def softplus(x):
    return jnp.maximum(x, 0.0) + jnp.log1p(jnp.exp(-jnp.abs(x)))


def sigmoid(x):
    return 1.0 / (1.0 + jnp.exp(-x))


def shifted(x):
    back = [x[EDGE : EDGE + SPAN]]
    fore = [back[0]]
    for k in range(1, KERNEL):
        back.append(pltpu.roll(x, k, 0)[EDGE : EDGE + SPAN])
        fore.append(pltpu.roll(x, EXT - k, 0)[EDGE : EDGE + SPAN])
    return back, fore


def conv(taps, rows):
    out = taps[0:1] * rows[0]
    for k in range(1, KERNEL):
        out = out + taps[k : k + 1] * rows[k]
    return out


def lanes(i):
    return pl.ds(pl.multiple_of(i * 128, 128), 128)


MESH = pl.DeviceIdType.MESH


def greet_all(sizes):
    barrier = pltpu.get_barrier_semaphore()
    for axis, size in sizes:
        me = lax.axis_index(axis)
        for k in range(1, size):
            pl.semaphore_signal(
                barrier, inc=1, device_id={axis: lax.rem(me + k, size)}, device_id_type=MESH
            )
    pl.semaphore_wait(barrier, sum(size - 1 for _, size in sizes))


def push(src, dst, send, recv, axis, peer):
    return pltpu.make_async_remote_copy(
        src_ref=src,
        dst_ref=dst,
        send_sem=send,
        recv_sem=recv,
        device_id={axis: peer},
        device_id_type=MESH,
    )


def greet_sides(me, count, more=0):
    barrier = pltpu.get_barrier_semaphore()
    for k in (1, count - 1):
        pl.semaphore_signal(
            barrier, inc=1, device_id={"seq": lax.rem(me + k, count)}, device_id_type=MESH
        )
    pl.semaphore_wait(barrier, 2 + more)


def split2(x):
    hi = x.astype(BF16)
    return hi, (x - hi.astype(F32)).astype(BF16)


def split3(x):
    hi = x.astype(BF16)
    rest = x - hi.astype(F32)
    mid = rest.astype(BF16)
    return hi, mid, (rest - mid.astype(F32)).astype(BF16)


def exact_left(a, x):
    n = x.shape[1]
    out = mm(a, jnp.concatenate(split3(x), axis=1))
    return out[:, :n] + out[:, n : 2 * n] + out[:, 2 * n :]


def exact_right(x, b):
    n = x.shape[0]
    out = mm(jnp.concatenate(split3(x), axis=0), b)
    return out[:n] + out[n : 2 * n] + out[2 * n :]


def ones_where(keep):
    return jnp.where(keep, 1.0, 0.0).astype(BF16)


def strand_swap():
    k, lane = iota(0), iota(1)
    return ones_where((lane >= 32) & (lane < 32 + HEADS) & (k + lane == 31 + HEADS))


def front_kernel(
    shards, count,
    hid_ref, go_ref, w_ref, c_ref, alog_ref, bias_ref,
    out_ref, gi_ref, gf_ref, ddt_ref, heads_ref, w_out, w_rev,
    x_ref, xf_ref, taps_ref, wp_ref, w_slots, c_own, c_slots, before, after,
    vals, slope, u_ref, fu_ref, eg_ref, yoff, duo, e_b, f_b, dt_b,
    own, in_slots, out_slots,
    rates, dtx_ref, stack, split, within_t, score, diag, bc_act, bc_t, bc_slope, masks,
    d_score, d_diag, d_bc, acc, y_first,
    send, recv, sides, c_send, c_recv,
):
    seq, zero = lax.axis_index("seq"), lax.axis_index("zero")
    barrier = pltpu.get_barrier_semaphore()
    for k in range(1, shards):
        pl.semaphore_signal(
            barrier, inc=1, device_id={"zero": lax.rem(zero + k, shards)}, device_id_type=MESH
        )
    greet_sides(seq, count, shards - 1)
    up = push(
        hid_ref.at[pl.ds(SPAN - 2 * EDGE, 2 * EDGE)], before, sides.at[0], sides.at[1], "seq",
        lax.rem(seq + 1, count),
    )
    down = push(
        hid_ref.at[pl.ds(0, 2 * EDGE)], after, sides.at[2], sides.at[3], "seq",
        lax.rem(seq + count - 1, count),
    )

    @pl.when(seq < count - 1)
    def _():
        up.start()

    @pl.when(seq > 0)
    def _():
        down.start()

    c_own[...] = jnp.zeros_like(c_own)
    c_own[:KERNEL] = c_ref[...].astype(F32)
    tap_copies, w_copies = [], []
    for k in range(1, shards):
        peer = lax.rem(zero + k, shards)
        tap_copies.append(
            push(c_own, c_slots.at[zero], send.at[k, 1], recv.at[k, 1], "zero", peer)
        )
        w_copies.append(push(w_ref, w_slots.at[zero], send.at[k, 0], recv.at[k, 0], "zero", peer))
    for copy in tap_copies + w_copies:
        copy.start()
    w_slots[zero] = w_ref[...]
    c_slots[zero] = c_own[...]
    w_out[:, 128:] = jnp.zeros((WIDTH, 128), BF16)
    x_ref[EDGE : EDGE + SPAN] = hid_ref[...]
    flip = mirror()
    swap = strand_swap()
    masks[0] = ones_where(iota(0) > iota(1))
    masks[1] = ones_where(iota(0) < iota(1))
    d_score[...] = jnp.zeros_like(d_score)
    d_diag[...] = jnp.zeros_like(d_diag)
    d_bc[...] = jnp.zeros_like(d_bc)
    acc[...] = jnp.zeros_like(acc)

    @pl.when(seq == 0)
    def _():
        x_ref[:EDGE] = jnp.zeros((EDGE, WIDTH), BF16)
        in_slots[0] = jnp.zeros(in_slots.shape[1:], BF16)

    @pl.when(seq > 0)
    def _():
        up.wait_recv()
        x_ref[:EDGE] = before[EDGE:]

    @pl.when(seq == count - 1)
    def _():
        x_ref[EDGE + SPAN :] = jnp.zeros((EDGE, WIDTH), BF16)
        in_slots[1] = jnp.zeros(in_slots.shape[1:], BF16)

    @pl.when(seq < count - 1)
    def _():
        down.wait_recv()
        x_ref[EDGE + SPAN :] = after[:EDGE]

    for copy in tap_copies:
        copy.wait()
    part = c_ref.shape[1]
    for z in range(shards):
        taps_ref[0, :, z * part : (z + 1) * part] = c_slots[z]
    for b in range(PAIRS):
        taps_ref[1, :, b * 128 : (b + 1) * 128] = mm(
            taps_ref[0, :, (PAIRS - 1 - b) * 128 : (PAIRS - b) * 128].astype(BF16), flip
        )

    def values_step(i, carry):
        x_low = x_ref[:, lanes(i)]
        xf_ref[:, lanes(PAIRS - 1 - i)] = mm(x_low, flip).astype(BF16)
        rows = shifted(x_low.astype(F32))
        for s in range(2):
            taps = taps_ref[s, :, lanes(i)]
            for d in range(2):
                mixed = conv(taps, rows[d])
                sig = sigmoid(mixed)
                act = mixed * sig
                vals[2 * i + s, d] = act.astype(BF16)
                slope[2 * i + s, d] = sig + act * (1.0 - sig)
        return carry

    lax.fori_loop(0, PAIRS, values_step, 0)

    for copy in w_copies:
        copy.wait()
    rows, columns = w_ref.shape
    for z in range(shards):
        w_out[z * rows : (z + 1) * rows, :columns] = w_slots[z]
    wp_ref[:, :128] = w_out[:, :128]
    wp_ref[:, 128:] = mm(w_out[:, 128:], swap).astype(BF16)
    proj = (mm(x_ref[...], w_out[...]), mm(xf_ref[...], wp_ref[...]))
    place = exact_right(jnp.concatenate([alog_ref[...], bias_ref[...]], axis=0), swap)
    rate = jnp.exp(alog_ref[0:1] + place[0:1])
    rates[0:1] = rate
    dtx = (proj[0] + proj[1])[EDGE : EDGE + SPAN, 128:] + (bias_ref[0:1] + place[8:9])
    dtx_ref[...] = dtx
    delta = softplus(dtx)
    both = jnp.concatenate(
        [ones_where(iota(0) >= iota(1)), ones_where(iota(0) <= iota(1))], axis=0
    )
    within = exact_left(both, -rate * delta)
    ends = jnp.concatenate(
        [
            jnp.broadcast_to(within[SPAN - 1 : SPAN], (SPAN, 128)),
            jnp.broadcast_to(within[SPAN : SPAN + 1], (SPAN, 128)),
        ],
        axis=0,
    )
    spread = jnp.concatenate([jnp.exp(within), jnp.exp(ends - within), delta], axis=0)
    hi, lo = split2(spread)
    wide_low = iota(1, spread.shape) < 64
    stack[...] = jnp.where(
        wide_low, hi.astype(F32), pltpu.roll(lo.astype(F32), 64, 1)
    ).astype(BF16)
    hi, mid, lo = split3(within)
    low_two = iota(1, (256, 128)) < 64
    split[:, :128] = jnp.where(
        low_two, hi.astype(F32), pltpu.roll(mid.astype(F32), 64, 1)
    ).astype(BF16)
    split[:, 128:] = jnp.where(low_two, lo.astype(F32), 0.0).astype(BF16)
    for d in range(2):
        within_t[d] = within[d * 128 : d * 128 + 128].T
    for s in range(2):
        bcx = shifted(proj[s][:, :128].astype(BF16).astype(F32))
        scores = []
        for d in range(2):
            c = 2 * s + d
            mixed = conv(taps_ref[0, :, WIDTH:], bcx[d])
            sig = sigmoid(mixed)
            full = mixed * sig
            act = full.astype(BF16)
            bc_slope[c] = sig + full * (1.0 - sig)
            bc_act[c, 0] = act[:, :STATE]
            bc_act[c, 1] = act[:, STATE:]
            act_t = act.astype(F32).T.astype(BF16)
            bc_t[c] = act_t
            scores.append(mm(act[:, STATE:], act_t[:STATE]))
            own_diag = jnp.sum(jnp.where(iota(0) == iota(1), scores[d], 0.0), axis=1, keepdims=True)
            diag[c] = jnp.broadcast_to(own_diag, (128, 128))
        score[s] = jnp.where(
            iota(0) > iota(1), scores[0], jnp.where(iota(0) < iota(1), scores[1], 0.0)
        )

    def produce(u):
        i, s = lax.div(u, 2), lax.rem(u, 2)
        head = 32 * s + 2 * i
        sel = ones_where(lax.rem(iota(0), 64) == head + jnp.where(iota(1) >= HEAD_DIM, 1, 0))
        wide = mm(stack[...], sel)
        dt = wide[512:]
        dt_b[u] = dt
        g = go_ref[:, lanes(i)].astype(F32)
        for d in range(2):
            e, f = wide[128 * d : 128 * d + 128], wide[256 + 128 * d : 384 + 128 * d]
            e_b[u, d] = e
            f_b[u, d] = f
            step = (vals[u, d].astype(F32) * dt).astype(BF16)
            u_ref[u, d] = step
            fu = (step.astype(F32) * f).astype(BF16)
            fu_ref[u, d] = fu
            eg = (e * g).astype(BF16)
            eg_ref[u, d] = eg
            own[d, u, 0] = mm(bc_t[2 * s + d, :STATE], fu)
            own[1 - d, u, 1] = mm(bc_t[2 * s + d, STATE:], eg)

    def decay_of(u, d):
        at = SPAN - 1 if d == 0 else 0
        return e_b[u, d, at : at + 1]

    chains = ((0, seq, seq + 1), (1, count - 1 - seq, seq - 1))

    def copy_of(d, u, peer):
        return push(
            out_slots.at[d, u], in_slots.at[d, u], c_send.at[d, u], c_recv.at[d, u], "seq", peer
        )

    def forward(t):
        for d, place, peer in chains:
            u = t - LAG * place

            @pl.when((u >= 0) & (u < UNITS))
            def _():
                @pl.when(place == 0)
                def _():
                    out_slots[d, u] = own[d, u].astype(BF16)

                @pl.when(place > 0)
                def _():
                    copy_of(d, u, seq).wait_recv()

                @pl.when((place > 0) & (place < count - 1))
                def _():
                    for q in range(2):
                        dec = decay_of(u, d if q == 0 else 1 - d)
                        out_slots[d, u, q] = (
                            own[d, u, q] + dec * in_slots[d, u, q].astype(F32)
                        ).astype(BF16)

                @pl.when(place < count - 1)
                def _():
                    copy_of(d, u, peer).start()

    def inside(u):
        i, s = lax.div(u, 2), lax.rem(u, 2)
        head = 32 * s + 2 * i
        square = (256, 256)
        line = iota(0, square)
        pick = ones_where(
            (lax.rem(line, 64) == head + jnp.where(iota(1, square) >= 128, 1, 0)) & (line < 192)
        )
        cols = mm(split[...], pick)
        lower = iota(0) >= iota(1)
        low = iota(1) < HEAD_DIM
        go = go_ref[:, lanes(i)]
        none = jnp.zeros((128, 128), BF16)
        g_two = jnp.concatenate([jnp.where(low, go, none), jnp.where(low, none, go)], axis=0)
        steps = jnp.concatenate([u_ref[u, 0], u_ref[u, 1]], axis=0)
        dw = mm_nt(g_two, steps)
        sc = score[s]
        ds = d_score[s]
        below, above = [], []
        for r in range(2):
            at = slice(128 * r, 128 * r + 128)
            gap = jnp.where(
                lower,
                cols[:128, at] - within_t[0, pl.ds(head + r, 1), :],
                cols[128:, at] - within_t[1, pl.ds(head + r, 1), :],
            )
            decay = jnp.exp(gap)
            w = (sc * decay).astype(BF16)
            below.append(w * masks[0])
            above.append(w * masks[1])
            ds = ds + decay * jnp.where(lower, dw[at, :128], dw[at, 128:])
        d_score[s] = ds
        g = go.astype(F32)
        for d, ws in enumerate((below, above)):
            y_two = mm(jnp.concatenate(ws, axis=0), steps[128 * d : 128 * d + 128])
            yoff[u, d] = jnp.where(low, y_two[:128], y_two[128:])
            duo[u, d] = jnp.where(low, mm_tn(ws[0], go), mm_tn(ws[1], go))
            d_diag[2 * s + d] += g * steps[128 * d : 128 * d + 128].astype(F32)

    def back(taps, dm, x, direction):
        zero_rows = jnp.zeros((EDGE, 128), F32)
        wide = jnp.concatenate([zero_rows, dm, zero_rows], axis=0)
        out = taps[0:1] * wide
        sums = [jnp.sum(wide * x, axis=0, keepdims=True)]
        for k in range(1, KERNEL):
            moved = pltpu.roll(wide, EXT - k if direction == 0 else k, 0)
            out = out + taps[k : k + 1] * moved
            sums.append(jnp.sum(moved * x, axis=0, keepdims=True))
        return out, jnp.concatenate(sums + [jnp.zeros((8 - KERNEL, 128), F32)], axis=0)

    def finish(u):
        i, s = lax.div(u, 2), lax.rem(u, 2)
        head = 32 * s + 2 * i
        g = go_ref[:, lanes(i)].astype(F32)
        x = x_ref[:, lanes(i)].astype(F32)
        taps = taps_ref[s, :, lanes(i)]
        dt = dt_b[u]
        y = jnp.zeros((128, 128), F32)
        gi = jnp.zeros((EXT, 128), F32)
        gf = jnp.zeros((8, 128), F32)
        qt = jnp.zeros((128, 128), F32)
        qs, ends = [], []
        for d in range(2):
            c = 2 * s + d
            s_in, g_in = in_slots[d, u, 0], in_slots[1 - d, u, 1]
            step = u_ref[u, d].astype(F32)
            across = mm(bc_act[c, 1], s_in) * e_b[u, d] + yoff[u, d]
            y = y + across + diag[c] * step
            du = duo[u, d] + f_b[u, d] * mm(bc_act[c, 0], g_in)
            qs.append(g * across - step * du)
            du = du + diag[c] * g
            qt = qt + vals[u, d].astype(F32) * du
            d_bc[c, 0] += mm_nt(fu_ref[u, d], g_in)
            d_bc[c, 1] += mm_nt(eg_ref[u, d], s_in)
            leaving = own[d, u, 0] + decay_of(u, d) * s_in.astype(F32)
            ends.append(jnp.sum(leaving * g_in.astype(F32), axis=0, keepdims=True))
            dm = (dt * du).astype(BF16).astype(F32) * slope[u, d]
            more, sums = back(taps, dm, x, d)
            gi = gi + more
            gf = gf + sums
        q = jnp.concatenate(qs + [qt] + ends + [jnp.zeros((6, 128), F32)], axis=0)
        tall = (256, 128)
        sel_t = ones_where(
            iota(1, tall) == head + jnp.where(lax.rem(iota(0, tall), 128) >= HEAD_DIM, 1, 0)
        )
        acc[...] += mm(jnp.concatenate(split2(q), axis=1), sel_t)
        gi_ref[s, :, lanes(i)] = gi
        gf_ref[s, :, lanes(i)] = gf

        @pl.when(s == 0)
        def _():
            y_first[...] = y.astype(BF16).astype(F32)

        @pl.when(s == 1)
        def _():
            out_ref[:, lanes(i)] = (y_first[...] + y.astype(BF16).astype(F32)).astype(BF16)

    lag_all = LAG * (count - 1)

    def slot(t, carry):
        @pl.when(t < UNITS)
        def _():
            produce(t)

        forward(t)

        @pl.when(t < UNITS)
        def _():
            inside(t)

        @pl.when(t >= lag_all)
        def _():
            finish(t - lag_all)

        return carry

    lax.fori_loop(0, UNITS + lag_all, slot, 0)

    end_rows = acc[3 * SPAN : 3 * SPAN + 8]
    dl0 = acc[:SPAN] + jnp.where(iota(0) == SPAN - 1, end_rows[0:1], 0.0)
    dl1 = acc[SPAN : 2 * SPAN] + jnp.where(iota(0) == 0, end_rows[1:2], 0.0)
    both_t = jnp.concatenate(
        [ones_where(iota(0) <= iota(1)), ones_where(iota(0) >= iota(1))], axis=1
    )
    d_log = exact_left(both_t, jnp.concatenate([dl0, dl1], axis=0))
    rate = rates[0:1]
    dtx = dtx_ref[...]
    d_raw = (acc[2 * SPAN : 3 * SPAN] - rate * d_log) * sigmoid(dtx)
    sums = jnp.concatenate(
        [
            jnp.sum(d_log * (-rate * softplus(dtx)), axis=0, keepdims=True),
            jnp.sum(d_raw, axis=0, keepdims=True),
            jnp.zeros((6, 128), F32),
        ],
        axis=0,
    )
    unswap = swap.astype(F32).T.astype(BF16)
    heads_ref[...] = jnp.where(iota(1, (8, 128)) < HEADS, sums, 0.0) + exact_right(sums, unswap)
    ddt_ref[0] = jnp.where(iota(1) < HEADS, d_raw, 0.0).astype(BF16)
    ddt_ref[1] = mm(d_raw.astype(BF16), unswap).astype(BF16)
    for s in range(2):
        taps = taps_ref[0, :, WIDTH:]
        bcx = mm(
            x_ref[...] if s == 0 else xf_ref[...], w_out[:, :128]
        ).astype(BF16).astype(F32)
        gi = jnp.zeros((EXT, 128), F32)
        gf = jnp.zeros((8, 128), F32)
        for d in range(2):
            c = 2 * s + d
            on_diag = jnp.sum(d_diag[c], axis=1, keepdims=True)
            off = iota(0) > iota(1) if d == 0 else iota(0) < iota(1)
            ds = jnp.where(
                off, d_score[s], jnp.where(iota(0) == iota(1), on_diag, 0.0)
            ).astype(BF16)
            db = d_bc[c, 0] + mm_tn(ds, bc_act[c, 1])
            dc = d_bc[c, 1] + mm(ds, bc_act[c, 0])
            dm = jnp.concatenate([db, dc], axis=1).astype(BF16).astype(F32) * bc_slope[c]
            more, some = back(taps, dm, bcx, d)
            gi = gi + more
            gf = gf + some
        gi_ref[s, :, WIDTH:] = gi
        gf_ref[s, :, WIDTH:] = gf
    for b in range(PAIRS):
        w_rev[b * 128 : (b + 1) * 128] = mm(
            flip, w_out[(PAIRS - 1 - b) * 128 : (PAIRS - b) * 128]
        ).astype(BF16)
    for d, place, peer in chains:

        @pl.when(place < count - 1)
        def _():
            def sent(u, carry):
                copy_of(d, u, peer).wait_send()
                return carry

            lax.fori_loop(0, UNITS, sent, 0)

    @pl.when(seq < count - 1)
    def _():
        up.wait_send()

    @pl.when(seq > 0)
    def _():
        down.wait_send()


def last_kernel(
    shards, count, fold,
    hid_ref, w_ref, wr_ref, gi_ref, ddt_ref, gf_ref, heads_ref,
    gh_ref, gw_ref, gc_ref, gd_ref,
    before, after, parts, part_in, mine, chunk_in, full, total, small, small_in, small2, small2_in,
    taps, sides, zs, zr, ss, sr,
):
    seq, zero = lax.axis_index("seq"), lax.axis_index("zero")
    rows = WIDTH // shards
    fold_rows = rows // fold
    chunk = mine.shape[0] // count
    greet_all((("zero", shards), ("seq", count)))
    up = push(
        gi_ref.at[:, pl.ds(EDGE + SPAN, EDGE)], before, sides.at[0], sides.at[1], "seq",
        lax.rem(seq + 1, count),
    )
    down = push(
        gi_ref.at[:, pl.ds(0, EDGE)], after, sides.at[2], sides.at[3], "seq",
        lax.rem(seq + count - 1, count),
    )

    @pl.when(seq < count - 1)
    def _():
        up.start()

    @pl.when(seq > 0)
    def _():
        down.start()

    @pl.when(seq == 0)
    def _():
        before[...] = jnp.zeros_like(before)

    @pl.when(seq == count - 1)
    def _():
        after[...] = jnp.zeros_like(after)

    flip = mirror()
    small[...] = jnp.zeros_like(small)
    for i in range(PAIRS):
        at = slice(i * 128, i * 128 + 128)
        other = slice((PAIRS - 1 - i) * 128, (PAIRS - i) * 128)
        block = gf_ref[0, :, at] + exact(gf_ref[1, :, other], mirror(F32))
        small[KERNEL * i : KERNEL * i + KERNEL] = block[:KERNEL]
    block = gf_ref[0, :, WIDTH:] + gf_ref[1, :, WIDTH:]
    small[KERNEL * PAIRS : KERNEL * PAIRS + KERNEL] = block[:KERNEL]
    small[KERNEL * PAIRS + KERNEL : KERNEL * PAIRS + KERNEL + 2] = heads_ref[:2]
    first = []
    for k in range(1, shards):
        peer = lax.rem(zero + k, shards)
        copy = push(small, small_in.at[zero], zs.at[1, k], zr.at[1, k], "zero", peer)
        copy.start()
        first.append(copy)
    small_in[zero] = small[...]

    @pl.when(seq > 0)
    def _():
        up.wait_recv()

    @pl.when(seq < count - 1)
    def _():
        down.wait_recv()

    def own(s, at):
        top = gi_ref[s, EDGE : 2 * EDGE, at] + before[s, :, at]
        low = gi_ref[s, SPAN : SPAN + EDGE, at] + after[s, :, at]
        return jnp.concatenate([top, gi_ref[s, 2 * EDGE : SPAN, at], low], axis=0).astype(BF16)

    gps = [
        jnp.concatenate([own(s, slice(WIDTH, CHANNELS)), ddt_ref[s]], axis=1) for s in range(2)
    ]
    for i in range(PAIRS):
        at = slice(i * 128, i * 128 + 128)
        other = slice((PAIRS - 1 - i) * 128, (PAIRS - i) * 128)
        hid_flip = mm(hid_ref[:, other], flip).astype(BF16)
        total[at] = mm_tn(hid_ref[:, at], gps[0]) + mm_tn(hid_flip, gps[1])
    for z in range(shards):
        parts[z, :rows] = total[z * rows : (z + 1) * rows, :128].astype(BF16)
        folded = jnp.zeros((fold_rows, 128), F32)
        for q in range(fold):
            start = z * rows + q * fold_rows
            piece = total[start : start + fold_rows, 128:]
            folded = folded + (pltpu.roll(piece, 32 * q, 1) if q else piece)
        parts[z, rows : rows + fold_rows] = folded.astype(BF16)
        spare = parts.shape[1] - rows - fold_rows
        if spare:
            parts[z, rows + fold_rows :] = jnp.zeros((spare, 128), BF16)
    scatter = []
    for k in range(1, shards):
        peer = lax.rem(zero + k, shards)
        copy = push(parts.at[peer], part_in.at[k], zs.at[0, k], zr.at[0, k], "zero", peer)
        copy.start()
        scatter.append(copy)
    for copy in first:
        copy.wait()
    small2[...] = small_in[0]
    for z in range(1, shards):
        small2[...] += small_in[z]
    second = []
    for k in range(1, count):
        peer = lax.rem(seq + k, count)
        copy = push(small2, small2_in.at[seq], ss.at[0, k], sr.at[0, k], "seq", peer)
        copy.start()
        second.append(copy)
    small2_in[seq] = small2[...]
    for i in range(PAIRS):
        at = slice(i * 128, i * 128 + 128)
        a = (own(0, at).astype(F32) + mm_nt(gps[0], w_ref[at])).astype(BF16)
        b = (own(1, at).astype(F32) + mm_nt(gps[1], wr_ref[at])).astype(BF16)
        gh_ref[:, at] = (a.astype(F32) + b.astype(F32)).astype(BF16)
    for copy in scatter:
        copy.wait()
    summed = parts[zero].astype(F32)
    for k in range(1, shards):
        summed = summed + part_in[k].astype(F32)
    mine[...] = summed.astype(BF16)
    third = []
    for k in range(1, count):
        peer = lax.rem(seq + k, count)
        src = mine.at[pl.ds(pl.multiple_of(peer * chunk, 16), chunk)]
        copy = push(src, chunk_in.at[k], ss.at[1, k], sr.at[1, k], "seq", peer)
        copy.start()
        third.append(copy)
    for copy in third:
        copy.wait()
    here = pl.ds(pl.multiple_of(seq * chunk, 16), chunk)
    summed = mine[here].astype(F32)
    for k in range(1, count):
        summed = summed + chunk_in[k].astype(F32)
    full[here] = summed.astype(BF16)
    third = []
    for k in range(1, count):
        peer = lax.rem(seq + k, count)
        copy = push(full.at[here], full.at[here], ss.at[2, k], sr.at[2, k], "seq", peer)
        copy.start()
        third.append(copy)
    for copy in second:
        copy.wait()
    summed = small2_in[0]
    for z in range(1, count):
        summed = summed + small2_in[z]
    gd_ref[...] = summed[KERNEL * PAIRS + KERNEL : KERNEL * PAIRS + KERNEL + 2, :HEADS]
    for i in range(PAIRS + 1):
        taps[:, i * 128 : i * 128 + 128] = summed[KERNEL * i : KERNEL * i + KERNEL]
    width = gc_ref.shape[1]
    for z in range(shards):

        @pl.when(zero == z)
        def _():
            gc_ref[...] = taps[:, z * width : (z + 1) * width]

    for copy in third:
        copy.wait()

    @pl.when(seq < count - 1)
    def _():
        up.wait_send()

    @pl.when(seq > 0)
    def _():
        down.wait_send()

    gw_ref[:, :128] = full[:rows].astype(F32)
    tail = full[rows : rows + fold_rows].astype(F32)
    for q in range(fold):
        gw_ref[q * fold_rows : (q + 1) * fold_rows, 128:] = tail[:, 32 * q : 32 * q + HEADS]


def call(body, outs, scratch=(), sems=(), number=None):
    return pl.pallas_call(
        body,
        out_shape=[jax.ShapeDtypeStruct(s, t) for s, t in outs],
        scratch_shapes=[pltpu.VMEM(s, t) for s, t in scratch]
        + [pltpu.SemaphoreType.DMA(s) for s in sems],
        compiler_params=pltpu.CompilerParams(
            vmem_limit_bytes=48 * 1024 * 1024,
            collective_id=number,
            has_side_effects=number is not None,
        ),
    )


SQ4 = (4, 128, 128)
TILES = (UNITS, 2, 128, 128)
SQ2 = (2, 128, 128)


def per_device(hidden, grad_out, w_proj, conv_w, a_log, dt_bias):
    hid, go = hidden[0], grad_out[0]
    assert hidden.shape[:2] == (1, SPAN)
    count, shards = lax.axis_size("seq"), lax.axis_size("zero")
    rows = WIDTH // shards
    part = CHANNELS // shards
    alog = jnp.pad(a_log[None], ((0, 7), (0, 128 - HEADS)))
    bias = jnp.pad(dt_bias[None], ((0, 7), (0, 128 - HEADS)))
    pieces = (2, UNITS, 2, STATE, 128)
    output, gi, gf, ddt, heads, w_full, w_rev = call(
        functools.partial(front_kernel, shards, count),
        [
            ((SPAN, WIDTH), BF16), ((2, EXT, CHANNELS), F32), ((2, 8, CHANNELS), F32),
            (SQ2, BF16), ((8, 128), F32), ((WIDTH, 256), BF16), ((WIDTH, 256), BF16),
        ],
        [
            ((EXT, WIDTH), BF16), ((EXT, WIDTH), BF16), ((2, 8, CHANNELS), F32),
            ((WIDTH, 256), BF16), ((shards,) + w_proj.shape, BF16), ((8, part), F32),
            ((shards, 8, part), F32), ((2 * EDGE, WIDTH), BF16), ((2 * EDGE, WIDTH), BF16),
            (TILES, BF16), (TILES, F32), (TILES, BF16), (TILES, BF16), (TILES, BF16),
            (TILES, F32), (TILES, F32), (TILES, F32), (TILES, F32), ((UNITS, 128, 128), F32),
            (pieces, F32), (pieces, BF16), (pieces, BF16),
            ((8, 128), F32), ((128, 128), F32), ((5 * 128, 128), BF16), ((256, 256), BF16),
            (SQ2, F32), (SQ2, F32), (SQ4, F32), ((4, 2, 128, STATE), BF16), (SQ4, BF16),
            (SQ4, F32), (SQ2, BF16), (SQ2, F32), (SQ4, F32), ((4, 2, 128, STATE), F32),
            ((3 * SPAN + 8, 128), F32), ((128, 128), F32),
        ],
        [(shards, 2), (shards, 2), (4,), (2, UNITS), (2, UNITS)],
        0,
    )(hid, go, w_proj, conv_w, alog, bias)
    fold = 4 if rows % 64 == 0 else 1
    step = 16 * count
    padded = -(-(rows + rows // fold) // step) * step
    lines = 48
    grad_hidden, share_w, share_c, grad_heads = call(
        functools.partial(last_kernel, shards, count, fold),
        [
            ((SPAN, WIDTH), BF16), (w_proj.shape, F32), ((KERNEL, part), F32), ((2, HEADS), F32),
        ],
        [
            ((2, EDGE, CHANNELS), F32), ((2, EDGE, CHANNELS), F32),
            ((shards, padded, 128), BF16), ((shards, padded, 128), BF16),
            ((padded, 128), BF16), ((count, padded // count, 128), BF16), ((padded, 128), BF16),
            ((WIDTH, 256), F32),
            ((lines, 128), F32), ((shards, lines, 128), F32),
            ((lines, 128), F32), ((count, lines, 128), F32), ((KERNEL, CHANNELS), F32),
        ],
        [(4,), (2, shards), (2, shards), (3, count), (3, count)],
        2,
    )(hid, w_full, w_rev, gi, ddt, gf, heads)
    return (output[None], grad_hidden[None], share_w, share_c, grad_heads)


def solution(mesh):
    return jax.shard_map(
        per_device,
        mesh=mesh,
        in_specs=(
            P(("grp", "zero"), "seq", None),
            P(("grp", "zero"), "seq", None),
            P("zero", None),
            P(None, "zero"),
            P(),
            P(),
        ),
        out_specs=(
            P(("grp", "zero"), "seq", None),
            P(("grp", "zero"), "seq", None),
            P(("grp", "zero"), None),
            P("grp", "zero"),
            P("grp", None),
        ),
        check_vma=False,
    )
```

```python
import functools
import jax
import jax.numpy as jnp
from jax import lax
from jax.experimental import pallas as pl
from jax.experimental.pallas import tpu as pltpu
from jax.sharding import PartitionSpec as P

WIDTH = 1280
STATE = 64
HEAD_DIM = 64
SPAN = 128
KERNEL = 4
HEADS = 20
PAIRS = WIDTH // 128
CHANNELS = WIDTH + 2 * STATE
EDGE = 8
EXT = SPAN + 2 * EDGE
F32 = jnp.float32
BF16 = jnp.bfloat16
UNITS = 2 * PAIRS
LAG = 3


def mm(a, b):
    return jnp.dot(a, b, preferred_element_type=F32)


def mm_nt(a, b):
    return lax.dot_general(a, b, (((1,), (1,)), ((), ())), preferred_element_type=F32)


def mm_tn(a, b):
    return lax.dot_general(a, b, (((0,), (0,)), ((), ())), preferred_element_type=F32)


def exact(a, b):
    return jnp.dot(a, b, preferred_element_type=F32, precision=lax.Precision.HIGHEST)


def iota(dim, shape=(128, 128)):
    return lax.broadcasted_iota(jnp.int32, shape, dim)


def mirror(dtype=BF16):
    return jnp.where(iota(0) + iota(1) == 127, 1.0, 0.0).astype(dtype)


def softplus(x):
    return jnp.maximum(x, 0.0) + jnp.log1p(jnp.exp(-jnp.abs(x)))


def sigmoid(x):
    return 1.0 / (1.0 + jnp.exp(-x))


def shifted(x):
    back = [x[EDGE : EDGE + SPAN]]
    fore = [back[0]]
    for k in range(1, KERNEL):
        back.append(pltpu.roll(x, k, 0)[EDGE : EDGE + SPAN])
        fore.append(pltpu.roll(x, EXT - k, 0)[EDGE : EDGE + SPAN])
    return back, fore


def conv(taps, rows):
    out = taps[0:1] * rows[0]
    for k in range(1, KERNEL):
        out = out + taps[k : k + 1] * rows[k]
    return out


def lanes(i):
    return pl.ds(pl.multiple_of(i * 128, 128), 128)


MESH = pl.DeviceIdType.MESH


def greet_all(sizes):
    barrier = pltpu.get_barrier_semaphore()
    for axis, size in sizes:
        me = lax.axis_index(axis)
        for k in range(1, size):
            pl.semaphore_signal(
                barrier, inc=1, device_id={axis: lax.rem(me + k, size)}, device_id_type=MESH
            )
    pl.semaphore_wait(barrier, sum(size - 1 for _, size in sizes))


def push(src, dst, send, recv, axis, peer):
    return pltpu.make_async_remote_copy(
        src_ref=src,
        dst_ref=dst,
        send_sem=send,
        recv_sem=recv,
        device_id={axis: peer},
        device_id_type=MESH,
    )


def split2(x):
    hi = x.astype(BF16)
    return hi, (x - hi.astype(F32)).astype(BF16)


def split3(x):
    hi = x.astype(BF16)
    rest = x - hi.astype(F32)
    mid = rest.astype(BF16)
    return hi, mid, (rest - mid.astype(F32)).astype(BF16)


def exact_left(a, x):
    n = x.shape[1]
    out = mm(a, jnp.concatenate(split3(x), axis=1))
    return out[:, :n] + out[:, n : 2 * n] + out[:, 2 * n :]


def exact_right(x, b):
    n = x.shape[0]
    out = mm(jnp.concatenate(split3(x), axis=0), b)
    return out[:n] + out[n : 2 * n] + out[2 * n :]


def ones_where(keep):
    return jnp.where(keep, 1.0, 0.0).astype(BF16)


def strand_swap():
    k, lane = iota(0), iota(1)
    return ones_where((lane >= 32) & (lane < 32 + HEADS) & (k + lane == 31 + HEADS))


def folded(tail, fold):
    size = tail.shape[0] // fold
    out = tail[:size]
    for q in range(1, fold):
        out = out + pltpu.roll(tail[q * size : (q + 1) * size], 32 * q, 1)
    return out


def whole_kernel(
    shards, count, fold,
    hid_hbm, go_hbm, wt_hbm, c_hbm, alog_ref, bias_ref,
    out_ref, gh_ref, full, total2,
    hid_ref, go_ref, wt_in, c_in, wt_pad,
    x_ref, xf_ref, xt_ref, taps_ref, wp_ref, w_out, w_rev, w_slots, c_own, c_slots, before, after,
    vals, slope, u_ref, fu_ref, eg_ref, yoff, duo, e_b, f_b, dt_b,
    own, in_slots, out_slots,
    heads_in, rates, dtx_ref, stack, split, within_t, score, diag, bc_act, bc_t, bc_slope, masks,
    d_score, d_diag, d_bc, acc, y_first,
    gi_ref, gf_ref, bcx_ref, g_before, g_after, parts, pair_in, pair_sum, part_in, mine, chunk_in, gathered,
    small, small_in, small2, small2_in,
    local, sides, w_send, w_recv, f_send, f_recv, t_send, t_recv, c_send, c_recv,
    g_sides, p_send, p_recv, zs, zr, ss, sr, ms, mr,
):
    seq, zero = lax.axis_index("seq"), lax.axis_index("zero")
    core = lax.rem(zero, 2)
    chip = lax.div(zero, 2)
    chips = shards // 2
    sibling = zero + 1 - 2 * core
    rows = WIDTH // shards
    fold_rows = rows // fold
    packed = rows + fold_rows
    loads = [
        pltpu.make_async_copy(src, dst, local.at[n])
        for n, (src, dst) in enumerate(
            ((c_hbm, c_in), (wt_hbm, wt_in), (hid_hbm, hid_ref), (go_hbm, go_ref))
        )
    ]
    for load in loads:
        load.start()
    c_own[...] = jnp.zeros_like(c_own)
    wt_pad[...] = jnp.zeros_like(wt_pad)
    loads[0].wait()
    c_own[:KERNEL] = c_in[...].astype(F32)
    loads[1].wait()
    wt_pad[: wt_in.shape[0], :rows] = wt_in[...].astype(F32)
    w_own = wt_pad[...].T
    w_slots[zero, :rows] = w_own[:rows, :128].astype(BF16)
    w_slots[zero, rows:] = folded(w_own[:rows, 128:], fold).astype(BF16)
    greet_all((("zero", shards), ("seq", count)))
    tap_copies = []
    for k in range(1, shards):
        peer = lax.rem(zero + k, shards)
        copy = push(c_own, c_slots.at[zero], t_send.at[k], t_recv.at[k], "zero", peer)
        copy.start()
        tap_copies.append(copy)
    loads[2].wait()
    up = push(
        hid_ref.at[pl.ds(SPAN - 2 * EDGE, 2 * EDGE)], before, sides.at[0], sides.at[1], "seq",
        lax.rem(seq + 1, count),
    )
    down = push(
        hid_ref.at[pl.ds(0, 2 * EDGE)], after, sides.at[2], sides.at[3], "seq",
        lax.rem(seq + count - 1, count),
    )

    @pl.when(seq < count - 1)
    def _():
        up.start()

    @pl.when(seq > 0)
    def _():
        down.start()

    w_copies = []
    for k in range(chips):
        peer = lax.rem(zero + 2 * k, shards) if k else sibling
        copy = push(w_slots.at[zero], w_slots.at[zero], w_send.at[k], w_recv.at[k], "zero", peer)
        copy.start()
        w_copies.append(copy)
    c_slots[zero] = c_own[...]
    w_out[:, 128:] = jnp.zeros((WIDTH, 128), BF16)
    x_ref[EDGE : EDGE + SPAN] = hid_ref[...]
    flip = mirror()
    swap = strand_swap()
    masks[0] = ones_where(iota(0) > iota(1))
    masks[1] = ones_where(iota(0) < iota(1))
    d_score[...] = jnp.zeros_like(d_score)
    d_diag[...] = jnp.zeros_like(d_diag)
    d_bc[...] = jnp.zeros_like(d_bc)
    acc[...] = jnp.zeros_like(acc)

    @pl.when(seq == 0)
    def _():
        x_ref[:EDGE] = jnp.zeros((EDGE, WIDTH), BF16)
        in_slots[0] = jnp.zeros(in_slots.shape[1:], BF16)

    @pl.when(seq > 0)
    def _():
        up.wait_recv()
        x_ref[:EDGE] = before[EDGE:]

    @pl.when(seq == count - 1)
    def _():
        x_ref[EDGE + SPAN :] = jnp.zeros((EDGE, WIDTH), BF16)
        in_slots[1] = jnp.zeros(in_slots.shape[1:], BF16)

    @pl.when(seq < count - 1)
    def _():
        down.wait_recv()
        x_ref[EDGE + SPAN :] = after[:EDGE]

    for copy in tap_copies:
        copy.wait()
    part = c_own.shape[1]
    for z in range(shards):
        taps_ref[0, :, z * part : (z + 1) * part] = c_slots[z]
    for b in range(PAIRS):
        taps_ref[1, :, b * 128 : (b + 1) * 128] = mm(
            taps_ref[0, :, (PAIRS - 1 - b) * 128 : (PAIRS - b) * 128].astype(BF16), flip
        )

    def values_step(i, carry):
        x_low = x_ref[:, lanes(i)]
        x_high = mm(x_low, flip)
        xf_ref[:, lanes(PAIRS - 1 - i)] = x_high.astype(BF16)
        xt_ref[0, lanes(i)] = x_low.astype(F32).T.astype(BF16)
        xt_ref[1, lanes(PAIRS - 1 - i)] = x_high.T.astype(BF16)
        rows = shifted(x_low.astype(F32))
        for s in range(2):
            taps = taps_ref[s, :, lanes(i)]
            for d in range(2):
                mixed = conv(taps, rows[d])
                sig = sigmoid(mixed)
                act = mixed * sig
                vals[2 * i + s, d] = act.astype(BF16)
                slope[2 * i + s, d] = sig + act * (1.0 - sig)
        return carry

    lax.fori_loop(0, PAIRS, values_step, 0)

    for copy in w_copies:
        copy.wait()
    forwards = []
    for k in range(1, chips):
        slot_of = w_slots.at[lax.rem(zero + shards - 2 * k, shards)]
        copy = push(slot_of, slot_of, f_send.at[k], f_recv.at[k], "zero", sibling)
        copy.start()
        forwards.append(copy)

    def unpack(z):
        at = pl.multiple_of(z * rows, 16)
        w_out[pl.ds(at, rows), :128] = w_slots[z, :rows]
        tail = w_slots[z, rows:].astype(F32)
        for q in range(fold):
            moved = pltpu.roll(tail, 128 - 32 * q, 1) if q else tail
            w_out[pl.ds(at + q * fold_rows, fold_rows), 128:] = jnp.where(
                iota(1, (fold_rows, 128)) < HEADS, moved, 0.0
            ).astype(BF16)

    for k in range(chips):
        unpack(lax.rem(zero + shards - 2 * k, shards))
    unpack(sibling)
    for copy in forwards:
        copy.wait()
    for k in range(1, chips):
        unpack(lax.rem(sibling + shards - 2 * k, shards))
    wp_ref[:, :128] = w_out[:, :128]
    wp_ref[:, 128:] = mm(w_out[:, 128:], swap).astype(BF16)
    proj = (mm(x_ref[...], w_out[...]), mm(xf_ref[...], wp_ref[...]))
    loads[3].wait()
    heads_in[...] = jnp.zeros_like(heads_in)
    heads_in[0:1, :HEADS] = alog_ref[...]
    heads_in[1:2, :HEADS] = bias_ref[...]
    place = heads_in[...] + exact_right(heads_in[...], swap)
    rate = jnp.exp(place[0:1])
    rates[0:1] = rate
    dtx = (proj[0] + proj[1])[EDGE : EDGE + SPAN, 128:] + place[1:2]
    dtx_ref[...] = dtx
    delta = softplus(dtx)
    both = jnp.concatenate(
        [ones_where(iota(0) >= iota(1)), ones_where(iota(0) <= iota(1))], axis=0
    )
    within = exact_left(both, -rate * delta)
    ends = jnp.concatenate(
        [
            jnp.broadcast_to(within[SPAN - 1 : SPAN], (SPAN, 128)),
            jnp.broadcast_to(within[SPAN : SPAN + 1], (SPAN, 128)),
        ],
        axis=0,
    )
    spread = jnp.concatenate([jnp.exp(within), jnp.exp(ends - within), delta], axis=0)
    hi, lo = split2(spread)
    wide_low = iota(1, spread.shape) < 64
    stack[...] = jnp.where(
        wide_low, hi.astype(F32), pltpu.roll(lo.astype(F32), 64, 1)
    ).astype(BF16)
    hi, mid, lo = split3(within)
    low_two = iota(1, (256, 128)) < 64
    split[:, :128] = jnp.where(
        low_two, hi.astype(F32), pltpu.roll(mid.astype(F32), 64, 1)
    ).astype(BF16)
    split[:, 128:] = jnp.where(low_two, lo.astype(F32), 0.0).astype(BF16)
    for d in range(2):
        within_t[d] = within[d * 128 : d * 128 + 128].T
    for s in range(2):
        bcx_ref[s] = proj[s][:, :128].astype(BF16).astype(F32)
        bcx = shifted(bcx_ref[s])
        scores = []
        for d in range(2):
            c = 2 * s + d
            mixed = conv(taps_ref[0, :, WIDTH:], bcx[d])
            sig = sigmoid(mixed)
            wide = mixed * sig
            act = wide.astype(BF16)
            bc_slope[c] = sig + wide * (1.0 - sig)
            bc_act[c, 0] = act[:, :STATE]
            bc_act[c, 1] = act[:, STATE:]
            act_t = act.astype(F32).T.astype(BF16)
            bc_t[c] = act_t
            scores.append(mm(act[:, STATE:], act_t[:STATE]))
            own_diag = jnp.sum(jnp.where(iota(0) == iota(1), scores[d], 0.0), axis=1, keepdims=True)
            diag[c] = jnp.broadcast_to(own_diag, (128, 128))
        score[s] = jnp.where(
            iota(0) > iota(1), scores[0], jnp.where(iota(0) < iota(1), scores[1], 0.0)
        )

    def produce(u):
        i, s = lax.div(u, 2), lax.rem(u, 2)
        head = 32 * s + 2 * i
        sel = ones_where(lax.rem(iota(0), 64) == head + jnp.where(iota(1) >= HEAD_DIM, 1, 0))
        wide = mm(stack[...], sel)
        dt = wide[512:]
        dt_b[u] = dt
        g = go_ref[:, lanes(i)].astype(F32)
        for d in range(2):
            e, f = wide[128 * d : 128 * d + 128], wide[256 + 128 * d : 384 + 128 * d]
            e_b[u, d] = e
            f_b[u, d] = f
            step = (vals[u, d].astype(F32) * dt).astype(BF16)
            u_ref[u, d] = step
            fu = (step.astype(F32) * f).astype(BF16)
            fu_ref[u, d] = fu
            eg = (e * g).astype(BF16)
            eg_ref[u, d] = eg
            own[d, u, 0] = mm(bc_t[2 * s + d, :STATE], fu)
            own[1 - d, u, 1] = mm(bc_t[2 * s + d, STATE:], eg)

    def decay_of(u, d):
        at = SPAN - 1 if d == 0 else 0
        return e_b[u, d, at : at + 1]

    chains = ((0, seq, seq + 1), (1, count - 1 - seq, seq - 1))

    def copy_of(d, u, peer):
        return push(
            out_slots.at[d, u], in_slots.at[d, u], c_send.at[d, u], c_recv.at[d, u], "seq", peer
        )

    def forward(t):
        for d, place, peer in chains:
            u = t - LAG * place

            @pl.when((u >= 0) & (u < UNITS))
            def _():
                @pl.when(place == 0)
                def _():
                    out_slots[d, u] = own[d, u].astype(BF16)

                @pl.when(place > 0)
                def _():
                    copy_of(d, u, seq).wait_recv()

                @pl.when((place > 0) & (place < count - 1))
                def _():
                    for q in range(2):
                        dec = decay_of(u, d if q == 0 else 1 - d)
                        out_slots[d, u, q] = (
                            own[d, u, q] + dec * in_slots[d, u, q].astype(F32)
                        ).astype(BF16)

                @pl.when(place < count - 1)
                def _():
                    copy_of(d, u, peer).start()

    def inside(u):
        i, s = lax.div(u, 2), lax.rem(u, 2)
        head = 32 * s + 2 * i
        square = (256, 256)
        line = iota(0, square)
        pick = ones_where(
            (lax.rem(line, 64) == head + jnp.where(iota(1, square) >= 128, 1, 0)) & (line < 192)
        )
        cols = mm(split[...], pick)
        lower = iota(0) >= iota(1)
        low = iota(1) < HEAD_DIM
        go = go_ref[:, lanes(i)]
        none = jnp.zeros((128, 128), BF16)
        g_two = jnp.concatenate([jnp.where(low, go, none), jnp.where(low, none, go)], axis=0)
        steps = jnp.concatenate([u_ref[u, 0], u_ref[u, 1]], axis=0)
        dw = mm_nt(g_two, steps)
        sc = score[s]
        ds = d_score[s]
        below, above = [], []
        for r in range(2):
            at = slice(128 * r, 128 * r + 128)
            gap = jnp.where(
                lower,
                cols[:128, at] - within_t[0, pl.ds(head + r, 1), :],
                cols[128:, at] - within_t[1, pl.ds(head + r, 1), :],
            )
            decay = jnp.exp(gap)
            w = (sc * decay).astype(BF16)
            below.append(w * masks[0])
            above.append(w * masks[1])
            ds = ds + decay * jnp.where(lower, dw[at, :128], dw[at, 128:])
        d_score[s] = ds
        g = go.astype(F32)
        for d, ws in enumerate((below, above)):
            y_two = mm(jnp.concatenate(ws, axis=0), steps[128 * d : 128 * d + 128])
            yoff[u, d] = jnp.where(low, y_two[:128], y_two[128:])
            duo[u, d] = jnp.where(low, mm_tn(ws[0], go), mm_tn(ws[1], go))
            d_diag[2 * s + d] += g * steps[128 * d : 128 * d + 128].astype(F32)

    def back(taps, dm, x, direction):
        zero_rows = jnp.zeros((EDGE, 128), F32)
        wide = jnp.concatenate([zero_rows, dm, zero_rows], axis=0)
        out = taps[0:1] * wide
        sums = [jnp.sum(wide * x, axis=0, keepdims=True)]
        for k in range(1, KERNEL):
            moved = pltpu.roll(wide, EXT - k if direction == 0 else k, 0)
            out = out + taps[k : k + 1] * moved
            sums.append(jnp.sum(moved * x, axis=0, keepdims=True))
        return out, jnp.concatenate(sums + [jnp.zeros((8 - KERNEL, 128), F32)], axis=0)

    def finish(u):
        i, s = lax.div(u, 2), lax.rem(u, 2)
        head = 32 * s + 2 * i
        g = go_ref[:, lanes(i)].astype(F32)
        x = x_ref[:, lanes(i)].astype(F32)
        taps = taps_ref[s, :, lanes(i)]
        dt = dt_b[u]
        y = jnp.zeros((128, 128), F32)
        gi = jnp.zeros((EXT, 128), F32)
        gf = jnp.zeros((8, 128), F32)
        qt = jnp.zeros((128, 128), F32)
        qs, ends = [], []
        for d in range(2):
            c = 2 * s + d
            s_in, g_in = in_slots[d, u, 0], in_slots[1 - d, u, 1]
            step = u_ref[u, d].astype(F32)
            across = mm(bc_act[c, 1], s_in) * e_b[u, d] + yoff[u, d]
            y = y + across + diag[c] * step
            du = duo[u, d] + f_b[u, d] * mm(bc_act[c, 0], g_in)
            qs.append(g * across - step * du)
            du = du + diag[c] * g
            qt = qt + vals[u, d].astype(F32) * du
            d_bc[c, 0] += mm_nt(fu_ref[u, d], g_in)
            d_bc[c, 1] += mm_nt(eg_ref[u, d], s_in)
            leaving = own[d, u, 0] + decay_of(u, d) * s_in.astype(F32)
            ends.append(jnp.sum(leaving * g_in.astype(F32), axis=0, keepdims=True))
            dm = (dt * du).astype(BF16).astype(F32) * slope[u, d]
            more, sums = back(taps, dm, x, d)
            gi = gi + more
            gf = gf + sums
        q = jnp.concatenate(qs + [qt] + ends + [jnp.zeros((6, 128), F32)], axis=0)
        tall = (256, 128)
        sel_t = ones_where(
            iota(1, tall) == head + jnp.where(lax.rem(iota(0, tall), 128) >= HEAD_DIM, 1, 0)
        )
        acc[...] += mm(jnp.concatenate(split2(q), axis=1), sel_t)
        gi_ref[s, :, lanes(i)] = gi
        gf_ref[u] = gf

        @pl.when(s == 0)
        def _():
            y_first[...] = y.astype(BF16).astype(F32)

        @pl.when(s == 1)
        def _():
            out_ref[:, lanes(i)] = (y_first[...] + y.astype(BF16).astype(F32)).astype(BF16)

    lag_all = LAG * (count - 1)

    def slot(t, carry):
        @pl.when(t < UNITS)
        def _():
            produce(t)

        forward(t)

        @pl.when(t < UNITS)
        def _():
            inside(t)

        @pl.when(t >= lag_all)
        def _():
            finish(t - lag_all)

        return carry

    lax.fori_loop(0, UNITS + lag_all, slot, 0)

    end_rows = acc[3 * SPAN : 3 * SPAN + 8]
    dl0 = acc[:SPAN] + jnp.where(iota(0) == SPAN - 1, end_rows[0:1], 0.0)
    dl1 = acc[SPAN : 2 * SPAN] + jnp.where(iota(0) == 0, end_rows[1:2], 0.0)
    both_t = jnp.concatenate(
        [ones_where(iota(0) <= iota(1)), ones_where(iota(0) >= iota(1))], axis=1
    )
    d_log = exact_left(both_t, jnp.concatenate([dl0, dl1], axis=0))
    rate = rates[0:1]
    dtx = dtx_ref[...]
    d_raw = (acc[2 * SPAN : 3 * SPAN] - rate * d_log) * sigmoid(dtx)
    sums = jnp.concatenate(
        [
            jnp.sum(d_log * (-rate * softplus(dtx)), axis=0, keepdims=True),
            jnp.sum(d_raw, axis=0, keepdims=True),
            jnp.zeros((6, 128), F32),
        ],
        axis=0,
    )
    unswap = swap.astype(F32).T.astype(BF16)
    heads = jnp.where(iota(1, (8, 128)) < HEADS, sums, 0.0) + exact_right(sums, unswap)
    ddt = (
        jnp.where(iota(1) < HEADS, d_raw, 0.0).astype(BF16),
        mm(d_raw.astype(BF16), unswap).astype(BF16),
    )
    wides = []
    for s in range(2):
        taps = taps_ref[0, :, WIDTH:]
        gi = jnp.zeros((EXT, 128), F32)
        gf = jnp.zeros((8, 128), F32)
        for d in range(2):
            c = 2 * s + d
            on_diag = jnp.sum(d_diag[c], axis=1, keepdims=True)
            off = iota(0) > iota(1) if d == 0 else iota(0) < iota(1)
            ds = jnp.where(
                off, d_score[s], jnp.where(iota(0) == iota(1), on_diag, 0.0)
            ).astype(BF16)
            db = d_bc[c, 0] + mm_tn(ds, bc_act[c, 1])
            dc = d_bc[c, 1] + mm(ds, bc_act[c, 0])
            dm = jnp.concatenate([db, dc], axis=1).astype(BF16).astype(F32) * bc_slope[c]
            more, some = back(taps, dm, bcx_ref[s], d)
            gi = gi + more
            gf = gf + some
        gi_ref[s, :, WIDTH:] = gi
        gf_ref[UNITS + s] = gf
        edge = jnp.zeros((EDGE, 128), F32)
        wides.append(
            jnp.concatenate(
                [gi, jnp.concatenate([edge, ddt[s].astype(F32), edge], axis=0)], axis=1
            ).astype(BF16)
        )
    g_up = push(
        gi_ref.at[:, pl.ds(EDGE + SPAN, EDGE)], g_before, g_sides.at[0], g_sides.at[1], "seq",
        lax.rem(seq + 1, count),
    )
    g_down = push(
        gi_ref.at[:, pl.ds(0, EDGE)], g_after, g_sides.at[2], g_sides.at[3], "seq",
        lax.rem(seq + count - 1, count),
    )

    def weight_part(z):
        at = pl.ds(pl.multiple_of(z * rows, 16), rows)
        total = mm(xt_ref[0, at], wides[0]) + mm(xt_ref[1, at], wides[1])
        parts[z, :rows] = total[:, :128].astype(BF16)
        parts[z, rows:] = folded(total[:, 128:], fold).astype(BF16)

    pairs = []
    for k in list(range(1, chips)) + [0]:
        z = 2 * lax.rem(chip + k, chips) + 1 - core
        weight_part(z)
        copy = push(
            parts.at[z], pair_in.at[lax.div(z, 2)], p_send.at[k], p_recv.at[k], "zero", sibling
        )
        copy.start()
        pairs.append(copy)
    for k in list(range(1, chips)) + [0]:
        weight_part(2 * lax.rem(chip + k, chips) + core)

    @pl.when(seq < count - 1)
    def _():
        g_up.start()

    @pl.when(seq > 0)
    def _():
        g_down.start()

    @pl.when(seq == 0)
    def _():
        g_before[...] = jnp.zeros_like(g_before)

    @pl.when(seq == count - 1)
    def _():
        g_after[...] = jnp.zeros_like(g_after)

    scatter = []
    for k in range(1, chips):
        there = lax.rem(chip + k, chips)
        pairs[k - 1].wait_send()
        push(
            parts.at[zero], pair_in.at[there], p_send.at[k],
            p_recv.at[lax.rem(chips + there - chip, chips)], "zero", sibling,
        ).wait_recv()
        pair_sum[there] = (
            parts[2 * there + core].astype(F32) + pair_in[there].astype(F32)
        ).astype(BF16)
        copy = push(
            pair_sum.at[there], part_in.at[k], zs.at[0, k], zr.at[0, k], "zero", 2 * there + core
        )
        copy.start()
        scatter.append(copy)
    swapped = exact_right(
        jnp.concatenate([gf_ref[2 * (PAIRS - 1 - i) + 1] for i in range(PAIRS)], axis=0), flip
    )
    small[...] = jnp.zeros_like(small)
    for i in range(PAIRS):
        block = gf_ref[2 * i] + swapped[8 * i : 8 * i + 8]
        small[KERNEL * i : KERNEL * i + KERNEL] = block[:KERNEL]
    block = gf_ref[UNITS] + gf_ref[UNITS + 1]
    small[KERNEL * PAIRS : KERNEL * PAIRS + KERNEL] = block[:KERNEL]
    small[KERNEL * PAIRS + KERNEL : KERNEL * PAIRS + KERNEL + 2] = heads[:2]
    first = []
    for k in range(1, shards):
        peer = lax.rem(zero + k, shards)
        copy = push(small, small_in.at[zero], ms.at[0, k], mr.at[0, k], "zero", peer)
        copy.start()
        first.append(copy)
    small_in[zero] = small[...]
    pairs[-1].wait()
    kept = parts[zero].astype(F32) + pair_in[chip].astype(F32)
    for b in range(PAIRS):
        w_rev[b * 128 : (b + 1) * 128] = mm(
            flip, w_out[(PAIRS - 1 - b) * 128 : (PAIRS - b) * 128]
        ).astype(BF16)

    @pl.when(seq > 0)
    def _():
        g_up.wait_recv()

    @pl.when(seq < count - 1)
    def _():
        g_down.wait_recv()

    def settled(s, at):
        top = gi_ref[s, EDGE : 2 * EDGE, at] + g_before[s, :, at]
        low = gi_ref[s, SPAN : SPAN + EDGE, at] + g_after[s, :, at]
        return jnp.concatenate([top, gi_ref[s, 2 * EDGE : SPAN, at], low], axis=0).astype(BF16)

    gps = [
        jnp.concatenate([settled(s, slice(WIDTH, CHANNELS)), ddt[s]], axis=1) for s in range(2)
    ]

    def hidden_part(i):
        at = slice(i * 128, i * 128 + 128)
        a = (settled(0, at).astype(F32) + mm_nt(gps[0], w_out[at])).astype(BF16)
        b = (settled(1, at).astype(F32) + mm_nt(gps[1], w_rev[at])).astype(BF16)
        gh_ref[:, at] = (a.astype(F32) + b.astype(F32)).astype(BF16)

    for i in range(PAIRS // 2):
        hidden_part(i)
    for copy in scatter:
        copy.wait()
    for k in range(1, chips):
        kept = kept + part_in[k].astype(F32)
    spare = mine.shape[0] - packed
    mine[:packed] = kept.astype(BF16)
    if spare:
        mine[packed:] = jnp.zeros((spare, 128), BF16)
    chunk = mine.shape[0] // count
    third = []
    for k in range(1, count):
        peer = lax.rem(seq + k, count)
        src = mine.at[pl.ds(pl.multiple_of(peer * chunk, 16), chunk)]
        copy = push(src, chunk_in.at[k], ss.at[0, k], sr.at[0, k], "seq", peer)
        copy.start()
        third.append(copy)
    for copy in first:
        copy.wait()
    summed = small_in[0]
    for z in range(1, shards):
        summed = summed + small_in[z]
    small2[...] = summed
    second = []
    for k in range(1, count):
        peer = lax.rem(seq + k, count)
        copy = push(small2, small2_in.at[seq], ms.at[1, shards + k], mr.at[1, shards + k], "seq", peer)
        copy.start()
        second.append(copy)
    small2_in[seq] = small2[...]
    for i in range(PAIRS // 2, PAIRS):
        hidden_part(i)
    for copy in third:
        copy.wait()
    here = pl.ds(pl.multiple_of(seq * chunk, 16), chunk)
    summed = mine[here].astype(F32)
    for k in range(1, count):
        summed = summed + chunk_in[k].astype(F32)
    gathered[here] = summed.astype(BF16)
    third = []
    for k in range(1, count):
        peer = lax.rem(seq + k, count)
        copy = push(gathered.at[here], gathered.at[here], ss.at[1, k], sr.at[1, k], "seq", peer)
        copy.start()
        third.append(copy)
    for copy in second:
        copy.wait()
    summed = small2_in[0]
    for z in range(1, count):
        summed = summed + small2_in[z]
    total2[...] = summed
    for d, place, peer in chains:

        @pl.when(place < count - 1)
        def _():
            def sent(u, carry):
                copy_of(d, u, peer).wait_send()
                return carry

            lax.fori_loop(0, UNITS, sent, 0)

    @pl.when(seq < count - 1)
    def _():
        up.wait_send()

    @pl.when(seq > 0)
    def _():
        down.wait_send()

    @pl.when(seq < count - 1)
    def _():
        g_up.wait_send()

    @pl.when(seq > 0)
    def _():
        g_down.wait_send()

    for copy in third:
        copy.wait()
    full[...] = gathered[...]


def emit_kernel(
    shards, fold, out_ref, gh_ref, full, total, out_hbm, gh_hbm, gw_ref, gc_ref, gd_ref,
    wide, taps, sems,
):
    copies = [
        pltpu.make_async_copy(out_ref, out_hbm, sems.at[0]),
        pltpu.make_async_copy(gh_ref, gh_hbm, sems.at[1]),
    ]
    for copy in copies:
        copy.start()
    rows = WIDTH // shards
    fold_rows = rows // fold
    tail = full[rows : rows + fold_rows].astype(F32)
    wide[...] = jnp.zeros_like(wide)
    wide[:rows, :128] = full[:rows].astype(F32)
    for q in range(fold):
        moved = pltpu.roll(tail, 128 - 32 * q, 1) if q else tail
        wide[q * fold_rows : (q + 1) * fold_rows, 128:] = moved
    gw_ref[...] = wide[...].T[: gw_ref.shape[0], :rows]
    gd_ref[...] = total[KERNEL * PAIRS + KERNEL : KERNEL * PAIRS + KERNEL + 2, :HEADS]
    for i in range(PAIRS + 1):
        taps[:, i * 128 : i * 128 + 128] = total[KERNEL * i : KERNEL * i + KERNEL]
    zero = lax.axis_index("zero")
    width = gc_ref.shape[1]
    for z in range(shards):

        @pl.when(zero == z)
        def _():
            gc_ref[...] = taps[:, z * width : (z + 1) * width]

    for copy in copies:
        copy.wait()


def spec(space):
    return pl.BlockSpec(memory_space=space)


SQ4 = (4, 128, 128)
SQ2 = (2, 128, 128)
TILES = (UNITS, 2, 128, 128)


def per_device(hidden, grad_out, w_proj, conv_w, a_log, dt_bias):
    assert hidden.shape[:2] == (1, SPAN)
    count, shards = lax.axis_size("seq"), lax.axis_size("zero")
    chips = shards // 2
    rows, columns = w_proj.shape
    part = CHANNELS // shards
    fold = 4 if rows % 64 == 0 else 1
    packed = rows + rows // fold
    step = 16 * count
    padded = -(-packed // step) * step
    lines = 48
    wide_rows = -(-rows // 128) * 128
    pieces = (2, UNITS, 2, STATE, 128)
    edges = (2, EDGE, CHANNELS)
    scratch = [
        ((SPAN, WIDTH), BF16), ((SPAN, WIDTH), BF16), ((columns, rows), BF16),
        ((KERNEL, part), BF16), ((256, wide_rows), F32),
        ((EXT, WIDTH), BF16), ((EXT, WIDTH), BF16), ((2, WIDTH, EXT), BF16),
        ((2, 8, CHANNELS), F32), ((WIDTH, 256), BF16), ((WIDTH, 256), BF16), ((WIDTH, 256), BF16),
        ((shards, packed, 128), BF16), ((8, part), F32), ((shards, 8, part), F32),
        ((2 * EDGE, WIDTH), BF16), ((2 * EDGE, WIDTH), BF16),
        (TILES, BF16), (TILES, F32), (TILES, BF16), (TILES, BF16), (TILES, BF16),
        (TILES, F32), (TILES, F32), (TILES, F32), (TILES, F32), ((UNITS, 128, 128), F32),
        (pieces, F32), (pieces, BF16), (pieces, BF16),
        ((8, 128), F32), ((8, 128), F32), ((128, 128), F32), ((5 * 128, 128), BF16), ((256, 256), BF16),
        (SQ2, F32), (SQ2, F32), (SQ4, F32), ((4, 2, 128, STATE), BF16), (SQ4, BF16),
        (SQ4, F32), (SQ2, BF16), (SQ2, F32), (SQ4, F32), ((4, 2, 128, STATE), F32),
        ((3 * SPAN + 8, 128), F32), ((128, 128), F32),
        ((2, EXT, CHANNELS), F32), ((UNITS + 2, 8, 128), F32), ((2, EXT, 128), F32),
        (edges, F32), (edges, F32),
        ((shards, packed, 128), BF16), ((chips, packed, 128), BF16),
        ((chips, packed, 128), BF16), ((chips, packed, 128), BF16),
        ((padded, 128), BF16), ((count, padded // count, 128), BF16), ((padded, 128), BF16),
        ((lines, 128), F32), ((shards, lines, 128), F32),
        ((lines, 128), F32), ((count, lines, 128), F32),
    ]
    sems = [
        (4,), (4,), (chips,), (chips,), (chips,), (chips,), (shards,), (shards,),
        (2, UNITS), (2, UNITS), (4,), (chips,), (chips,), (1, chips), (1, chips),
        (2, count), (2, count), (2, shards + count), (2, shards + count),
    ]
    anywhere = spec(pl.ANY)
    outs = pl.pallas_call(
        functools.partial(whole_kernel, shards, count, fold),
        out_shape=[
            jax.ShapeDtypeStruct((SPAN, WIDTH), BF16), jax.ShapeDtypeStruct((SPAN, WIDTH), BF16),
            jax.ShapeDtypeStruct((padded, 128), BF16), jax.ShapeDtypeStruct((lines, 128), F32),
        ],
        in_specs=[spec(pltpu.HBM)] * 4 + [spec(pltpu.VMEM)] * 2,
        scratch_shapes=[pltpu.VMEM(s, t) for s, t in scratch]
        + [pltpu.SemaphoreType.DMA(s) for s in sems],
        compiler_params=pltpu.CompilerParams(
            vmem_limit_bytes=54300 * 1024, collective_id=0, has_side_effects=True
        ),
    )(hidden[0], grad_out[0], w_proj.T, conv_w, a_log[None], dt_bias[None])
    output, grad_hidden, share_w, share_c, grad_heads = pl.pallas_call(
        functools.partial(emit_kernel, shards, fold),
        out_shape=[
            jax.ShapeDtypeStruct((SPAN, WIDTH), BF16), jax.ShapeDtypeStruct((SPAN, WIDTH), BF16),
            jax.ShapeDtypeStruct((columns, rows), F32),
            jax.ShapeDtypeStruct((KERNEL, part), F32), jax.ShapeDtypeStruct((2, HEADS), F32),
        ],
        out_specs=[anywhere] * 2 + [spec(pltpu.VMEM)] * 3,
        scratch_shapes=[
            pltpu.VMEM((wide_rows, 256), F32), pltpu.VMEM((KERNEL, CHANNELS), F32),
            pltpu.SemaphoreType.DMA((2,)),
        ],
        compiler_params=pltpu.CompilerParams(vmem_limit_bytes=8 * 1024 * 1024),
    )(*outs)
    return (output[None], grad_hidden[None], share_w.T, share_c, grad_heads)


def solution(mesh):
    return jax.shard_map(
        per_device,
        mesh=mesh,
        in_specs=(
            P(("grp", "zero"), "seq", None),
            P(("grp", "zero"), "seq", None),
            P("zero", None),
            P(None, "zero"),
            P(),
            P(),
        ),
        out_specs=(
            P(("grp", "zero"), "seq", None),
            P(("grp", "zero"), "seq", None),
            P(("grp", "zero"), None),
            P("grp", "zero"),
            P("grp", None),
        ),
        check_vma=False,
    )
```

```python
import functools
import jax
import jax.numpy as jnp
from jax import lax
from jax.experimental import pallas as pl
from jax.experimental.pallas import tpu as pltpu
from jax.sharding import PartitionSpec as P

WIDTH = 1280
STATE = 64
HEAD_DIM = 64
SPAN = 128
KERNEL = 4
HEADS = 20
PAIRS = WIDTH // 128
CHANNELS = WIDTH + 2 * STATE
EDGE = 8
EXT = SPAN + 2 * EDGE
F32 = jnp.float32
BF16 = jnp.bfloat16
UNITS = 2 * PAIRS
LAG = 2


def mm(a, b):
    return jnp.dot(a, b, preferred_element_type=F32)


def mm_nt(a, b):
    return lax.dot_general(a, b, (((1,), (1,)), ((), ())), preferred_element_type=F32)


def mm_tn(a, b):
    return lax.dot_general(a, b, (((0,), (0,)), ((), ())), preferred_element_type=F32)


def exact(a, b):
    return jnp.dot(a, b, preferred_element_type=F32, precision=lax.Precision.HIGHEST)


def iota(dim, shape=(128, 128)):
    return lax.broadcasted_iota(jnp.int32, shape, dim)


def mirror(dtype=BF16):
    return jnp.where(iota(0) + iota(1) == 127, 1.0, 0.0).astype(dtype)


def softplus(x):
    return jnp.maximum(x, 0.0) + jnp.log1p(jnp.exp(-jnp.abs(x)))


def sigmoid(x):
    return 1.0 / (1.0 + jnp.exp(-x))


def shifted(x):
    back = [x[EDGE : EDGE + SPAN]]
    fore = [back[0]]
    for k in range(1, KERNEL):
        back.append(pltpu.roll(x, k, 0)[EDGE : EDGE + SPAN])
        fore.append(pltpu.roll(x, EXT - k, 0)[EDGE : EDGE + SPAN])
    return back, fore


def conv(taps, rows):
    out = taps[0:1] * rows[0]
    for k in range(1, KERNEL):
        out = out + taps[k : k + 1] * rows[k]
    return out


def lanes(i):
    return pl.ds(pl.multiple_of(i * 128, 128), 128)


MESH = pl.DeviceIdType.MESH


def greet_all(sizes):
    barrier = pltpu.get_barrier_semaphore()
    for axis, size in sizes:
        me = lax.axis_index(axis)
        for k in range(1, size):
            pl.semaphore_signal(
                barrier, inc=1, device_id={axis: lax.rem(me + k, size)}, device_id_type=MESH
            )
    pl.semaphore_wait(barrier, sum(size - 1 for _, size in sizes))


def push(src, dst, send, recv, axis, peer):
    return pltpu.make_async_remote_copy(
        src_ref=src,
        dst_ref=dst,
        send_sem=send,
        recv_sem=recv,
        device_id={axis: peer},
        device_id_type=MESH,
    )


def split2(x):
    hi = x.astype(BF16)
    return hi, (x - hi.astype(F32)).astype(BF16)


def split3(x):
    hi = x.astype(BF16)
    rest = x - hi.astype(F32)
    mid = rest.astype(BF16)
    return hi, mid, (rest - mid.astype(F32)).astype(BF16)


def exact_left(a, x):
    n = x.shape[1]
    out = mm(a, jnp.concatenate(split3(x), axis=1))
    return out[:, :n] + out[:, n : 2 * n] + out[:, 2 * n :]


def exact_right(x, b):
    n = x.shape[0]
    out = mm(jnp.concatenate(split3(x), axis=0), b)
    return out[:n] + out[n : 2 * n] + out[2 * n :]


def ones_where(keep):
    return jnp.where(keep, 1.0, 0.0).astype(BF16)


def strand_swap():
    k, lane = iota(0), iota(1)
    return ones_where((lane >= 32) & (lane < 32 + HEADS) & (k + lane == 31 + HEADS))


def folded(tail, fold):
    size = tail.shape[0] // fold
    out = tail[:size]
    for q in range(1, fold):
        out = out + pltpu.roll(tail[q * size : (q + 1) * size], 32 * q, 1)
    return out


def whole_kernel(
    shards, count, fold,
    hid_hbm, go_hbm, wt_hbm, c_hbm, alog_ref, bias_ref,
    out_ref, gh_ref, full, total2,
    hid_ref, go_ref, wt_in, c_in, wt_pad,
    x_ref, xf_ref, xt_ref, taps_ref, wp_ref, w_out, w_rev, w_slots, c_own, c_slots, before, after,
    vals, slope, u_ref, fu_ref, eg_ref, yoff, duo, e_b, f_b, dt_b,
    own, in_slots, out_slots,
    heads_in, rates, dtx_ref, stack, split, within_t, score, diag, bc_act, bc_t, bc_slope, masks,
    d_score, d_diag, d_bc, acc,
    gi_ref, gf_ref, bcx_ref, g_before, g_after, parts, pair_in, pair_sum, part_in, mine, chunk_in, gathered,
    small, small_in, small2, small2_in,
    local, sides, w_send, w_recv, f_send, f_recv, t_send, t_recv, c_send, c_recv,
    g_sides, p_send, p_recv, zs, zr, ss, sr, ms, mr,
):
    seq, zero = lax.axis_index("seq"), lax.axis_index("zero")
    core = lax.rem(zero, 2)
    chip = lax.div(zero, 2)
    chips = shards // 2
    sibling = zero + 1 - 2 * core
    rows = WIDTH // shards
    fold_rows = rows // fold
    packed = rows + fold_rows
    loads = [
        pltpu.make_async_copy(src, dst, local.at[n])
        for n, (src, dst) in enumerate(
            ((c_hbm, c_in), (wt_hbm, wt_in), (hid_hbm, hid_ref), (go_hbm, go_ref))
        )
    ]
    for load in loads:
        load.start()
    c_own[...] = jnp.zeros_like(c_own)
    wt_pad[...] = jnp.zeros_like(wt_pad)
    loads[0].wait()
    c_own[:KERNEL] = c_in[...].astype(F32)
    loads[1].wait()
    wt_pad[: wt_in.shape[0], :rows] = wt_in[...].astype(F32)
    w_own = wt_pad[...].T
    w_slots[zero, :rows] = w_own[:rows, :128].astype(BF16)
    w_slots[zero, rows:] = folded(w_own[:rows, 128:], fold).astype(BF16)
    greet_all((("zero", shards), ("seq", count)))
    tap_copies = []
    for k in range(1, shards):
        peer = lax.rem(zero + k, shards)
        copy = push(c_own, c_slots.at[zero], t_send.at[k], t_recv.at[k], "zero", peer)
        copy.start()
        tap_copies.append(copy)
    loads[2].wait()
    up = push(
        hid_ref.at[pl.ds(SPAN - 2 * EDGE, 2 * EDGE)], before, sides.at[0], sides.at[1], "seq",
        lax.rem(seq + 1, count),
    )
    down = push(
        hid_ref.at[pl.ds(0, 2 * EDGE)], after, sides.at[2], sides.at[3], "seq",
        lax.rem(seq + count - 1, count),
    )

    @pl.when(seq < count - 1)
    def _():
        up.start()

    @pl.when(seq > 0)
    def _():
        down.start()

    w_copies = []
    for k in range(chips):
        peer = lax.rem(zero + 2 * k, shards) if k else sibling
        copy = push(w_slots.at[zero], w_slots.at[zero], w_send.at[k], w_recv.at[k], "zero", peer)
        copy.start()
        w_copies.append(copy)
    c_slots[zero] = c_own[...]
    w_out[:, 128:] = jnp.zeros((WIDTH, 128), BF16)
    x_ref[EDGE : EDGE + SPAN] = hid_ref[...]
    flip = mirror()
    swap = strand_swap()
    masks[0] = ones_where(iota(0) > iota(1))
    masks[1] = ones_where(iota(0) < iota(1))
    d_score[...] = jnp.zeros_like(d_score)
    d_diag[...] = jnp.zeros_like(d_diag)
    d_bc[...] = jnp.zeros_like(d_bc)
    acc[...] = jnp.zeros_like(acc)

    @pl.when(seq == 0)
    def _():
        x_ref[:EDGE] = jnp.zeros((EDGE, WIDTH), BF16)
        in_slots[0] = jnp.zeros(in_slots.shape[1:], BF16)

    @pl.when(seq > 0)
    def _():
        up.wait_recv()
        x_ref[:EDGE] = before[EDGE:]

    @pl.when(seq == count - 1)
    def _():
        x_ref[EDGE + SPAN :] = jnp.zeros((EDGE, WIDTH), BF16)
        in_slots[1] = jnp.zeros(in_slots.shape[1:], BF16)

    @pl.when(seq < count - 1)
    def _():
        down.wait_recv()
        x_ref[EDGE + SPAN :] = after[:EDGE]

    for copy in tap_copies:
        copy.wait()
    part = c_own.shape[1]
    for z in range(shards):
        taps_ref[0, :, z * part : (z + 1) * part] = c_slots[z]
    for b in range(PAIRS):
        taps_ref[1, :, b * 128 : (b + 1) * 128] = mm(
            taps_ref[0, :, (PAIRS - 1 - b) * 128 : (PAIRS - b) * 128].astype(BF16), flip
        )

    def values_step(i, carry):
        x_low = x_ref[:, lanes(i)]
        x_high = mm(x_low, flip)
        xf_ref[:, lanes(PAIRS - 1 - i)] = x_high.astype(BF16)
        xt_ref[0, lanes(i)] = x_low.astype(F32).T.astype(BF16)
        xt_ref[1, lanes(PAIRS - 1 - i)] = x_high.T.astype(BF16)
        rows = shifted(x_low.astype(F32))
        for s in range(2):
            taps = taps_ref[s, :, lanes(i)]
            for d in range(2):
                mixed = conv(taps, rows[d])
                sig = sigmoid(mixed)
                act = mixed * sig
                vals[2 * i + s, d] = act.astype(BF16)
                slope[2 * i + s, d] = sig + act * (1.0 - sig)
        return carry

    lax.fori_loop(0, PAIRS, values_step, 0)

    for copy in w_copies:
        copy.wait()
    forwards = []
    for k in range(1, chips):
        slot_of = w_slots.at[lax.rem(zero + shards - 2 * k, shards)]
        copy = push(slot_of, slot_of, f_send.at[k], f_recv.at[k], "zero", sibling)
        copy.start()
        forwards.append(copy)

    def unpack(z):
        at = pl.multiple_of(z * rows, 16)
        w_out[pl.ds(at, rows), :128] = w_slots[z, :rows]
        tail = w_slots[z, rows:].astype(F32)
        for q in range(fold):
            moved = pltpu.roll(tail, 128 - 32 * q, 1) if q else tail
            w_out[pl.ds(at + q * fold_rows, fold_rows), 128:] = jnp.where(
                iota(1, (fold_rows, 128)) < HEADS, moved, 0.0
            ).astype(BF16)

    for k in range(chips):
        unpack(lax.rem(zero + shards - 2 * k, shards))
    unpack(sibling)
    for copy in forwards:
        copy.wait()
    for k in range(1, chips):
        unpack(lax.rem(sibling + shards - 2 * k, shards))
    wp_ref[:, :128] = w_out[:, :128]
    wp_ref[:, 128:] = mm(w_out[:, 128:], swap).astype(BF16)
    proj = (mm(x_ref[...], w_out[...]), mm(xf_ref[...], wp_ref[...]))
    loads[3].wait()
    heads_in[...] = jnp.zeros_like(heads_in)
    heads_in[0:1, :HEADS] = alog_ref[...]
    heads_in[1:2, :HEADS] = bias_ref[...]
    place = heads_in[...] + exact_right(heads_in[...], swap)
    rate = jnp.exp(place[0:1])
    rates[0:1] = rate
    dtx = (proj[0] + proj[1])[EDGE : EDGE + SPAN, 128:] + place[1:2]
    dtx_ref[...] = dtx
    delta = softplus(dtx)
    both = jnp.concatenate(
        [ones_where(iota(0) >= iota(1)), ones_where(iota(0) <= iota(1))], axis=0
    )
    within = exact_left(both, -rate * delta)
    ends = jnp.concatenate(
        [
            jnp.broadcast_to(within[SPAN - 1 : SPAN], (SPAN, 128)),
            jnp.broadcast_to(within[SPAN : SPAN + 1], (SPAN, 128)),
        ],
        axis=0,
    )
    spread = jnp.concatenate([jnp.exp(within), jnp.exp(ends - within), delta], axis=0)
    hi, lo = split2(spread)
    wide_low = iota(1, spread.shape) < 64
    stack[...] = jnp.where(
        wide_low, hi.astype(F32), pltpu.roll(lo.astype(F32), 64, 1)
    ).astype(BF16)
    hi, mid, lo = split3(within)
    low_two = iota(1, (256, 128)) < 64
    split[:, :128] = jnp.where(
        low_two, hi.astype(F32), pltpu.roll(mid.astype(F32), 64, 1)
    ).astype(BF16)
    split[:, 128:] = jnp.where(low_two, lo.astype(F32), 0.0).astype(BF16)
    for d in range(2):
        within_t[d] = within[d * 128 : d * 128 + 128].T
    for s in range(2):
        bcx_ref[s] = proj[s][:, :128].astype(BF16).astype(F32)
        bcx = shifted(bcx_ref[s])
        scores = []
        for d in range(2):
            c = 2 * s + d
            mixed = conv(taps_ref[0, :, WIDTH:], bcx[d])
            sig = sigmoid(mixed)
            wide = mixed * sig
            act = wide.astype(BF16)
            bc_slope[c] = sig + wide * (1.0 - sig)
            bc_act[c, 0] = act[:, :STATE]
            bc_act[c, 1] = act[:, STATE:]
            act_t = act.astype(F32).T.astype(BF16)
            bc_t[c] = act_t
            scores.append(mm(act[:, STATE:], act_t[:STATE]))
            own_diag = jnp.sum(jnp.where(iota(0) == iota(1), scores[d], 0.0), axis=1, keepdims=True)
            diag[c] = jnp.broadcast_to(own_diag, (128, 128))
        score[s] = jnp.where(
            iota(0) > iota(1), scores[0], jnp.where(iota(0) < iota(1), scores[1], 0.0)
        )

    def produce(i):
        line, lane = iota(0, (128, 256)), iota(1, (128, 256))
        head = 2 * i + jnp.where(lane >= 128, 32, 0) + jnp.where(lax.rem(lane, 128) >= HEAD_DIM, 1, 0)
        both_wide = mm(stack[...], ones_where(lax.rem(line, 64) == head))
        g = go_ref[:, lanes(i)].astype(F32)
        for s in range(2):
            u = 2 * i + s
            wide = both_wide[:, 128 * s : 128 * s + 128]
            dt = wide[512:]
            dt_b[u] = dt
            for d in range(2):
                e, f = wide[128 * d : 128 * d + 128], wide[256 + 128 * d : 384 + 128 * d]
                e_b[u, d] = e
                f_b[u, d] = f
                step = (vals[u, d].astype(F32) * dt).astype(BF16)
                u_ref[u, d] = step
                fu = (step.astype(F32) * f).astype(BF16)
                fu_ref[u, d] = fu
                eg = (e * g).astype(BF16)
                eg_ref[u, d] = eg
                own[d, i, s, 0] = mm(bc_t[2 * s + d, :STATE], fu)
                own[1 - d, i, s, 1] = mm(bc_t[2 * s + d, STATE:], eg)

    def decay_of(u, d):
        at = SPAN - 1 if d == 0 else 0
        return e_b[u, d, at : at + 1]

    chains = ((0, seq, seq + 1), (1, count - 1 - seq, seq - 1))

    def copy_of(d, i, peer):
        return push(
            out_slots.at[d, i], in_slots.at[d, i], c_send.at[d, i], c_recv.at[d, i], "seq", peer
        )

    def forward(t):
        for d, place, peer in chains:
            i = t - LAG * place

            @pl.when((i >= 0) & (i < PAIRS))
            def _():
                @pl.when(place == 0)
                def _():
                    out_slots[d, i] = own[d, i].astype(BF16)

                @pl.when(place > 0)
                def _():
                    copy_of(d, i, seq).wait_recv()

                @pl.when((place > 0) & (place < count - 1))
                def _():
                    for s in range(2):
                        for q in range(2):
                            dec = decay_of(2 * i + s, d if q == 0 else 1 - d)
                            out_slots[d, i, s, q] = (
                                own[d, i, s, q] + dec * in_slots[d, i, s, q].astype(F32)
                            ).astype(BF16)

                @pl.when(place < count - 1)
                def _():
                    copy_of(d, i, peer).start()

    def inside(i):
        lower = iota(0) >= iota(1)
        low = iota(1) < HEAD_DIM
        go = go_ref[:, lanes(i)]
        g = go.astype(F32)
        none = jnp.zeros((128, 128), BF16)
        g_two = jnp.concatenate([jnp.where(low, go, none), jnp.where(low, none, go)], axis=0)
        square = (256, 256)
        line = iota(0, square)
        kept_ins = []
        for s in range(2):
            u = 2 * i + s
            head = 32 * s + 2 * i
            pick = ones_where(
                (lax.rem(line, 64) == head + jnp.where(iota(1, square) >= 128, 1, 0)) & (line < 192)
            )
            cols = mm(split[...], pick)
            steps = jnp.concatenate([u_ref[u, 0], u_ref[u, 1]], axis=0)
            dw = mm_nt(g_two, steps)
            sc = score[s]
            ds = jnp.zeros((128, 128), F32)
            below, above = [], []
            for r in range(2):
                at = slice(128 * r, 128 * r + 128)
                gap = jnp.where(
                    lower,
                    cols[:128, at] - within_t[0, pl.ds(head + r, 1), :],
                    cols[128:, at] - within_t[1, pl.ds(head + r, 1), :],
                )
                decay = jnp.exp(gap)
                w = (sc * decay).astype(BF16)
                below.append(w * masks[0])
                above.append(w * masks[1])
                ds = ds + decay * jnp.where(lower, dw[at, :128], dw[at, 128:])
            for d, ws in enumerate((below, above)):
                step = steps[128 * d : 128 * d + 128]
                y_two = mm(jnp.concatenate(ws, axis=0), step)
                kept_ins.append(
                    (
                        jnp.where(low, y_two[:128], y_two[128:]),
                        jnp.where(low, mm_tn(ws[0], go), mm_tn(ws[1], go)),
                        g * step.astype(F32),
                    )
                )
            kept_ins.append(ds)
        for s in range(2):
            for d in range(2):
                y_two, du, on_diag = kept_ins[3 * s + d]
                yoff[2 * i + s, d] = y_two
                duo[2 * i + s, d] = du
                d_diag[2 * s + d] += on_diag
            d_score[s] += kept_ins[3 * s + 2]

    def back(taps, dm, x, direction):
        zero_rows = jnp.zeros((EDGE, 128), F32)
        wide = jnp.concatenate([zero_rows, dm, zero_rows], axis=0)
        out = taps[0:1] * wide
        sums = [jnp.sum(wide * x, axis=0, keepdims=True)]
        for k in range(1, KERNEL):
            moved = pltpu.roll(wide, EXT - k if direction == 0 else k, 0)
            out = out + taps[k : k + 1] * moved
            sums.append(jnp.sum(moved * x, axis=0, keepdims=True))
        return out, jnp.concatenate(sums + [jnp.zeros((8 - KERNEL, 128), F32)], axis=0)

    def finish(i):
        g = go_ref[:, lanes(i)].astype(F32)
        x = x_ref[:, lanes(i)].astype(F32)
        tall = (512, 128)
        hold = lax.rem(iota(0, tall), 128)
        sel_t = ones_where(
            iota(1, tall)
            == 2 * i + jnp.where(iota(0, tall) >= 256, 32, 0) + jnp.where(hold >= HEAD_DIM, 1, 0)
        )
        ys, parts_of, adds = [], [], []
        for s in range(2):
            u = 2 * i + s
            taps = taps_ref[s, :, lanes(i)]
            dt = dt_b[u]
            y = jnp.zeros((128, 128), F32)
            gi = jnp.zeros((EXT, 128), F32)
            gf = jnp.zeros((8, 128), F32)
            qt = jnp.zeros((128, 128), F32)
            qs, ends = [], []
            for d in range(2):
                c = 2 * s + d
                s_in, g_in = in_slots[d, i, s, 0], in_slots[1 - d, i, s, 1]
                step = u_ref[u, d].astype(F32)
                across = mm(bc_act[c, 1], s_in) * e_b[u, d] + yoff[u, d]
                y = y + across + diag[c] * step
                du = duo[u, d] + f_b[u, d] * mm(bc_act[c, 0], g_in)
                qs.append(g * across - step * du)
                du = du + diag[c] * g
                qt = qt + vals[u, d].astype(F32) * du
                adds.append((c, mm_nt(fu_ref[u, d], g_in), mm_nt(eg_ref[u, d], s_in)))
                leaving = own[d, i, s, 0] + decay_of(u, d) * s_in.astype(F32)
                ends.append(jnp.sum(leaving * g_in.astype(F32), axis=0, keepdims=True))
                dm = (dt * du).astype(BF16).astype(F32) * slope[u, d]
                more, sums = back(taps, dm, x, d)
                gi = gi + more
                gf = gf + sums
            q = jnp.concatenate(qs + [qt] + ends + [jnp.zeros((6, 128), F32)], axis=0)
            parts_of.extend(split2(q))
            ys.append(y.astype(BF16).astype(F32))
            adds.append((s, gi, gf))
        totals = mm(jnp.concatenate(parts_of, axis=1), sel_t)
        for s in range(2):
            for c, db, dc in adds[3 * s : 3 * s + 2]:
                d_bc[c, 0] += db
                d_bc[c, 1] += dc
            _, gi, gf = adds[3 * s + 2]
            gi_ref[s, :, lanes(i)] = gi
            gf_ref[2 * i + s] = gf
        acc[...] += totals
        out_ref[:, lanes(i)] = (ys[0] + ys[1]).astype(BF16)

    lag_all = LAG * (count - 1) + 1

    def slot(t, first, last):
        if last:
            finish(t - lag_all)
        if first:
            inside(t - 1)
            produce(t)
        forward(t)

    def run(start, stop, first, last):
        def body(t, carry):
            slot(t, first, last)
            return carry

        if stop > start:
            lax.fori_loop(start, stop, body, 0)

    produce(0)
    forward(0)
    split_at = min(max(lag_all, 1), PAIRS)
    run(1, split_at, True, False)
    run(split_at, PAIRS, True, True)

    def idle(t, carry):
        forward(t)
        return carry

    inside(PAIRS - 1)
    if lag_all > PAIRS:
        lax.fori_loop(PAIRS, lag_all, idle, 0)
    run(max(PAIRS, lag_all), PAIRS + lag_all, False, True)

    end_rows = acc[3 * SPAN : 3 * SPAN + 8]
    dl0 = acc[:SPAN] + jnp.where(iota(0) == SPAN - 1, end_rows[0:1], 0.0)
    dl1 = acc[SPAN : 2 * SPAN] + jnp.where(iota(0) == 0, end_rows[1:2], 0.0)
    both_t = jnp.concatenate(
        [ones_where(iota(0) <= iota(1)), ones_where(iota(0) >= iota(1))], axis=1
    )
    d_log = exact_left(both_t, jnp.concatenate([dl0, dl1], axis=0))
    rate = rates[0:1]
    dtx = dtx_ref[...]
    d_raw = (acc[2 * SPAN : 3 * SPAN] - rate * d_log) * sigmoid(dtx)
    sums = jnp.concatenate(
        [
            jnp.sum(d_log * (-rate * softplus(dtx)), axis=0, keepdims=True),
            jnp.sum(d_raw, axis=0, keepdims=True),
            jnp.zeros((6, 128), F32),
        ],
        axis=0,
    )
    unswap = swap.astype(F32).T.astype(BF16)
    heads = jnp.where(iota(1, (8, 128)) < HEADS, sums, 0.0) + exact_right(sums, unswap)
    ddt = (
        jnp.where(iota(1) < HEADS, d_raw, 0.0).astype(BF16),
        mm(d_raw.astype(BF16), unswap).astype(BF16),
    )
    wides = []
    for s in range(2):
        taps = taps_ref[0, :, WIDTH:]
        gi = jnp.zeros((EXT, 128), F32)
        gf = jnp.zeros((8, 128), F32)
        for d in range(2):
            c = 2 * s + d
            on_diag = jnp.sum(d_diag[c], axis=1, keepdims=True)
            off = iota(0) > iota(1) if d == 0 else iota(0) < iota(1)
            ds = jnp.where(
                off, d_score[s], jnp.where(iota(0) == iota(1), on_diag, 0.0)
            ).astype(BF16)
            db = d_bc[c, 0] + mm_tn(ds, bc_act[c, 1])
            dc = d_bc[c, 1] + mm(ds, bc_act[c, 0])
            dm = jnp.concatenate([db, dc], axis=1).astype(BF16).astype(F32) * bc_slope[c]
            more, some = back(taps, dm, bcx_ref[s], d)
            gi = gi + more
            gf = gf + some
        gi_ref[s, :, WIDTH:] = gi
        gf_ref[UNITS + s] = gf
        edge = jnp.zeros((EDGE, 128), F32)
        wides.append(
            jnp.concatenate(
                [gi, jnp.concatenate([edge, ddt[s].astype(F32), edge], axis=0)], axis=1
            ).astype(BF16)
        )
    g_up = push(
        gi_ref.at[:, pl.ds(EDGE + SPAN, EDGE)], g_before, g_sides.at[0], g_sides.at[1], "seq",
        lax.rem(seq + 1, count),
    )
    g_down = push(
        gi_ref.at[:, pl.ds(0, EDGE)], g_after, g_sides.at[2], g_sides.at[3], "seq",
        lax.rem(seq + count - 1, count),
    )

    def weight_part(z):
        at = pl.ds(pl.multiple_of(z * rows, 16), rows)
        total = mm(xt_ref[0, at], wides[0]) + mm(xt_ref[1, at], wides[1])
        parts[z, :rows] = total[:, :128].astype(BF16)
        parts[z, rows:] = folded(total[:, 128:], fold).astype(BF16)

    pairs = []
    for k in list(range(1, chips)) + [0]:
        z = 2 * lax.rem(chip + k, chips) + 1 - core
        weight_part(z)
        copy = push(
            parts.at[z], pair_in.at[lax.div(z, 2)], p_send.at[k], p_recv.at[k], "zero", sibling
        )
        copy.start()
        pairs.append(copy)
    for k in list(range(1, chips)) + [0]:
        weight_part(2 * lax.rem(chip + k, chips) + core)

    @pl.when(seq < count - 1)
    def _():
        g_up.start()

    @pl.when(seq > 0)
    def _():
        g_down.start()

    @pl.when(seq == 0)
    def _():
        g_before[...] = jnp.zeros_like(g_before)

    @pl.when(seq == count - 1)
    def _():
        g_after[...] = jnp.zeros_like(g_after)

    scatter = []
    for k in range(1, chips):
        there = lax.rem(chip + k, chips)
        pairs[k - 1].wait_send()
        push(
            parts.at[zero], pair_in.at[there], p_send.at[k],
            p_recv.at[lax.rem(chips + there - chip, chips)], "zero", sibling,
        ).wait_recv()
        pair_sum[there] = (
            parts[2 * there + core].astype(F32) + pair_in[there].astype(F32)
        ).astype(BF16)
        copy = push(
            pair_sum.at[there], part_in.at[k], zs.at[0, k], zr.at[0, k], "zero", 2 * there + core
        )
        copy.start()
        scatter.append(copy)
    swapped = exact_right(
        jnp.concatenate([gf_ref[2 * (PAIRS - 1 - i) + 1] for i in range(PAIRS)], axis=0), flip
    )
    small[...] = jnp.zeros_like(small)
    for i in range(PAIRS):
        block = gf_ref[2 * i] + swapped[8 * i : 8 * i + 8]
        small[KERNEL * i : KERNEL * i + KERNEL] = block[:KERNEL]
    block = gf_ref[UNITS] + gf_ref[UNITS + 1]
    small[KERNEL * PAIRS : KERNEL * PAIRS + KERNEL] = block[:KERNEL]
    small[KERNEL * PAIRS + KERNEL : KERNEL * PAIRS + KERNEL + 2] = heads[:2]
    first = []
    for k in range(1, shards):
        peer = lax.rem(zero + k, shards)
        copy = push(small, small_in.at[zero], ms.at[0, k], mr.at[0, k], "zero", peer)
        copy.start()
        first.append(copy)
    small_in[zero] = small[...]
    pairs[-1].wait()
    kept = parts[zero].astype(F32) + pair_in[chip].astype(F32)
    for b in range(PAIRS):
        w_rev[b * 128 : (b + 1) * 128] = mm(
            flip, w_out[(PAIRS - 1 - b) * 128 : (PAIRS - b) * 128]
        ).astype(BF16)

    @pl.when(seq > 0)
    def _():
        g_up.wait_recv()

    @pl.when(seq < count - 1)
    def _():
        g_down.wait_recv()

    def settled(s, at):
        top = gi_ref[s, EDGE : 2 * EDGE, at] + g_before[s, :, at]
        low = gi_ref[s, SPAN : SPAN + EDGE, at] + g_after[s, :, at]
        return jnp.concatenate([top, gi_ref[s, 2 * EDGE : SPAN, at], low], axis=0).astype(BF16)

    gps = [
        jnp.concatenate([settled(s, slice(WIDTH, CHANNELS)), ddt[s]], axis=1) for s in range(2)
    ]

    def hidden_part(i):
        at = slice(i * 128, i * 128 + 128)
        a = (settled(0, at).astype(F32) + mm_nt(gps[0], w_out[at])).astype(BF16)
        b = (settled(1, at).astype(F32) + mm_nt(gps[1], w_rev[at])).astype(BF16)
        gh_ref[:, at] = (a.astype(F32) + b.astype(F32)).astype(BF16)

    for i in range(PAIRS // 2):
        hidden_part(i)
    for copy in scatter:
        copy.wait()
    for k in range(1, chips):
        kept = kept + part_in[k].astype(F32)
    spare = mine.shape[0] - packed
    mine[:packed] = kept.astype(BF16)
    if spare:
        mine[packed:] = jnp.zeros((spare, 128), BF16)
    chunk = mine.shape[0] // count
    third = []
    for k in range(1, count):
        peer = lax.rem(seq + k, count)
        src = mine.at[pl.ds(pl.multiple_of(peer * chunk, 16), chunk)]
        copy = push(src, chunk_in.at[k], ss.at[0, k], sr.at[0, k], "seq", peer)
        copy.start()
        third.append(copy)
    for copy in first:
        copy.wait()
    summed = small_in[0]
    for z in range(1, shards):
        summed = summed + small_in[z]
    small2[...] = summed
    second = []
    for k in range(1, count):
        peer = lax.rem(seq + k, count)
        copy = push(small2, small2_in.at[seq], ms.at[1, shards + k], mr.at[1, shards + k], "seq", peer)
        copy.start()
        second.append(copy)
    small2_in[seq] = small2[...]
    for i in range(PAIRS // 2, PAIRS):
        hidden_part(i)
    for copy in third:
        copy.wait()
    here = pl.ds(pl.multiple_of(seq * chunk, 16), chunk)
    summed = mine[here].astype(F32)
    for k in range(1, count):
        summed = summed + chunk_in[k].astype(F32)
    gathered[here] = summed.astype(BF16)
    third = []
    for k in range(1, count):
        peer = lax.rem(seq + k, count)
        copy = push(gathered.at[here], gathered.at[here], ss.at[1, k], sr.at[1, k], "seq", peer)
        copy.start()
        third.append(copy)
    for copy in second:
        copy.wait()
    summed = small2_in[0]
    for z in range(1, count):
        summed = summed + small2_in[z]
    total2[...] = summed
    for d, place, peer in chains:

        @pl.when(place < count - 1)
        def _():
            def sent(i, carry):
                copy_of(d, i, peer).wait_send()
                return carry

            lax.fori_loop(0, PAIRS, sent, 0)

    @pl.when(seq < count - 1)
    def _():
        up.wait_send()

    @pl.when(seq > 0)
    def _():
        down.wait_send()

    @pl.when(seq < count - 1)
    def _():
        g_up.wait_send()

    @pl.when(seq > 0)
    def _():
        g_down.wait_send()

    for copy in third:
        copy.wait()
    full[...] = gathered[...]


def emit_kernel(
    shards, fold, out_ref, gh_ref, full, total, out_hbm, gh_hbm, gw_ref, gc_ref, gd_ref,
    wide, taps, sems,
):
    copies = [
        pltpu.make_async_copy(out_ref, out_hbm, sems.at[0]),
        pltpu.make_async_copy(gh_ref, gh_hbm, sems.at[1]),
    ]
    for copy in copies:
        copy.start()
    rows = WIDTH // shards
    fold_rows = rows // fold
    tail = full[rows : rows + fold_rows].astype(F32)
    wide[...] = jnp.zeros_like(wide)
    wide[:rows, :128] = full[:rows].astype(F32)
    for q in range(fold):
        moved = pltpu.roll(tail, 128 - 32 * q, 1) if q else tail
        wide[q * fold_rows : (q + 1) * fold_rows, 128:] = moved
    gw_ref[...] = wide[...].T[: gw_ref.shape[0], :rows]
    gd_ref[...] = total[KERNEL * PAIRS + KERNEL : KERNEL * PAIRS + KERNEL + 2, :HEADS]
    for i in range(PAIRS + 1):
        taps[:, i * 128 : i * 128 + 128] = total[KERNEL * i : KERNEL * i + KERNEL]
    zero = lax.axis_index("zero")
    width = gc_ref.shape[1]
    for z in range(shards):

        @pl.when(zero == z)
        def _():
            gc_ref[...] = taps[:, z * width : (z + 1) * width]

    for copy in copies:
        copy.wait()


def spec(space):
    return pl.BlockSpec(memory_space=space)


SQ4 = (4, 128, 128)
SQ2 = (2, 128, 128)
TILES = (UNITS, 2, 128, 128)


def per_device(hidden, grad_out, w_proj, conv_w, a_log, dt_bias):
    assert hidden.shape[:2] == (1, SPAN)
    count, shards = lax.axis_size("seq"), lax.axis_size("zero")
    chips = shards // 2
    rows, columns = w_proj.shape
    part = CHANNELS // shards
    fold = 4 if rows % 64 == 0 else 1
    packed = rows + rows // fold
    step = 16 * count
    padded = -(-packed // step) * step
    lines = 48
    wide_rows = -(-rows // 128) * 128
    pieces = (2, PAIRS, 2, 2, STATE, 128)
    edges = (2, EDGE, CHANNELS)
    scratch = [
        ((SPAN, WIDTH), BF16), ((SPAN, WIDTH), BF16), ((columns, rows), BF16),
        ((KERNEL, part), BF16), ((256, wide_rows), F32),
        ((EXT, WIDTH), BF16), ((EXT, WIDTH), BF16), ((2, WIDTH, EXT), BF16),
        ((2, 8, CHANNELS), F32), ((WIDTH, 256), BF16), ((WIDTH, 256), BF16), ((WIDTH, 256), BF16),
        ((shards, packed, 128), BF16), ((8, part), F32), ((shards, 8, part), F32),
        ((2 * EDGE, WIDTH), BF16), ((2 * EDGE, WIDTH), BF16),
        (TILES, BF16), (TILES, F32), (TILES, BF16), (TILES, BF16), (TILES, BF16),
        (TILES, F32), (TILES, F32), (TILES, F32), (TILES, F32), ((UNITS, 128, 128), F32),
        (pieces, F32), (pieces, BF16), (pieces, BF16),
        ((8, 128), F32), ((8, 128), F32), ((128, 128), F32), ((5 * 128, 128), BF16), ((256, 256), BF16),
        (SQ2, F32), (SQ2, F32), (SQ4, F32), ((4, 2, 128, STATE), BF16), (SQ4, BF16),
        (SQ4, F32), (SQ2, BF16), (SQ2, F32), (SQ4, F32), ((4, 2, 128, STATE), F32),
        ((3 * SPAN + 8, 128), F32),
        ((2, EXT, CHANNELS), F32), ((UNITS + 2, 8, 128), F32), ((2, EXT, 128), F32),
        (edges, F32), (edges, F32),
        ((shards, packed, 128), BF16), ((chips, packed, 128), BF16),
        ((chips, packed, 128), BF16), ((chips, packed, 128), BF16),
        ((padded, 128), BF16), ((count, padded // count, 128), BF16), ((padded, 128), BF16),
        ((lines, 128), F32), ((shards, lines, 128), F32),
        ((lines, 128), F32), ((count, lines, 128), F32),
    ]
    sems = [
        (4,), (4,), (chips,), (chips,), (chips,), (chips,), (shards,), (shards,),
        (2, PAIRS), (2, PAIRS), (4,), (chips,), (chips,), (1, chips), (1, chips),
        (2, count), (2, count), (2, shards + count), (2, shards + count),
    ]
    anywhere = spec(pl.ANY)
    outs = pl.pallas_call(
        functools.partial(whole_kernel, shards, count, fold),
        out_shape=[
            jax.ShapeDtypeStruct((SPAN, WIDTH), BF16), jax.ShapeDtypeStruct((SPAN, WIDTH), BF16),
            jax.ShapeDtypeStruct((padded, 128), BF16), jax.ShapeDtypeStruct((lines, 128), F32),
        ],
        in_specs=[spec(pltpu.HBM)] * 4 + [spec(pltpu.VMEM)] * 2,
        scratch_shapes=[pltpu.VMEM(s, t) for s, t in scratch]
        + [pltpu.SemaphoreType.DMA(s) for s in sems],
        compiler_params=pltpu.CompilerParams(
            vmem_limit_bytes=54300 * 1024, collective_id=0, has_side_effects=True
        ),
    )(hidden[0], grad_out[0], w_proj.T, conv_w, a_log[None], dt_bias[None])
    output, grad_hidden, share_w, share_c, grad_heads = pl.pallas_call(
        functools.partial(emit_kernel, shards, fold),
        out_shape=[
            jax.ShapeDtypeStruct((SPAN, WIDTH), BF16), jax.ShapeDtypeStruct((SPAN, WIDTH), BF16),
            jax.ShapeDtypeStruct((columns, rows), F32),
            jax.ShapeDtypeStruct((KERNEL, part), F32), jax.ShapeDtypeStruct((2, HEADS), F32),
        ],
        out_specs=[anywhere] * 2 + [spec(pltpu.VMEM)] * 3,
        scratch_shapes=[
            pltpu.VMEM((wide_rows, 256), F32), pltpu.VMEM((KERNEL, CHANNELS), F32),
            pltpu.SemaphoreType.DMA((2,)),
        ],
        compiler_params=pltpu.CompilerParams(vmem_limit_bytes=8 * 1024 * 1024),
    )(*outs)
    return (output[None], grad_hidden[None], share_w.T, share_c, grad_heads)


def solution(mesh):
    return jax.shard_map(
        per_device,
        mesh=mesh,
        in_specs=(
            P(("grp", "zero"), "seq", None),
            P(("grp", "zero"), "seq", None),
            P("zero", None),
            P(None, "zero"),
            P(),
            P(),
        ),
        out_specs=(
            P(("grp", "zero"), "seq", None),
            P(("grp", "zero"), "seq", None),
            P(("grp", "zero"), None),
            P("grp", "zero"),
            P("grp", None),
        ),
        check_vma=False,
    )
```

```python
import functools
import jax
import jax.numpy as jnp
from jax import lax
from jax.experimental import pallas as pl
from jax.experimental.pallas import tpu as pltpu
from jax.sharding import PartitionSpec as P

WIDTH = 1280
STATE = 64
HEAD_DIM = 64
SPAN = 128
KERNEL = 4
HEADS = 20
PAIRS = WIDTH // 128
CHANNELS = WIDTH + 2 * STATE
EDGE = 8
EXT = SPAN + 2 * EDGE
F32 = jnp.float32
BF16 = jnp.bfloat16
UNITS = 2 * PAIRS
LAG = 5
GROUP = 2
EARLY = 4


def mm(a, b):
    return jnp.dot(a, b, preferred_element_type=F32)


def mm_nt(a, b):
    return lax.dot_general(a, b, (((1,), (1,)), ((), ())), preferred_element_type=F32)


def mm_tn(a, b):
    return lax.dot_general(a, b, (((0,), (0,)), ((), ())), preferred_element_type=F32)


def exact(a, b):
    return jnp.dot(a, b, preferred_element_type=F32, precision=lax.Precision.HIGHEST)


def iota(dim, shape=(128, 128)):
    return lax.broadcasted_iota(jnp.int32, shape, dim)


def mirror(dtype=BF16):
    return jnp.where(iota(0) + iota(1) == 127, 1.0, 0.0).astype(dtype)


def softplus(x):
    return jnp.maximum(x, 0.0) + jnp.log1p(jnp.exp(-jnp.abs(x)))


def sigmoid(x):
    return 1.0 / (1.0 + jnp.exp(-x))


def shifted(x):
    back = [x[EDGE : EDGE + SPAN]]
    fore = [back[0]]
    for k in range(1, KERNEL):
        back.append(pltpu.roll(x, k, 0)[EDGE : EDGE + SPAN])
        fore.append(pltpu.roll(x, EXT - k, 0)[EDGE : EDGE + SPAN])
    return back, fore


def conv(taps, rows):
    out = taps[0:1] * rows[0]
    for k in range(1, KERNEL):
        out = out + taps[k : k + 1] * rows[k]
    return out


def lanes(i):
    return pl.ds(pl.multiple_of(i * 128, 128), 128)


MESH = pl.DeviceIdType.MESH


def greet_all(shards, count):
    barrier = pltpu.get_barrier_semaphore()
    seq, zero = lax.axis_index("seq"), lax.axis_index("zero")
    total = 0
    for n in range(count):
        for k in range(shards):
            if (k or n) and (n == 0 or k % 2 == 0):
                there = {"zero": lax.rem(zero + k, shards), "seq": lax.rem(seq + n, count)}
                pl.semaphore_signal(barrier, inc=1, device_id=there, device_id_type=MESH)
                total += 1
    pl.semaphore_wait(barrier, total)


def push(src, dst, send, recv, axis, peer):
    return pltpu.make_async_remote_copy(
        src_ref=src,
        dst_ref=dst,
        send_sem=send,
        recv_sem=recv,
        device_id={axis: peer},
        device_id_type=MESH,
    )


def split2(x):
    hi = x.astype(BF16)
    return hi, (x - hi.astype(F32)).astype(BF16)


def split3(x):
    hi = x.astype(BF16)
    rest = x - hi.astype(F32)
    mid = rest.astype(BF16)
    return hi, mid, (rest - mid.astype(F32)).astype(BF16)


def exact_left(a, x):
    n = x.shape[1]
    out = mm(a, jnp.concatenate(split3(x), axis=1))
    return out[:, :n] + out[:, n : 2 * n] + out[:, 2 * n :]


def exact_right(x, b):
    n = x.shape[0]
    out = mm(jnp.concatenate(split3(x), axis=0), b)
    return out[:n] + out[n : 2 * n] + out[2 * n :]


def ones_where(keep):
    return jnp.where(keep, 1.0, 0.0).astype(BF16)


def strand_swap():
    k, lane = iota(0), iota(1)
    return ones_where((lane >= 32) & (lane < 32 + HEADS) & (k + lane == 31 + HEADS))


def folded(tail, fold):
    size = tail.shape[0] // fold
    out = tail[:size]
    for q in range(1, fold):
        out = out + pltpu.roll(tail[q * size : (q + 1) * size], 32 * q, 1)
    return out


def whole_kernel(
    shards, count, fold,
    hid_hbm, go_hbm, wt_hbm, c_hbm, alog_ref, bias_ref,
    out_ref, gh_ref, full, total2,
    hid_ref, go_ref, wt_in, c_in, wt_pad,
    x_ref, xf_ref, xt_ref, taps_ref, wp_ref, w_out, w_rev, w_slots, c_own, c_slots, before, after,
    vals, slope, u_ref, fu_ref, eg_ref, yoff, duo, e_b, f_b, dt_b,
    own, in_slots, out_slots,
    heads_in, rates, dtx_ref, stack, split, within_t, score, diag, bc_act, bc_t, bc_slope, masks,
    d_score, d_diag, d_bc, acc,
    gi_ref, gf_ref, bcx_ref, g_before, g_after, parts, pair_in, pair_sum, part_in, gathered,
    small, small_in, small2, small2_in,
    local, sides, w_send, w_recv, f_send, f_recv, t_send, t_recv, c_send, c_recv,
    g_sides, p_send, p_recv, zs, zr, ss, sr, ms, mr,
):
    seq, zero = lax.axis_index("seq"), lax.axis_index("zero")
    core = lax.rem(zero, 2)
    chip = lax.div(zero, 2)
    chips = shards // 2
    sibling = zero + 1 - 2 * core
    rows = WIDTH // shards
    fold_rows = rows // fold
    packed = rows + fold_rows
    loads = [
        pltpu.make_async_copy(src, dst, local.at[n])
        for n, (src, dst) in enumerate(
            ((c_hbm, c_in), (wt_hbm, wt_in), (hid_hbm, hid_ref), (go_hbm, go_ref))
        )
    ]
    for load in loads:
        load.start()
    c_own[...] = jnp.zeros_like(c_own)
    wt_pad[...] = jnp.zeros_like(wt_pad)
    loads[0].wait()
    c_own[:KERNEL] = c_in[...].astype(F32)
    loads[1].wait()
    wt_pad[: wt_in.shape[0], :rows] = wt_in[...].astype(F32)
    w_own = wt_pad[...].T
    w_slots[zero, :rows] = w_own[:rows, :128].astype(BF16)
    w_slots[zero, rows:] = folded(w_own[:rows, 128:], fold).astype(BF16)
    greet_all(shards, count)
    tap_copies = []
    for k in range(1, shards):
        peer = lax.rem(zero + k, shards)
        copy = push(c_own, c_slots.at[zero], t_send.at[k], t_recv.at[k], "zero", peer)
        copy.start()
        tap_copies.append(copy)
    loads[2].wait()
    up = push(
        hid_ref.at[pl.ds(SPAN - 2 * EDGE, 2 * EDGE)], before, sides.at[0], sides.at[1], "seq",
        lax.rem(seq + 1, count),
    )
    down = push(
        hid_ref.at[pl.ds(0, 2 * EDGE)], after, sides.at[2], sides.at[3], "seq",
        lax.rem(seq + count - 1, count),
    )

    @pl.when(seq < count - 1)
    def _():
        up.start()

    @pl.when(seq > 0)
    def _():
        down.start()

    w_copies = []
    for k in range(chips):
        peer = lax.rem(zero + 2 * k, shards) if k else sibling
        copy = push(w_slots.at[zero], w_slots.at[zero], w_send.at[k], w_recv.at[k], "zero", peer)
        copy.start()
        w_copies.append(copy)
    c_slots[zero] = c_own[...]
    w_out[:, 128:] = jnp.zeros((WIDTH, 128), BF16)
    x_ref[EDGE : EDGE + SPAN] = hid_ref[...]
    flip = mirror()
    swap = strand_swap()
    masks[0] = ones_where(iota(0) > iota(1))
    masks[1] = ones_where(iota(0) < iota(1))
    if parts.shape[1] > packed:
        spare = (shards, parts.shape[1] - packed, 128)
        parts[:, packed:] = jnp.zeros(spare, BF16)
    d_score[...] = jnp.zeros_like(d_score)
    d_diag[...] = jnp.zeros_like(d_diag)
    d_bc[...] = jnp.zeros_like(d_bc)
    acc[...] = jnp.zeros_like(acc)

    @pl.when(seq == 0)
    def _():
        x_ref[:EDGE] = jnp.zeros((EDGE, WIDTH), BF16)
        in_slots[0] = jnp.zeros(in_slots.shape[1:], BF16)

    @pl.when(seq > 0)
    def _():
        up.wait_recv()
        x_ref[:EDGE] = before[EDGE:]

    @pl.when(seq == count - 1)
    def _():
        x_ref[EDGE + SPAN :] = jnp.zeros((EDGE, WIDTH), BF16)
        in_slots[1] = jnp.zeros(in_slots.shape[1:], BF16)

    @pl.when(seq < count - 1)
    def _():
        down.wait_recv()
        x_ref[EDGE + SPAN :] = after[:EDGE]

    for copy in tap_copies:
        copy.wait()
    part = c_own.shape[1]
    for z in range(shards):
        taps_ref[0, :, z * part : (z + 1) * part] = c_slots[z]
    for b in range(PAIRS):
        taps_ref[1, :, b * 128 : (b + 1) * 128] = mm(
            taps_ref[0, :, (PAIRS - 1 - b) * 128 : (PAIRS - b) * 128].astype(BF16), flip
        )

    def values_of(i):
        rows = shifted(x_ref[:, lanes(i)].astype(F32))
        for s in range(2):
            taps = taps_ref[s, :, lanes(i)]
            for d in range(2):
                mixed = conv(taps, rows[d])
                sig = sigmoid(mixed)
                act = mixed * sig
                vals[2 * i + s, d] = act.astype(BF16)
                slope[2 * i + s, d] = sig + act * (1.0 - sig)

    def values_step(i, carry):
        values_of(i)
        return carry

    for b in range(PAIRS):
        xf_ref[:, (PAIRS - 1 - b) * 128 : (PAIRS - b) * 128] = mm(
            x_ref[:, b * 128 : (b + 1) * 128], flip
        ).astype(BF16)
    lax.fori_loop(0, EARLY, values_step, 0)

    for copy in w_copies:
        copy.wait()
    forwards = []
    for k in range(1, chips):
        slot_of = w_slots.at[lax.rem(zero + shards - 2 * k, shards)]
        copy = push(slot_of, slot_of, f_send.at[k], f_recv.at[k], "zero", sibling)
        copy.start()
        forwards.append(copy)

    def unpack(z):
        at = pl.multiple_of(z * rows, 16)
        w_out[pl.ds(at, rows), :128] = w_slots[z, :rows]
        tail = w_slots[z, rows:].astype(F32)
        for q in range(fold):
            moved = pltpu.roll(tail, 128 - 32 * q, 1) if q else tail
            w_out[pl.ds(at + q * fold_rows, fold_rows), 128:] = jnp.where(
                iota(1, (fold_rows, 128)) < HEADS, moved, 0.0
            ).astype(BF16)

    for k in range(chips):
        unpack(lax.rem(zero + shards - 2 * k, shards))
    unpack(sibling)
    for copy in forwards:
        copy.wait()
    for k in range(1, chips):
        unpack(lax.rem(sibling + shards - 2 * k, shards))
    wp_ref[:, :128] = w_out[:, :128]
    wp_ref[:, 128:] = mm(w_out[:, 128:], swap).astype(BF16)
    proj = (mm(x_ref[...], w_out[...]), mm(xf_ref[...], wp_ref[...]))
    loads[3].wait()
    heads_in[...] = jnp.zeros_like(heads_in)
    heads_in[0:1, :HEADS] = alog_ref[...]
    heads_in[1:2, :HEADS] = bias_ref[...]
    place = heads_in[...] + exact_right(heads_in[...], swap)
    rate = jnp.exp(place[0:1])
    rates[0:1] = rate
    dtx = (proj[0] + proj[1])[EDGE : EDGE + SPAN, 128:] + place[1:2]
    dtx_ref[...] = dtx
    delta = softplus(dtx)
    both = jnp.concatenate(
        [ones_where(iota(0) >= iota(1)), ones_where(iota(0) <= iota(1))], axis=0
    )
    within = exact_left(both, -rate * delta)
    ends = jnp.concatenate(
        [
            jnp.broadcast_to(within[SPAN - 1 : SPAN], (SPAN, 128)),
            jnp.broadcast_to(within[SPAN : SPAN + 1], (SPAN, 128)),
        ],
        axis=0,
    )
    spread = jnp.concatenate([jnp.exp(within), jnp.exp(ends - within), delta], axis=0)
    hi, lo = split2(spread)
    wide_low = iota(1, spread.shape) < 64
    stack[...] = jnp.where(
        wide_low, hi.astype(F32), pltpu.roll(lo.astype(F32), 64, 1)
    ).astype(BF16)
    hi, mid, lo = split3(within)
    low_two = iota(1, (256, 128)) < 64
    split[:, :128] = jnp.where(
        low_two, hi.astype(F32), pltpu.roll(mid.astype(F32), 64, 1)
    ).astype(BF16)
    split[:, 128:] = jnp.where(low_two, lo.astype(F32), 0.0).astype(BF16)
    for d in range(2):
        within_t[d] = within[d * 128 : d * 128 + 128].T
    for s in range(2):
        bcx_ref[s] = proj[s][:, :128].astype(BF16).astype(F32)
        bcx = shifted(bcx_ref[s])
        scores = []
        for d in range(2):
            c = 2 * s + d
            mixed = conv(taps_ref[0, :, WIDTH:], bcx[d])
            sig = sigmoid(mixed)
            wide = mixed * sig
            act = wide.astype(BF16)
            bc_slope[c] = sig + wide * (1.0 - sig)
            bc_act[c, 0] = act[:, :STATE]
            bc_act[c, 1] = act[:, STATE:]
            act_t = act.astype(F32).T.astype(BF16)
            bc_t[c] = act_t
            scores.append(mm(act[:, STATE:], act_t[:STATE]))
            own_diag = jnp.sum(jnp.where(iota(0) == iota(1), scores[d], 0.0), axis=1, keepdims=True)
            diag[c] = jnp.broadcast_to(own_diag, (128, 128))
        score[s] = jnp.where(
            iota(0) > iota(1), scores[0], jnp.where(iota(0) < iota(1), scores[1], 0.0)
        )

    def produce(t):
        shape = (128, 256 * GROUP)
        line, lane = iota(0, shape), iota(1, shape)
        head = (
            2 * (GROUP * t + lax.div(lane, 256))
            + jnp.where(lax.rem(lane, 256) >= 128, 32, 0)
            + jnp.where(lax.rem(lane, 128) >= HEAD_DIM, 1, 0)
        )
        all_wide = mm(stack[...], ones_where(lax.rem(line, 64) == head))
        for n in range(GROUP):
            g = go_ref[:, lanes(GROUP * t + n)].astype(F32)
            for s in range(2):
                u = 2 * GROUP * t + 2 * n + s
                at = 256 * n + 128 * s
                wide = all_wide[:, at : at + 128]
                dt = wide[512:]
                dt_b[u] = dt
                for d in range(2):
                    e, f = wide[128 * d : 128 * d + 128], wide[256 + 128 * d : 384 + 128 * d]
                    e_b[u, d] = e
                    f_b[u, d] = f
                    step = (vals[u, d].astype(F32) * dt).astype(BF16)
                    u_ref[u, d] = step
                    fu = (step.astype(F32) * f).astype(BF16)
                    fu_ref[u, d] = fu
                    eg = (e * g).astype(BF16)
                    eg_ref[u, d] = eg
                    own[d, u, 0] = mm(bc_t[2 * s + d, :STATE], fu)
                    own[1 - d, u, 1] = mm(bc_t[2 * s + d, STATE:], eg)

    def decay_of(u, d):
        at = SPAN - 1 if d == 0 else 0
        return e_b[u, d, at : at + 1]

    chains = ((0, seq, seq + 1), (1, count - 1 - seq, seq - 1))

    def copy_of(d, u, peer):
        return push(
            out_slots.at[d, u], in_slots.at[d, u], c_send.at[d, u], c_recv.at[d, u], "seq", peer
        )

    def send_first(t):
        for d, place, peer in chains:

            @pl.when(place == 0)
            def _():
                for n in range(2 * GROUP):
                    u = 2 * GROUP * t + n
                    out_slots[d, u] = own[d, u].astype(BF16)
                    copy_of(d, u, peer).start()

    def forward(n):
        for d, place, peer in chains:
            u = n - LAG * place

            @pl.when((place > 0) & (place < count - 1) & (u >= 0) & (u < UNITS))
            def _():
                copy_of(d, u, seq).wait_recv()
                for q in range(2):
                    dec = decay_of(u, d if q == 0 else 1 - d)
                    out_slots[d, u, q] = (
                        own[d, u, q] + dec * in_slots[d, u, q].astype(F32)
                    ).astype(BF16)
                copy_of(d, u, peer).start()

    def arrive(i):
        for d, place, peer in chains:

            @pl.when(place == count - 1)
            def _():
                for s in range(2):
                    copy_of(d, 2 * i + s, seq).wait_recv()

    def inside(i):
        lower = iota(0) >= iota(1)
        low = iota(1) < HEAD_DIM
        go = go_ref[:, lanes(i)]
        g = go.astype(F32)
        none = jnp.zeros((128, 128), BF16)
        g_two = jnp.concatenate([jnp.where(low, go, none), jnp.where(low, none, go)], axis=0)
        square = (256, 256)
        line = iota(0, square)
        kept_ins = []
        for s in range(2):
            u = 2 * i + s
            head = 32 * s + 2 * i
            pick = ones_where(
                (lax.rem(line, 64) == head + jnp.where(iota(1, square) >= 128, 1, 0)) & (line < 192)
            )
            cols = mm(split[...], pick)
            steps = jnp.concatenate([u_ref[u, 0], u_ref[u, 1]], axis=0)
            dw = mm_nt(g_two, steps)
            sc = score[s]
            ds = jnp.zeros((128, 128), F32)
            below, above = [], []
            for r in range(2):
                at = slice(128 * r, 128 * r + 128)
                gap = jnp.where(
                    lower,
                    cols[:128, at] - within_t[0, pl.ds(head + r, 1), :],
                    cols[128:, at] - within_t[1, pl.ds(head + r, 1), :],
                )
                decay = jnp.exp(gap)
                w = (sc * decay).astype(BF16)
                below.append(w * masks[0])
                above.append(w * masks[1])
                ds = ds + decay * jnp.where(lower, dw[at, :128], dw[at, 128:])
            for d, ws in enumerate((below, above)):
                step = steps[128 * d : 128 * d + 128]
                y_two = mm(jnp.concatenate(ws, axis=0), step)
                kept_ins.append(
                    (
                        jnp.where(low, y_two[:128], y_two[128:]),
                        jnp.where(low, mm_tn(ws[0], go), mm_tn(ws[1], go)),
                        g * step.astype(F32),
                    )
                )
            kept_ins.append(ds)
        for s in range(2):
            for d in range(2):
                y_two, du, on_diag = kept_ins[3 * s + d]
                yoff[2 * i + s, d] = y_two
                duo[2 * i + s, d] = du
                d_diag[2 * s + d] += on_diag
            d_score[s] += kept_ins[3 * s + 2]

    def back(taps, dm, x, direction):
        zero_rows = jnp.zeros((EDGE, 128), F32)
        wide = jnp.concatenate([zero_rows, dm, zero_rows], axis=0)
        out = taps[0:1] * wide
        sums = [jnp.sum(wide * x, axis=0, keepdims=True)]
        for k in range(1, KERNEL):
            moved = pltpu.roll(wide, EXT - k if direction == 0 else k, 0)
            out = out + taps[k : k + 1] * moved
            sums.append(jnp.sum(moved * x, axis=0, keepdims=True))
        return out, jnp.concatenate(sums + [jnp.zeros((8 - KERNEL, 128), F32)], axis=0)

    def finish(i):
        g = go_ref[:, lanes(i)].astype(F32)
        x = x_ref[:, lanes(i)].astype(F32)
        tall = (512, 128)
        hold = lax.rem(iota(0, tall), 128)
        sel_t = ones_where(
            iota(1, tall)
            == 2 * i + jnp.where(iota(0, tall) >= 256, 32, 0) + jnp.where(hold >= HEAD_DIM, 1, 0)
        )
        ys, parts_of, adds = [], [], []
        for s in range(2):
            u = 2 * i + s
            taps = taps_ref[s, :, lanes(i)]
            dt = dt_b[u]
            y = jnp.zeros((128, 128), F32)
            gi = jnp.zeros((EXT, 128), F32)
            gf = jnp.zeros((8, 128), F32)
            qt = jnp.zeros((128, 128), F32)
            qs, ends = [], []
            for d in range(2):
                c = 2 * s + d
                s_in, g_in = in_slots[d, u, 0], in_slots[1 - d, u, 1]
                step = u_ref[u, d].astype(F32)
                across = mm(bc_act[c, 1], s_in) * e_b[u, d] + yoff[u, d]
                y = y + across + diag[c] * step
                du = duo[u, d] + f_b[u, d] * mm(bc_act[c, 0], g_in)
                qs.append(g * across - step * du)
                du = du + diag[c] * g
                qt = qt + vals[u, d].astype(F32) * du
                adds.append((c, mm_nt(fu_ref[u, d], g_in), mm_nt(eg_ref[u, d], s_in)))
                leaving = own[d, u, 0] + decay_of(u, d) * s_in.astype(F32)
                ends.append(jnp.sum(leaving * g_in.astype(F32), axis=0, keepdims=True))
                dm = (dt * du).astype(BF16).astype(F32) * slope[u, d]
                more, sums = back(taps, dm, x, d)
                gi = gi + more
                gf = gf + sums
            q = jnp.concatenate(qs + [qt] + ends + [jnp.zeros((6, 128), F32)], axis=0)
            parts_of.extend(split2(q))
            ys.append(y.astype(BF16).astype(F32))
            adds.append((s, gi, gf))
        totals = mm(jnp.concatenate(parts_of, axis=1), sel_t)
        for s in range(2):
            for c, db, dc in adds[3 * s : 3 * s + 2]:
                d_bc[c, 0] += db
                d_bc[c, 1] += dc
            _, gi, gf = adds[3 * s + 2]
            gi_ref[s, :, lanes(i)] = gi
            gf_ref[2 * i + s] = gf
        acc[...] += totals
        out_ref[:, lanes(i)] = (ys[0] + ys[1]).astype(BF16)

    groups = PAIRS // GROUP

    def first_part(t, carry):
        produce(t)
        send_first(t)
        forward(t)
        return carry

    def second_part(i, carry):
        xt_ref[0, lanes(i)] = x_ref[:, lanes(i)].astype(F32).T.astype(BF16)
        xt_ref[1, lanes(i)] = xf_ref[:, lanes(i)].astype(F32).T.astype(BF16)
        w_rev[lanes(i)] = mm(flip, w_out[lanes(PAIRS - 1 - i)]).astype(BF16)
        inside(i)
        forward(groups + i)
        return carry

    def idle(n, carry):
        forward(n)
        return carry

    began = max(groups + PAIRS, 2 + LAG * (count - 2))

    def third_part(i, carry):
        forward(began + 2 * i)
        forward(began + 2 * i + 1)
        arrive(i)
        finish(i)
        return carry

    def late_part(t, carry):
        for n in range(GROUP):
            values_of(GROUP * t + n)
        return first_part(t, carry)

    lax.fori_loop(0, EARLY // GROUP, first_part, 0)
    lax.fori_loop(EARLY // GROUP, groups, late_part, 0)
    lax.fori_loop(0, PAIRS, second_part, 0)
    if began > groups + PAIRS:
        lax.fori_loop(groups + PAIRS, began, idle, 0)
    lax.fori_loop(0, PAIRS, third_part, 0)

    end_rows = acc[3 * SPAN : 3 * SPAN + 8]
    dl0 = acc[:SPAN] + jnp.where(iota(0) == SPAN - 1, end_rows[0:1], 0.0)
    dl1 = acc[SPAN : 2 * SPAN] + jnp.where(iota(0) == 0, end_rows[1:2], 0.0)
    both_t = jnp.concatenate(
        [ones_where(iota(0) <= iota(1)), ones_where(iota(0) >= iota(1))], axis=1
    )
    d_log = exact_left(both_t, jnp.concatenate([dl0, dl1], axis=0))
    rate = rates[0:1]
    dtx = dtx_ref[...]
    d_raw = (acc[2 * SPAN : 3 * SPAN] - rate * d_log) * sigmoid(dtx)
    sums = jnp.concatenate(
        [
            jnp.sum(d_log * (-rate * softplus(dtx)), axis=0, keepdims=True),
            jnp.sum(d_raw, axis=0, keepdims=True),
            jnp.zeros((6, 128), F32),
        ],
        axis=0,
    )
    unswap = swap.astype(F32).T.astype(BF16)
    heads = jnp.where(iota(1, (8, 128)) < HEADS, sums, 0.0) + exact_right(sums, unswap)
    ddt = (
        jnp.where(iota(1) < HEADS, d_raw, 0.0).astype(BF16),
        mm(d_raw.astype(BF16), unswap).astype(BF16),
    )
    wides = []
    for s in range(2):
        taps = taps_ref[0, :, WIDTH:]
        gi = jnp.zeros((EXT, 128), F32)
        gf = jnp.zeros((8, 128), F32)
        for d in range(2):
            c = 2 * s + d
            on_diag = jnp.sum(d_diag[c], axis=1, keepdims=True)
            off = iota(0) > iota(1) if d == 0 else iota(0) < iota(1)
            ds = jnp.where(
                off, d_score[s], jnp.where(iota(0) == iota(1), on_diag, 0.0)
            ).astype(BF16)
            db = d_bc[c, 0] + mm_tn(ds, bc_act[c, 1])
            dc = d_bc[c, 1] + mm(ds, bc_act[c, 0])
            dm = jnp.concatenate([db, dc], axis=1).astype(BF16).astype(F32) * bc_slope[c]
            more, some = back(taps, dm, bcx_ref[s], d)
            gi = gi + more
            gf = gf + some
        gi_ref[s, :, WIDTH:] = gi
        gf_ref[UNITS + s] = gf
        edge = jnp.zeros((EDGE, 128), F32)
        wides.append(
            jnp.concatenate(
                [gi, jnp.concatenate([edge, ddt[s].astype(F32), edge], axis=0)], axis=1
            ).astype(BF16)
        )
    g_up = push(
        gi_ref.at[:, pl.ds(EDGE + SPAN, EDGE)], g_before, g_sides.at[0], g_sides.at[1], "seq",
        lax.rem(seq + 1, count),
    )
    g_down = push(
        gi_ref.at[:, pl.ds(0, EDGE)], g_after, g_sides.at[2], g_sides.at[3], "seq",
        lax.rem(seq + count - 1, count),
    )

    def weight_part(z):
        at = pl.ds(pl.multiple_of(z * rows, 16), rows)
        total = mm(xt_ref[0, at], wides[0]) + mm(xt_ref[1, at], wides[1])
        parts[z, :rows] = total[:, :128].astype(BF16)
        parts[z, rows:packed] = folded(total[:, 128:], fold).astype(BF16)

    pairs = []
    for k in list(range(1, chips)) + [0]:
        z = 2 * lax.rem(chip + k, chips) + 1 - core
        weight_part(z)
        copy = push(
            parts.at[z], pair_in.at[lax.div(z, 2)], p_send.at[k], p_recv.at[k], "zero", sibling
        )
        copy.start()
        pairs.append(copy)
    for k in list(range(1, chips)) + [0]:
        weight_part(2 * lax.rem(chip + k, chips) + core)

    @pl.when(seq < count - 1)
    def _():
        g_up.start()

    @pl.when(seq > 0)
    def _():
        g_down.start()

    @pl.when(seq == 0)
    def _():
        g_before[...] = jnp.zeros_like(g_before)

    @pl.when(seq == count - 1)
    def _():
        g_after[...] = jnp.zeros_like(g_after)

    chunk = gathered.shape[0] // count
    here = pl.ds(pl.multiple_of(seq * chunk, 16), chunk)
    scatter = []
    for k in list(range(1, chips)) + [0]:
        there = lax.rem(chip + k, chips)
        pairs[k - 1].wait()
        pair_sum[there] = (
            parts[2 * there + core].astype(F32) + pair_in[there].astype(F32)
        ).astype(BF16)
        for n in range(count):
            if k or n:
                peer = lax.rem(seq + n, count)
                copy = pltpu.make_async_remote_copy(
                    src_ref=pair_sum.at[there, pl.ds(pl.multiple_of(peer * chunk, 16), chunk)],
                    dst_ref=part_in.at[k, n],
                    send_sem=zs.at[k, n],
                    recv_sem=zr.at[k, n],
                    device_id={"zero": 2 * there + core, "seq": peer},
                    device_id_type=MESH,
                )
                copy.start()
                scatter.append(copy)
    swapped = exact_right(
        jnp.concatenate([gf_ref[2 * (PAIRS - 1 - i) + 1] for i in range(PAIRS)], axis=0), flip
    )
    small[...] = jnp.zeros_like(small)
    for i in range(PAIRS):
        block = gf_ref[2 * i] + swapped[8 * i : 8 * i + 8]
        small[KERNEL * i : KERNEL * i + KERNEL] = block[:KERNEL]
    block = gf_ref[UNITS] + gf_ref[UNITS + 1]
    small[KERNEL * PAIRS : KERNEL * PAIRS + KERNEL] = block[:KERNEL]
    small[KERNEL * PAIRS + KERNEL : KERNEL * PAIRS + KERNEL + 2] = heads[:2]
    first = []
    for k in range(1, shards):
        peer = lax.rem(zero + k, shards)
        copy = push(small, small_in.at[zero], ms.at[0, k], mr.at[0, k], "zero", peer)
        copy.start()
        first.append(copy)
    small_in[zero] = small[...]

    @pl.when(seq > 0)
    def _():
        g_up.wait_recv()

    @pl.when(seq < count - 1)
    def _():
        g_down.wait_recv()

    def settled(s, at):
        top = gi_ref[s, EDGE : 2 * EDGE, at] + g_before[s, :, at]
        low = gi_ref[s, SPAN : SPAN + EDGE, at] + g_after[s, :, at]
        return jnp.concatenate([top, gi_ref[s, 2 * EDGE : SPAN, at], low], axis=0).astype(BF16)

    gps = [
        jnp.concatenate([settled(s, slice(WIDTH, CHANNELS)), ddt[s]], axis=1) for s in range(2)
    ]

    def hidden_part(i):
        at = slice(i * 128, i * 128 + 128)
        a = (settled(0, at).astype(F32) + mm_nt(gps[0], w_out[at])).astype(BF16)
        b = (settled(1, at).astype(F32) + mm_nt(gps[1], w_rev[at])).astype(BF16)
        gh_ref[:, at] = (a.astype(F32) + b.astype(F32)).astype(BF16)

    for copy in first:
        copy.wait()
    summed = small_in[0]
    for z in range(1, shards):
        summed = summed + small_in[z]
    small2[...] = summed
    second = []
    for k in range(1, count):
        peer = lax.rem(seq + k, count)
        copy = push(small2, small2_in.at[seq], ms.at[1, shards + k], mr.at[1, shards + k], "seq", peer)
        copy.start()
        second.append(copy)
    small2_in[seq] = small2[...]
    for i in range(PAIRS // 2):
        hidden_part(i)
    for copy in scatter:
        copy.wait()
    summed = parts[zero, here].astype(F32) + pair_in[chip, here].astype(F32)
    for k in range(chips):
        for n in range(count):
            if k or n:
                summed = summed + part_in[k, n].astype(F32)
    gathered[here] = summed.astype(BF16)
    third = []
    for k in range(1, count):
        peer = lax.rem(seq + k, count)
        copy = push(gathered.at[here], gathered.at[here], ss.at[1, k], sr.at[1, k], "seq", peer)
        copy.start()
        third.append(copy)
    for i in range(PAIRS // 2, PAIRS):
        hidden_part(i)
    for copy in second:
        copy.wait()
    summed = small2_in[0]
    for z in range(1, count):
        summed = summed + small2_in[z]
    total2[...] = summed
    for d, place, peer in chains:

        @pl.when(place < count - 1)
        def _():
            def sent(u, carry):
                copy_of(d, u, peer).wait_send()
                return carry

            lax.fori_loop(0, UNITS, sent, 0)

    @pl.when(seq < count - 1)
    def _():
        up.wait_send()

    @pl.when(seq > 0)
    def _():
        down.wait_send()

    @pl.when(seq < count - 1)
    def _():
        g_up.wait_send()

    @pl.when(seq > 0)
    def _():
        g_down.wait_send()

    for copy in third:
        copy.wait()
    full[...] = gathered[...]


def emit_kernel(
    shards, fold, out_ref, gh_ref, full, total, out_hbm, gh_hbm, gw_ref, gc_ref, gd_ref,
    wide, taps, sems,
):
    copies = [
        pltpu.make_async_copy(out_ref, out_hbm, sems.at[0]),
        pltpu.make_async_copy(gh_ref, gh_hbm, sems.at[1]),
    ]
    for copy in copies:
        copy.start()
    rows = WIDTH // shards
    fold_rows = rows // fold
    tail = full[rows : rows + fold_rows].astype(F32)
    wide[...] = jnp.zeros_like(wide)
    wide[:rows, :128] = full[:rows].astype(F32)
    for q in range(fold):
        moved = pltpu.roll(tail, 128 - 32 * q, 1) if q else tail
        wide[q * fold_rows : (q + 1) * fold_rows, 128:] = moved
    gw_ref[...] = wide[...].T[: gw_ref.shape[0], :rows]
    gd_ref[...] = total[KERNEL * PAIRS + KERNEL : KERNEL * PAIRS + KERNEL + 2, :HEADS]
    for i in range(PAIRS + 1):
        taps[:, i * 128 : i * 128 + 128] = total[KERNEL * i : KERNEL * i + KERNEL]
    zero = lax.axis_index("zero")
    width = gc_ref.shape[1]
    for z in range(shards):

        @pl.when(zero == z)
        def _():
            gc_ref[...] = taps[:, z * width : (z + 1) * width]

    for copy in copies:
        copy.wait()


def spec(space):
    return pl.BlockSpec(memory_space=space)


SQ4 = (4, 128, 128)
SQ2 = (2, 128, 128)
TILES = (UNITS, 2, 128, 128)


def per_device(hidden, grad_out, w_proj, conv_w, a_log, dt_bias):
    assert hidden.shape[:2] == (1, SPAN)
    count, shards = lax.axis_size("seq"), lax.axis_size("zero")
    chips = shards // 2
    rows, columns = w_proj.shape
    part = CHANNELS // shards
    fold = 4 if rows % 64 == 0 else 1
    packed = rows + rows // fold
    step = 16 * count
    padded = -(-packed // step) * step
    lines = 48
    wide_rows = -(-rows // 128) * 128
    pieces = (2, UNITS, 2, STATE, 128)
    edges = (2, EDGE, CHANNELS)
    scratch = [
        ((SPAN, WIDTH), BF16), ((SPAN, WIDTH), BF16), ((columns, rows), BF16),
        ((KERNEL, part), BF16), ((256, wide_rows), F32),
        ((EXT, WIDTH), BF16), ((EXT, WIDTH), BF16), ((2, WIDTH, EXT), BF16),
        ((2, 8, CHANNELS), F32), ((WIDTH, 256), BF16), ((WIDTH, 256), BF16), ((WIDTH, 256), BF16),
        ((shards, packed, 128), BF16), ((8, part), F32), ((shards, 8, part), F32),
        ((2 * EDGE, WIDTH), BF16), ((2 * EDGE, WIDTH), BF16),
        (TILES, BF16), (TILES, F32), (TILES, BF16), (TILES, BF16), (TILES, BF16),
        (TILES, F32), (TILES, F32), (TILES, F32), (TILES, F32), ((UNITS, 128, 128), F32),
        (pieces, F32), (pieces, BF16), (pieces, BF16),
        ((8, 128), F32), ((8, 128), F32), ((128, 128), F32), ((5 * 128, 128), BF16), ((256, 256), BF16),
        (SQ2, F32), (SQ2, F32), (SQ4, F32), ((4, 2, 128, STATE), BF16), (SQ4, BF16),
        (SQ4, F32), (SQ2, BF16), (SQ2, F32), (SQ4, F32), ((4, 2, 128, STATE), F32),
        ((3 * SPAN + 8, 128), F32),
        ((2, EXT, CHANNELS), F32), ((UNITS + 2, 8, 128), F32), ((2, EXT, 128), F32),
        (edges, F32), (edges, F32),
        ((shards, padded, 128), BF16), ((chips, padded, 128), BF16),
        ((chips, padded, 128), BF16), ((chips, count, padded // count, 128), BF16),
        ((padded, 128), BF16),
        ((lines, 128), F32), ((shards, lines, 128), F32),
        ((lines, 128), F32), ((count, lines, 128), F32),
    ]
    sems = [
        (4,), (4,), (chips,), (chips,), (chips,), (chips,), (shards,), (shards,),
        (2, UNITS), (2, UNITS), (4,), (chips,), (chips,), (chips, count), (chips, count),
        (2, count), (2, count), (2, shards + count), (2, shards + count),
    ]
    anywhere = spec(pl.ANY)
    outs = pl.pallas_call(
        functools.partial(whole_kernel, shards, count, fold),
        out_shape=[
            jax.ShapeDtypeStruct((SPAN, WIDTH), BF16), jax.ShapeDtypeStruct((SPAN, WIDTH), BF16),
            jax.ShapeDtypeStruct((padded, 128), BF16), jax.ShapeDtypeStruct((lines, 128), F32),
        ],
        in_specs=[spec(pltpu.HBM)] * 4 + [spec(pltpu.VMEM)] * 2,
        scratch_shapes=[pltpu.VMEM(s, t) for s, t in scratch]
        + [pltpu.SemaphoreType.DMA(s) for s in sems],
        compiler_params=pltpu.CompilerParams(
            vmem_limit_bytes=54300 * 1024, collective_id=0, has_side_effects=True
        ),
    )(hidden[0], grad_out[0], w_proj.T, conv_w, a_log[None], dt_bias[None])
    output, grad_hidden, share_w, share_c, grad_heads = pl.pallas_call(
        functools.partial(emit_kernel, shards, fold),
        out_shape=[
            jax.ShapeDtypeStruct((SPAN, WIDTH), BF16), jax.ShapeDtypeStruct((SPAN, WIDTH), BF16),
            jax.ShapeDtypeStruct((columns, rows), F32),
            jax.ShapeDtypeStruct((KERNEL, part), F32), jax.ShapeDtypeStruct((2, HEADS), F32),
        ],
        out_specs=[anywhere] * 2 + [spec(pltpu.VMEM)] * 3,
        scratch_shapes=[
            pltpu.VMEM((wide_rows, 256), F32), pltpu.VMEM((KERNEL, CHANNELS), F32),
            pltpu.SemaphoreType.DMA((2,)),
        ],
        compiler_params=pltpu.CompilerParams(vmem_limit_bytes=8 * 1024 * 1024),
    )(*outs)
    return (output[None], grad_hidden[None], share_w.T, share_c, grad_heads)


def solution(mesh):
    return jax.shard_map(
        per_device,
        mesh=mesh,
        in_specs=(
            P(("grp", "zero"), "seq", None),
            P(("grp", "zero"), "seq", None),
            P("zero", None),
            P(None, "zero"),
            P(),
            P(),
        ),
        out_specs=(
            P(("grp", "zero"), "seq", None),
            P(("grp", "zero"), "seq", None),
            P(("grp", "zero"), None),
            P("grp", "zero"),
            P("grp", None),
        ),
        check_vma=False,
    )
```

```python
import functools
import jax
import jax.numpy as jnp
from jax import lax
from jax.experimental import pallas as pl
from jax.experimental.pallas import tpu as pltpu
from jax.sharding import PartitionSpec as P

WIDTH = 1280
STATE = 64
HEAD_DIM = 64
SPAN = 128
KERNEL = 4
HEADS = 20
PAIRS = WIDTH // 128
CHANNELS = WIDTH + 2 * STATE
EDGE = 8
EXT = SPAN + 2 * EDGE
F32 = jnp.float32
BF16 = jnp.bfloat16
UNITS = 2 * PAIRS
HOP = 6
OFFSET = 3
GROUP = 2
EARLY = 4


def mm(a, b):
    return jnp.dot(a, b, preferred_element_type=F32)


def mm_nt(a, b):
    return lax.dot_general(a, b, (((1,), (1,)), ((), ())), preferred_element_type=F32)


def mm_tn(a, b):
    return lax.dot_general(a, b, (((0,), (0,)), ((), ())), preferred_element_type=F32)


def exact(a, b):
    return jnp.dot(a, b, preferred_element_type=F32, precision=lax.Precision.HIGHEST)


def iota(dim, shape=(128, 128)):
    return lax.broadcasted_iota(jnp.int32, shape, dim)


def mirror(dtype=BF16):
    return jnp.where(iota(0) + iota(1) == 127, 1.0, 0.0).astype(dtype)


def softplus(x):
    return jnp.maximum(x, 0.0) + jnp.log1p(jnp.exp(-jnp.abs(x)))


def sigmoid(x):
    return 1.0 / (1.0 + jnp.exp(-x))


def shifted(x):
    back = [x[EDGE : EDGE + SPAN]]
    fore = [back[0]]
    for k in range(1, KERNEL):
        back.append(pltpu.roll(x, k, 0)[EDGE : EDGE + SPAN])
        fore.append(pltpu.roll(x, EXT - k, 0)[EDGE : EDGE + SPAN])
    return back, fore


def conv(taps, rows):
    out = taps[0:1] * rows[0]
    for k in range(1, KERNEL):
        out = out + taps[k : k + 1] * rows[k]
    return out


def lanes(i):
    return pl.ds(pl.multiple_of(i * 128, 128), 128)


MESH = pl.DeviceIdType.MESH


def greet_all(shards, count):
    barrier = pltpu.get_barrier_semaphore()
    seq, zero = lax.axis_index("seq"), lax.axis_index("zero")
    total = 0
    for n in range(count):
        for k in range(shards):
            if (k or n) and (n == 0 or k % 2 == 0):
                there = {"zero": lax.rem(zero + k, shards), "seq": lax.rem(seq + n, count)}
                pl.semaphore_signal(barrier, inc=1, device_id=there, device_id_type=MESH)
                total += 1
    return functools.partial(pl.semaphore_wait, barrier, total)


def push(src, dst, send, recv, axis, peer):
    return pltpu.make_async_remote_copy(
        src_ref=src,
        dst_ref=dst,
        send_sem=send,
        recv_sem=recv,
        device_id={axis: peer},
        device_id_type=MESH,
    )


def split2(x):
    hi = x.astype(BF16)
    return hi, (x - hi.astype(F32)).astype(BF16)


def split3(x):
    hi = x.astype(BF16)
    rest = x - hi.astype(F32)
    mid = rest.astype(BF16)
    return hi, mid, (rest - mid.astype(F32)).astype(BF16)


def exact_left(a, x):
    n = x.shape[1]
    out = mm(a, jnp.concatenate(split3(x), axis=1))
    return out[:, :n] + out[:, n : 2 * n] + out[:, 2 * n :]


def exact_right(x, b):
    n = x.shape[0]
    out = mm(jnp.concatenate(split3(x), axis=0), b)
    return out[:n] + out[n : 2 * n] + out[2 * n :]


def ones_where(keep):
    return jnp.where(keep, 1.0, 0.0).astype(BF16)


def one_hot(at_ref, head):
    at = at_ref[...]
    same = at == head.astype(F32).astype(BF16)
    return jnp.where(same, jnp.ones_like(at), jnp.zeros_like(at))


def strand_swap():
    k, lane = iota(0), iota(1)
    return ones_where((lane >= 32) & (lane < 32 + HEADS) & (k + lane == 31 + HEADS))


def folded(tail, fold):
    size = tail.shape[0] // fold
    out = tail[:size]
    for q in range(1, fold):
        out = out + pltpu.roll(tail[q * size : (q + 1) * size], 24 * q, 1)
    return out


def whole_kernel(
    shards, count, fold,
    hid_hbm, go_hbm, wt_hbm, c_hbm, alog_ref, bias_ref,
    out_ref, gh_ref, full, total2,
    hid_ref, go_ref, wt_in, c_in, wt_pad,
    x_ref, xf_ref, xt_ref, taps_ref, wp_ref, w_out, w_rev, w_slots, c_own, c_slots, before, after,
    vals, slope, u_ref, fu_ref, eg_ref, yoff, duo, e_b, f_b, dt_b,
    own, in_slots, out_slots,
    pick_at, sel_at, sum_at, heads_in, rates, dtx_ref, stack, split, within_t, score, diag, bc_act, bc_t, bc_slope, masks,
    d_score, d_diag, d_bc, acc,
    gi_ref, gf_ref, bcx_ref, g_before, g_after, parts, pair_in, pair_sum, part_in, gathered,
    small, small_in, small2, small2_in,
    local, sides, w_send, w_recv, f_send, f_recv, t_send, t_recv, c_send, c_recv,
    g_sides, p_send, p_recv, zs, zr, ss, sr, ms, mr,
):
    seq, zero = lax.axis_index("seq"), lax.axis_index("zero")
    core = lax.rem(zero, 2)
    chip = lax.div(zero, 2)
    chips = shards // 2
    sibling = zero + 1 - 2 * core
    rows = WIDTH // shards
    fold_rows = rows // fold
    packed = rows + fold_rows
    greeted = greet_all(shards, count)
    loads = [
        pltpu.make_async_copy(src, dst, local.at[n])
        for n, (src, dst) in enumerate(
            ((c_hbm, c_in), (wt_hbm, wt_in), (hid_hbm, hid_ref), (go_hbm, go_ref))
        )
    ]
    for load in loads:
        load.start()
    c_own[...] = jnp.zeros_like(c_own)
    wt_pad[...] = jnp.zeros_like(wt_pad)
    loads[0].wait()
    c_own[:KERNEL] = c_in[...].astype(F32)
    loads[1].wait()
    wt_pad[: wt_in.shape[0], :rows] = wt_in[...].astype(F32)
    w_own = wt_pad[...].T
    w_slots[zero, :rows] = w_own[:rows, :128].astype(BF16)
    w_slots[zero, rows:] = folded(w_own[:rows, 128:], fold).astype(BF16)
    greeted()
    tap_copies = []
    for k in range(1, shards):
        peer = lax.rem(zero + k, shards)
        copy = push(c_own, c_slots.at[zero], t_send.at[k], t_recv.at[k], "zero", peer)
        copy.start()
        tap_copies.append(copy)
    loads[2].wait()
    up = push(
        hid_ref.at[pl.ds(SPAN - 2 * EDGE, 2 * EDGE)], before, sides.at[0], sides.at[1], "seq",
        lax.rem(seq + 1, count),
    )
    down = push(
        hid_ref.at[pl.ds(0, 2 * EDGE)], after, sides.at[2], sides.at[3], "seq",
        lax.rem(seq + count - 1, count),
    )

    @pl.when(seq < count - 1)
    def _():
        up.start()

    @pl.when(seq > 0)
    def _():
        down.start()

    w_copies = []
    for k in range(chips):
        peer = lax.rem(zero + 2 * k, shards) if k else sibling
        copy = push(w_slots.at[zero], w_slots.at[zero], w_send.at[k], w_recv.at[k], "zero", peer)
        copy.start()
        w_copies.append(copy)
    c_slots[zero] = c_own[...]
    w_out[:, 128:] = jnp.zeros((WIDTH, 128), BF16)
    x_ref[EDGE : EDGE + SPAN] = hid_ref[...]
    flip = mirror()
    swap = strand_swap()
    masks[0] = ones_where(iota(0) > iota(1))
    masks[1] = ones_where(iota(0) < iota(1))
    if parts.shape[1] > packed:
        spare = (shards, parts.shape[1] - packed, 128)
        parts[:, packed:] = jnp.zeros(spare, BF16)
    square = (256, 256)
    line, lane = iota(0, square), iota(1, square)
    pick_at[...] = jnp.where(
        line < 192, lax.rem(line, 64) - jnp.where(lane >= 128, 1, 0), -2
    ).astype(F32).astype(BF16)
    wide_shape = (128, 256 * GROUP)
    line, lane = iota(0, wide_shape), iota(1, wide_shape)
    sel_at[...] = (
        lax.rem(line, 64)
        - 2 * lax.div(lane, 256)
        - jnp.where(lax.rem(lane, 256) >= 128, 32, 0)
        - jnp.where(lax.rem(lane, 128) >= HEAD_DIM, 1, 0)
    ).astype(F32).astype(BF16)
    tall = (512, 128)
    line, lane = iota(0, tall), iota(1, tall)
    sum_at[...] = (
        lane
        - jnp.where(line >= 256, 32, 0)
        - jnp.where(lax.rem(line, 128) >= HEAD_DIM, 1, 0)
    ).astype(F32).astype(BF16)
    d_score[...] = jnp.zeros_like(d_score)
    d_diag[...] = jnp.zeros_like(d_diag)
    d_bc[...] = jnp.zeros_like(d_bc)
    acc[...] = jnp.zeros_like(acc)

    @pl.when(seq == 0)
    def _():
        x_ref[:EDGE] = jnp.zeros((EDGE, WIDTH), BF16)
        in_slots[0] = jnp.zeros(in_slots.shape[1:], BF16)

    @pl.when(seq > 0)
    def _():
        up.wait_recv()
        x_ref[:EDGE] = before[EDGE:]

    @pl.when(seq == count - 1)
    def _():
        x_ref[EDGE + SPAN :] = jnp.zeros((EDGE, WIDTH), BF16)
        in_slots[1] = jnp.zeros(in_slots.shape[1:], BF16)

    @pl.when(seq < count - 1)
    def _():
        down.wait_recv()
        x_ref[EDGE + SPAN :] = after[:EDGE]

    for copy in tap_copies:
        copy.wait()
    part = c_own.shape[1]
    for z in range(shards):
        taps_ref[0, :, z * part : (z + 1) * part] = c_slots[z]
    for b in range(PAIRS):
        taps_ref[1, :, b * 128 : (b + 1) * 128] = mm(
            taps_ref[0, :, (PAIRS - 1 - b) * 128 : (PAIRS - b) * 128].astype(BF16), flip
        )

    def values_of(i):
        rows = shifted(x_ref[:, lanes(i)].astype(F32))
        for s in range(2):
            taps = taps_ref[s, :, lanes(i)]
            for d in range(2):
                mixed = conv(taps, rows[d])
                sig = sigmoid(mixed)
                act = mixed * sig
                vals[2 * i + s, d] = act.astype(BF16)
                slope[2 * i + s, d] = sig + act * (1.0 - sig)

    def values_step(i, carry):
        values_of(i)
        return carry

    for b in range(PAIRS):
        xf_ref[:, (PAIRS - 1 - b) * 128 : (PAIRS - b) * 128] = mm(
            x_ref[:, b * 128 : (b + 1) * 128], flip
        ).astype(BF16)
    lax.fori_loop(0, EARLY, values_step, 0)

    for copy in w_copies:
        copy.wait()
    forwards = []
    for k in range(1, chips):
        slot_of = w_slots.at[lax.rem(zero + shards - 2 * k, shards)]
        copy = push(slot_of, slot_of, f_send.at[k], f_recv.at[k], "zero", sibling)
        copy.start()
        forwards.append(copy)

    def unpack(z):
        at = pl.multiple_of(z * rows, 16)
        w_out[pl.ds(at, rows), :128] = w_slots[z, :rows]
        tail = w_slots[z, rows:].astype(F32)
        for q in range(fold):
            moved = pltpu.roll(tail, 128 - 24 * q, 1) if q else tail
            w_out[pl.ds(at + q * fold_rows, fold_rows), 128:] = jnp.where(
                iota(1, (fold_rows, 128)) < HEADS, moved, 0.0
            ).astype(BF16)

    for k in range(chips):
        unpack(lax.rem(zero + shards - 2 * k, shards))
    unpack(sibling)
    for copy in forwards:
        copy.wait()
    for k in range(1, chips):
        unpack(lax.rem(sibling + shards - 2 * k, shards))
    wp_ref[:, :128] = w_out[:, :128]
    wp_ref[:, 128:] = mm(w_out[:, 128:], swap).astype(BF16)
    proj = (mm(x_ref[...], w_out[...]), mm(xf_ref[...], wp_ref[...]))
    loads[3].wait()
    heads_in[...] = jnp.zeros_like(heads_in)
    heads_in[0:1, :HEADS] = alog_ref[...]
    heads_in[1:2, :HEADS] = bias_ref[...]
    place = heads_in[...] + exact_right(heads_in[...], swap)
    rate = jnp.exp(place[0:1])
    rates[0:1] = rate
    dtx = (proj[0] + proj[1])[EDGE : EDGE + SPAN, 128:] + place[1:2]
    dtx_ref[...] = dtx
    delta = softplus(dtx)
    both = jnp.concatenate(
        [ones_where(iota(0) >= iota(1)), ones_where(iota(0) <= iota(1))], axis=0
    )
    within = exact_left(both, -rate * delta)
    ends = jnp.concatenate(
        [
            jnp.broadcast_to(within[SPAN - 1 : SPAN], (SPAN, 128)),
            jnp.broadcast_to(within[SPAN : SPAN + 1], (SPAN, 128)),
        ],
        axis=0,
    )
    spread = jnp.concatenate([jnp.exp(within), jnp.exp(ends - within), delta], axis=0)
    hi, lo = split2(spread)
    wide_low = iota(1, spread.shape) < 64
    stack[...] = jnp.where(
        wide_low, hi.astype(F32), pltpu.roll(lo.astype(F32), 64, 1)
    ).astype(BF16)
    hi, mid, lo = split3(within)
    low_two = iota(1, (256, 128)) < 64
    split[:, :128] = jnp.where(
        low_two, hi.astype(F32), pltpu.roll(mid.astype(F32), 64, 1)
    ).astype(BF16)
    split[:, 128:] = jnp.where(low_two, lo.astype(F32), 0.0).astype(BF16)
    for d in range(2):
        within_t[d] = within[d * 128 : d * 128 + 128].T
    for s in range(2):
        bcx_ref[s] = proj[s][:, :128].astype(BF16).astype(F32)
        bcx = shifted(bcx_ref[s])
        for d in range(2):
            c = 2 * s + d
            mixed = conv(taps_ref[0, :, WIDTH:], bcx[d])
            sig = sigmoid(mixed)
            wide = mixed * sig
            act = wide.astype(BF16)
            bc_slope[c] = sig + wide * (1.0 - sig)
            bc_act[c, 0] = act[:, :STATE]
            bc_act[c, 1] = act[:, STATE:]
            act_t = act.astype(F32).T.astype(BF16)
            bc_t[c] = act_t

    def make_scores():
        for s in range(2):
            scores = []
            for d in range(2):
                c = 2 * s + d
                scores.append(mm(bc_act[c, 1], bc_t[c, :STATE]))
                own_diag = jnp.sum(
                    jnp.where(iota(0) == iota(1), scores[d], 0.0), axis=1, keepdims=True
                )
                diag[c] = jnp.broadcast_to(own_diag, (128, 128))
            score[s] = jnp.where(
                iota(0) > iota(1), scores[0], jnp.where(iota(0) < iota(1), scores[1], 0.0)
            )

    def produce(t):
        all_wide = mm(stack[...], one_hot(sel_at, 2 * GROUP * t))
        for n in range(GROUP):
            g = go_ref[:, lanes(GROUP * t + n)].astype(F32)
            for s in range(2):
                u = 2 * GROUP * t + 2 * n + s
                at = 256 * n + 128 * s
                wide = all_wide[:, at : at + 128]
                dt = wide[512:]
                dt_b[u] = dt
                for d in range(2):
                    e, f = wide[128 * d : 128 * d + 128], wide[256 + 128 * d : 384 + 128 * d]
                    e_b[u, d] = e
                    f_b[u, d] = f
                    step = (vals[u, d].astype(F32) * dt).astype(BF16)
                    u_ref[u, d] = step
                    fu = (step.astype(F32) * f).astype(BF16)
                    fu_ref[u, d] = fu
                    eg = (e * g).astype(BF16)
                    eg_ref[u, d] = eg
                    own[d, u, 0] = mm(bc_t[2 * s + d, :STATE], fu)
                    own[1 - d, u, 1] = mm(bc_t[2 * s + d, STATE:], eg)

    def decay_of(u, d):
        at = SPAN - 1 if d == 0 else 0
        return e_b[u, d, at : at + 1]

    chains = ((0, seq, seq + 1), (1, count - 1 - seq, seq - 1))

    def copy_of(d, u, peer):
        return push(
            out_slots.at[d, u], in_slots.at[d, u], c_send.at[d, u], c_recv.at[d, u], "seq", peer
        )

    def send_first(t):
        for d, place, peer in chains:

            @pl.when(place == 0)
            def _():
                for n in range(2 * GROUP):
                    u = 2 * GROUP * t + n
                    out_slots[d, u] = own[d, u].astype(BF16)
                    copy_of(d, u, peer).start()

    def forward(n):
        for d, place, peer in chains:
            u = n - OFFSET - HOP * place

            @pl.when((place > 0) & (place < count - 1) & (u >= 0) & (u < UNITS))
            def _():
                copy_of(d, u, seq).wait_recv()
                for q in range(2):
                    dec = decay_of(u, d if q == 0 else 1 - d)
                    out_slots[d, u, q] = (
                        own[d, u, q] + dec * in_slots[d, u, q].astype(F32)
                    ).astype(BF16)
                copy_of(d, u, peer).start()

    def arrive(i):
        for d, place, peer in chains:

            @pl.when(place == count - 1)
            def _():
                for s in range(2):
                    copy_of(d, 2 * i + s, seq).wait_recv()

    def inside(i):
        lower = iota(0) >= iota(1)
        low = iota(1) < HEAD_DIM
        go = go_ref[:, lanes(i)]
        g = go.astype(F32)
        none = jnp.zeros((128, 128), BF16)
        g_two = jnp.concatenate([jnp.where(low, go, none), jnp.where(low, none, go)], axis=0)
        kept_ins = []
        for s in range(2):
            u = 2 * i + s
            head = 32 * s + 2 * i
            cols = mm(split[...], one_hot(pick_at, head))
            steps = jnp.concatenate([u_ref[u, 0], u_ref[u, 1]], axis=0)
            dw = mm_nt(g_two, steps)
            sc = score[s]
            ds = jnp.zeros((128, 128), F32)
            below, above = [], []
            for r in range(2):
                at = slice(128 * r, 128 * r + 128)
                gap = jnp.where(
                    lower,
                    cols[:128, at] - within_t[0, pl.ds(head + r, 1), :],
                    cols[128:, at] - within_t[1, pl.ds(head + r, 1), :],
                )
                decay = jnp.exp(gap)
                w = (sc * decay).astype(BF16)
                below.append(w * masks[0])
                above.append(w * masks[1])
                ds = ds + decay * jnp.where(lower, dw[at, :128], dw[at, 128:])
            for d, ws in enumerate((below, above)):
                step = steps[128 * d : 128 * d + 128]
                y_two = mm(jnp.concatenate(ws, axis=0), step)
                kept_ins.append(
                    (
                        jnp.where(low, y_two[:128], y_two[128:]),
                        jnp.where(low, mm_tn(ws[0], go), mm_tn(ws[1], go)),
                        g * step.astype(F32),
                    )
                )
            kept_ins.append(ds)
        for s in range(2):
            for d in range(2):
                y_two, du, on_diag = kept_ins[3 * s + d]
                yoff[2 * i + s, d] = y_two
                duo[2 * i + s, d] = du
                d_diag[2 * s + d] += on_diag
            d_score[s] += kept_ins[3 * s + 2]

    def back(taps, dms, x):
        zero_rows = jnp.zeros((EDGE, 128), F32)
        wides = [jnp.concatenate([zero_rows, dm, zero_rows], axis=0) for dm in dms]
        both = wides[0] + wides[1]
        out = taps[0:1] * both
        sums = [jnp.sum(both * x, axis=0, keepdims=True)]
        for k in range(1, KERNEL):
            both = pltpu.roll(wides[0], EXT - k, 0) + pltpu.roll(wides[1], k, 0)
            out = out + taps[k : k + 1] * both
            sums.append(jnp.sum(both * x, axis=0, keepdims=True))
        return out, jnp.concatenate(sums + [jnp.zeros((8 - KERNEL, 128), F32)], axis=0)

    def finish(i):
        g = go_ref[:, lanes(i)].astype(F32)
        x = x_ref[:, lanes(i)].astype(F32)
        sel_t = one_hot(sum_at, 2 * i)
        ys, parts_of, adds = [], [], []
        for s in range(2):
            u = 2 * i + s
            taps = taps_ref[s, :, lanes(i)]
            dt = dt_b[u]
            y = jnp.zeros((128, 128), F32)
            dms = []
            qt = jnp.zeros((128, 128), F32)
            qs, ends = [], []
            for d in range(2):
                c = 2 * s + d
                s_in, g_in = in_slots[d, u, 0], in_slots[1 - d, u, 1]
                step = u_ref[u, d].astype(F32)
                across = mm(bc_act[c, 1], s_in) * e_b[u, d] + yoff[u, d]
                y = y + across + diag[c] * step
                du = duo[u, d] + f_b[u, d] * mm(bc_act[c, 0], g_in)
                qs.append(g * across - step * du)
                du = du + diag[c] * g
                qt = qt + vals[u, d].astype(F32) * du
                adds.append((c, mm_nt(fu_ref[u, d], g_in), mm_nt(eg_ref[u, d], s_in)))
                leaving = own[d, u, 0] + decay_of(u, d) * s_in.astype(F32)
                ends.append(jnp.sum(leaving * g_in.astype(F32), axis=0, keepdims=True))
                dms.append((dt * du).astype(BF16).astype(F32) * slope[u, d])
            gi, gf = back(taps, dms, x)
            q = jnp.concatenate(qs + [qt] + ends + [jnp.zeros((6, 128), F32)], axis=0)
            parts_of.extend(split2(q))
            ys.append(y.astype(BF16).astype(F32))
            adds.append((s, gi, gf))
        totals = mm(jnp.concatenate(parts_of, axis=1), sel_t)
        for s in range(2):
            for c, db, dc in adds[3 * s : 3 * s + 2]:
                d_bc[c, 0] += db
                d_bc[c, 1] += dc
            _, gi, gf = adds[3 * s + 2]
            gi_ref[s, :, lanes(i)] = gi
            gf_ref[2 * i + s] = gf
        acc[...] += totals
        out_ref[:, lanes(i)] = (ys[0] + ys[1]).astype(BF16)

    groups = PAIRS // GROUP

    def first_part(t, carry):
        produce(t)
        send_first(t)
        return carry

    early = EARLY // GROUP

    def late_part(t, carry):
        for n in range(GROUP):
            values_of(GROUP * t + n)
        first_part(t, carry)
        for n in range(3):
            forward(3 * (t - early) + 3 + n)
        return carry

    before_second = 3 * (groups - early) + 3

    def second_part(i, carry):
        xt_ref[0, lanes(i)] = x_ref[:, lanes(i)].astype(F32).T.astype(BF16)
        xt_ref[1, lanes(i)] = xf_ref[:, lanes(i)].astype(F32).T.astype(BF16)
        w_rev[lanes(i)] = mm(flip, w_out[lanes(PAIRS - 1 - i)]).astype(BF16)
        inside(i)
        forward(before_second + i)
        return carry

    def idle(n, carry):
        forward(n)
        return carry

    before_third = before_second + PAIRS
    began = max(before_third, 2 + OFFSET + HOP * (count - 2))

    def third_part(i, carry):
        forward(began + 2 * i)
        forward(began + 2 * i + 1)
        arrive(i)
        finish(i)
        return carry

    lax.fori_loop(0, early, first_part, 0)
    lax.fori_loop(early, groups, late_part, 0)
    make_scores()
    lax.fori_loop(0, PAIRS, second_part, 0)
    if began > before_third:
        lax.fori_loop(before_third, began, idle, 0)
    lax.fori_loop(0, PAIRS, third_part, 0)

    end_rows = acc[3 * SPAN : 3 * SPAN + 8]
    dl0 = acc[:SPAN] + jnp.where(iota(0) == SPAN - 1, end_rows[0:1], 0.0)
    dl1 = acc[SPAN : 2 * SPAN] + jnp.where(iota(0) == 0, end_rows[1:2], 0.0)
    both_t = jnp.concatenate(
        [ones_where(iota(0) <= iota(1)), ones_where(iota(0) >= iota(1))], axis=1
    )
    d_log = exact_left(both_t, jnp.concatenate([dl0, dl1], axis=0))
    rate = rates[0:1]
    dtx = dtx_ref[...]
    d_raw = (acc[2 * SPAN : 3 * SPAN] - rate * d_log) * sigmoid(dtx)
    sums = jnp.concatenate(
        [
            jnp.sum(d_log * (-rate * softplus(dtx)), axis=0, keepdims=True),
            jnp.sum(d_raw, axis=0, keepdims=True),
            jnp.zeros((6, 128), F32),
        ],
        axis=0,
    )
    unswap = swap.astype(F32).T.astype(BF16)
    heads = jnp.where(iota(1, (8, 128)) < HEADS, sums, 0.0) + exact_right(sums, unswap)
    ddt = (
        jnp.where(iota(1) < HEADS, d_raw, 0.0).astype(BF16),
        mm(d_raw.astype(BF16), unswap).astype(BF16),
    )
    wides = []
    for s in range(2):
        taps = taps_ref[0, :, WIDTH:]
        dms = []
        for d in range(2):
            c = 2 * s + d
            on_diag = jnp.sum(d_diag[c], axis=1, keepdims=True)
            off = iota(0) > iota(1) if d == 0 else iota(0) < iota(1)
            ds = jnp.where(
                off, d_score[s], jnp.where(iota(0) == iota(1), on_diag, 0.0)
            ).astype(BF16)
            db = d_bc[c, 0] + mm_tn(ds, bc_act[c, 1])
            dc = d_bc[c, 1] + mm(ds, bc_act[c, 0])
            dms.append(jnp.concatenate([db, dc], axis=1).astype(BF16).astype(F32) * bc_slope[c])
        gi, gf = back(taps, dms, bcx_ref[s])
        gi_ref[s, :, WIDTH:] = gi
        gf_ref[UNITS + s] = gf
        edge = jnp.zeros((EDGE, 128), F32)
        wides.append(
            jnp.concatenate(
                [gi, jnp.concatenate([edge, ddt[s].astype(F32), edge], axis=0)], axis=1
            ).astype(BF16)
        )
    g_up = push(
        gi_ref.at[:, pl.ds(EDGE + SPAN, EDGE)], g_before, g_sides.at[0], g_sides.at[1], "seq",
        lax.rem(seq + 1, count),
    )
    g_down = push(
        gi_ref.at[:, pl.ds(0, EDGE)], g_after, g_sides.at[2], g_sides.at[3], "seq",
        lax.rem(seq + count - 1, count),
    )

    def weight_part(z):
        at = pl.ds(pl.multiple_of(z * rows, 16), rows)
        total = mm(xt_ref[0, at], wides[0]) + mm(xt_ref[1, at], wides[1])
        parts[z, :rows] = total[:, :128].astype(BF16)
        parts[z, rows:packed] = folded(total[:, 128:], fold).astype(BF16)

    pairs = []
    for k in list(range(1, chips)) + [0]:
        z = 2 * lax.rem(chip + k, chips) + 1 - core
        weight_part(z)
        copy = push(
            parts.at[z], pair_in.at[lax.div(z, 2)], p_send.at[k], p_recv.at[k], "zero", sibling
        )
        copy.start()
        pairs.append(copy)
    for k in list(range(1, chips)) + [0]:
        weight_part(2 * lax.rem(chip + k, chips) + core)

    @pl.when(seq < count - 1)
    def _():
        g_up.start()

    @pl.when(seq > 0)
    def _():
        g_down.start()

    @pl.when(seq == 0)
    def _():
        g_before[...] = jnp.zeros_like(g_before)

    @pl.when(seq == count - 1)
    def _():
        g_after[...] = jnp.zeros_like(g_after)

    chunk = gathered.shape[0] // count
    here = pl.ds(pl.multiple_of(seq * chunk, 16), chunk)
    scatter = []
    for k in list(range(1, chips)) + [0]:
        there = lax.rem(chip + k, chips)
        pairs[k - 1].wait()
        pair_sum[there] = (
            parts[2 * there + core].astype(F32) + pair_in[there].astype(F32)
        ).astype(BF16)
        for n in range(count):
            if k or n:
                peer = lax.rem(seq + n, count)
                copy = pltpu.make_async_remote_copy(
                    src_ref=pair_sum.at[there, pl.ds(pl.multiple_of(peer * chunk, 16), chunk)],
                    dst_ref=part_in.at[k, n],
                    send_sem=zs.at[k, n],
                    recv_sem=zr.at[k, n],
                    device_id={"zero": 2 * there + core, "seq": peer},
                    device_id_type=MESH,
                )
                copy.start()
                scatter.append(copy)
    swapped = exact_right(
        jnp.concatenate([gf_ref[2 * (PAIRS - 1 - i) + 1] for i in range(PAIRS)], axis=0), flip
    )
    small[...] = jnp.zeros_like(small)
    for i in range(PAIRS):
        block = gf_ref[2 * i] + swapped[8 * i : 8 * i + 8]
        small[KERNEL * i : KERNEL * i + KERNEL] = block[:KERNEL]
    block = gf_ref[UNITS] + gf_ref[UNITS + 1]
    small[KERNEL * PAIRS : KERNEL * PAIRS + KERNEL] = block[:KERNEL]
    small[KERNEL * PAIRS + KERNEL : KERNEL * PAIRS + KERNEL + 2] = heads[:2]
    first = []
    for k in range(1, shards):
        peer = lax.rem(zero + k, shards)
        copy = push(small, small_in.at[zero], ms.at[0, k], mr.at[0, k], "zero", peer)
        copy.start()
        first.append(copy)
    small_in[zero] = small[...]

    @pl.when(seq > 0)
    def _():
        g_up.wait_recv()

    @pl.when(seq < count - 1)
    def _():
        g_down.wait_recv()

    def settled(s, at):
        top = gi_ref[s, EDGE : 2 * EDGE, at] + g_before[s, :, at]
        low = gi_ref[s, SPAN : SPAN + EDGE, at] + g_after[s, :, at]
        return jnp.concatenate([top, gi_ref[s, 2 * EDGE : SPAN, at], low], axis=0).astype(BF16)

    gps = [
        jnp.concatenate([settled(s, slice(WIDTH, CHANNELS)), ddt[s]], axis=1) for s in range(2)
    ]

    def hidden_part(i):
        at = slice(i * 128, i * 128 + 128)
        a = (settled(0, at).astype(F32) + mm_nt(gps[0], w_out[at])).astype(BF16)
        b = (settled(1, at).astype(F32) + mm_nt(gps[1], w_rev[at])).astype(BF16)
        gh_ref[:, at] = (a.astype(F32) + b.astype(F32)).astype(BF16)

    for copy in first:
        copy.wait()
    summed = small_in[0]
    for z in range(1, shards):
        summed = summed + small_in[z]
    small2[...] = summed
    second = []
    for k in range(1, count):
        peer = lax.rem(seq + k, count)
        copy = push(small2, small2_in.at[seq], ms.at[1, shards + k], mr.at[1, shards + k], "seq", peer)
        copy.start()
        second.append(copy)
    small2_in[seq] = small2[...]
    for i in range(PAIRS // 2):
        hidden_part(i)
    for copy in scatter:
        copy.wait()
    summed = parts[zero, here].astype(F32) + pair_in[chip, here].astype(F32)
    for k in range(chips):
        for n in range(count):
            if k or n:
                summed = summed + part_in[k, n].astype(F32)
    gathered[here] = summed.astype(BF16)
    third = []
    for k in range(1, count):
        peer = lax.rem(seq + k, count)
        copy = push(gathered.at[here], gathered.at[here], ss.at[1, k], sr.at[1, k], "seq", peer)
        copy.start()
        third.append(copy)
    for i in range(PAIRS // 2, PAIRS):
        hidden_part(i)
    for copy in second:
        copy.wait()
    summed = small2_in[0]
    for z in range(1, count):
        summed = summed + small2_in[z]
    total2[...] = summed
    for d, place, peer in chains:

        @pl.when(place < count - 1)
        def _():
            def sent(u, carry):
                copy_of(d, u, peer).wait_send()
                return carry

            lax.fori_loop(0, UNITS, sent, 0)

    @pl.when(seq < count - 1)
    def _():
        up.wait_send()

    @pl.when(seq > 0)
    def _():
        down.wait_send()

    @pl.when(seq < count - 1)
    def _():
        g_up.wait_send()

    @pl.when(seq > 0)
    def _():
        g_down.wait_send()

    for copy in third:
        copy.wait()
    full[...] = gathered[...]


def emit_kernel(
    shards, fold, out_ref, gh_ref, full, total, out_hbm, gh_hbm, gw_ref, gc_ref, gd_ref,
    wide, taps, sems,
):
    copies = [
        pltpu.make_async_copy(out_ref, out_hbm, sems.at[0]),
        pltpu.make_async_copy(gh_ref, gh_hbm, sems.at[1]),
    ]
    for copy in copies:
        copy.start()
    rows = WIDTH // shards
    fold_rows = rows // fold
    tail = full[rows : rows + fold_rows].astype(F32)
    wide[...] = jnp.zeros_like(wide)
    wide[:rows, :128] = full[:rows].astype(F32)
    for q in range(fold):
        moved = pltpu.roll(tail, 128 - 24 * q, 1) if q else tail
        wide[q * fold_rows : (q + 1) * fold_rows, 128:] = moved
    gw_ref[...] = wide[...].T[: gw_ref.shape[0], :rows]
    gd_ref[...] = total[KERNEL * PAIRS + KERNEL : KERNEL * PAIRS + KERNEL + 2, :HEADS]
    for i in range(PAIRS + 1):
        taps[:, i * 128 : i * 128 + 128] = total[KERNEL * i : KERNEL * i + KERNEL]
    zero = lax.axis_index("zero")
    width = gc_ref.shape[1]
    for z in range(shards):

        @pl.when(zero == z)
        def _():
            gc_ref[...] = taps[:, z * width : (z + 1) * width]

    for copy in copies:
        copy.wait()


def spec(space):
    return pl.BlockSpec(memory_space=space)


SQ4 = (4, 128, 128)
SQ2 = (2, 128, 128)
TILES = (UNITS, 2, 128, 128)


def per_device(hidden, grad_out, w_proj, conv_w, a_log, dt_bias):
    assert hidden.shape[:2] == (1, SPAN)
    count, shards = lax.axis_size("seq"), lax.axis_size("zero")
    chips = shards // 2
    rows, columns = w_proj.shape
    part = CHANNELS // shards
    fold = 5 if rows % 80 == 0 else 1
    packed = rows + rows // fold
    step = 16 * count
    padded = -(-packed // step) * step
    lines = 48
    wide_rows = -(-rows // 128) * 128
    pieces = (2, UNITS, 2, STATE, 128)
    edges = (2, EDGE, CHANNELS)
    scratch = [
        ((SPAN, WIDTH), BF16), ((SPAN, WIDTH), BF16), ((columns, rows), BF16),
        ((KERNEL, part), BF16), ((256, wide_rows), F32),
        ((EXT, WIDTH), BF16), ((EXT, WIDTH), BF16), ((2, WIDTH, EXT), BF16),
        ((2, 8, CHANNELS), F32), ((WIDTH, 256), BF16), ((WIDTH, 256), BF16), ((WIDTH, 256), BF16),
        ((shards, packed, 128), BF16), ((8, part), F32), ((shards, 8, part), F32),
        ((2 * EDGE, WIDTH), BF16), ((2 * EDGE, WIDTH), BF16),
        (TILES, BF16), (TILES, F32), (TILES, BF16), (TILES, BF16), (TILES, BF16),
        (TILES, F32), (TILES, F32), (TILES, F32), (TILES, F32), ((UNITS, 128, 128), F32),
        (pieces, F32), (pieces, BF16), (pieces, BF16),
        ((256, 256), BF16), ((128, 256 * GROUP), BF16), ((512, 128), BF16),
        ((8, 128), F32), ((8, 128), F32), ((128, 128), F32), ((5 * 128, 128), BF16), ((256, 256), BF16),
        (SQ2, F32), (SQ2, F32), (SQ4, F32), ((4, 2, 128, STATE), BF16), (SQ4, BF16),
        (SQ4, F32), (SQ2, BF16), (SQ2, F32), (SQ4, F32), ((4, 2, 128, STATE), F32),
        ((3 * SPAN + 8, 128), F32),
        ((2, EXT, CHANNELS), F32), ((UNITS + 2, 8, 128), F32), ((2, EXT, 128), F32),
        (edges, F32), (edges, F32),
        ((shards, padded, 128), BF16), ((chips, padded, 128), BF16),
        ((chips, padded, 128), BF16), ((chips, count, padded // count, 128), BF16),
        ((padded, 128), BF16),
        ((lines, 128), F32), ((shards, lines, 128), F32),
        ((lines, 128), F32), ((count, lines, 128), F32),
    ]
    sems = [
        (4,), (4,), (chips,), (chips,), (chips,), (chips,), (shards,), (shards,),
        (2, UNITS), (2, UNITS), (4,), (chips,), (chips,), (chips, count), (chips, count),
        (2, count), (2, count), (2, shards + count), (2, shards + count),
    ]
    anywhere = spec(pl.ANY)
    outs = pl.pallas_call(
        functools.partial(whole_kernel, shards, count, fold),
        out_shape=[
            jax.ShapeDtypeStruct((SPAN, WIDTH), BF16), jax.ShapeDtypeStruct((SPAN, WIDTH), BF16),
            jax.ShapeDtypeStruct((padded, 128), BF16), jax.ShapeDtypeStruct((lines, 128), F32),
        ],
        in_specs=[spec(pltpu.HBM)] * 4 + [spec(pltpu.VMEM)] * 2,
        scratch_shapes=[pltpu.VMEM(s, t) for s, t in scratch]
        + [pltpu.SemaphoreType.DMA(s) for s in sems],
        compiler_params=pltpu.CompilerParams(
            vmem_limit_bytes=54300 * 1024, collective_id=0, has_side_effects=True
        ),
    )(hidden[0], grad_out[0], w_proj.T, conv_w, a_log[None], dt_bias[None])
    output, grad_hidden, share_w, share_c, grad_heads = pl.pallas_call(
        functools.partial(emit_kernel, shards, fold),
        out_shape=[
            jax.ShapeDtypeStruct((SPAN, WIDTH), BF16), jax.ShapeDtypeStruct((SPAN, WIDTH), BF16),
            jax.ShapeDtypeStruct((columns, rows), F32),
            jax.ShapeDtypeStruct((KERNEL, part), F32), jax.ShapeDtypeStruct((2, HEADS), F32),
        ],
        out_specs=[anywhere] * 2 + [spec(pltpu.VMEM)] * 3,
        scratch_shapes=[
            pltpu.VMEM((wide_rows, 256), F32), pltpu.VMEM((KERNEL, CHANNELS), F32),
            pltpu.SemaphoreType.DMA((2,)),
        ],
        compiler_params=pltpu.CompilerParams(vmem_limit_bytes=8 * 1024 * 1024),
    )(*outs)
    return (output[None], grad_hidden[None], share_w.T, share_c, grad_heads)


def solution(mesh):
    return jax.shard_map(
        per_device,
        mesh=mesh,
        in_specs=(
            P(("grp", "zero"), "seq", None),
            P(("grp", "zero"), "seq", None),
            P("zero", None),
            P(None, "zero"),
            P(),
            P(),
        ),
        out_specs=(
            P(("grp", "zero"), "seq", None),
            P(("grp", "zero"), "seq", None),
            P(("grp", "zero"), None),
            P("grp", "zero"),
            P("grp", None),
        ),
        check_vma=False,
    )
```

```python
import functools
import jax
import jax.numpy as jnp
from jax import lax
from jax.experimental import pallas as pl
from jax.experimental.pallas import tpu as pltpu
from jax.sharding import PartitionSpec as P

WIDTH = 1280
STATE = 64
HEAD_DIM = 64
SPAN = 128
KERNEL = 4
HEADS = 20
PAIRS = WIDTH // 128
CHANNELS = WIDTH + 2 * STATE
EDGE = 8
EXT = SPAN + 2 * EDGE
F32 = jnp.float32
BF16 = jnp.bfloat16
UNITS = 2 * PAIRS
HOP = 6
OFFSET = 3
GROUP = 2
EARLY = 4


def mm(a, b):
    return jnp.dot(a, b, preferred_element_type=F32)


def mm_nt(a, b):
    return lax.dot_general(a, b, (((1,), (1,)), ((), ())), preferred_element_type=F32)


def mm_tn(a, b):
    return lax.dot_general(a, b, (((0,), (0,)), ((), ())), preferred_element_type=F32)


def exact(a, b):
    return jnp.dot(a, b, preferred_element_type=F32, precision=lax.Precision.HIGHEST)


def iota(dim, shape=(128, 128)):
    return lax.broadcasted_iota(jnp.int32, shape, dim)


def mirror(dtype=BF16):
    return jnp.where(iota(0) + iota(1) == 127, 1.0, 0.0).astype(dtype)


def softplus(x):
    return jnp.maximum(x, 0.0) + jnp.log1p(jnp.exp(-jnp.abs(x)))


def sigmoid(x):
    return 1.0 / (1.0 + jnp.exp(-x))


def shifted(x):
    back = [x[EDGE : EDGE + SPAN]]
    fore = [back[0]]
    for k in range(1, KERNEL):
        back.append(pltpu.roll(x, k, 0)[EDGE : EDGE + SPAN])
        fore.append(pltpu.roll(x, EXT - k, 0)[EDGE : EDGE + SPAN])
    return back, fore


def conv(taps, rows):
    out = taps[0:1] * rows[0]
    for k in range(1, KERNEL):
        out = out + taps[k : k + 1] * rows[k]
    return out


def lanes(i):
    return pl.ds(pl.multiple_of(i * 128, 128), 128)


MESH = pl.DeviceIdType.MESH


def greet_all(shards, count):
    barrier = pltpu.get_barrier_semaphore()
    seq, zero = lax.axis_index("seq"), lax.axis_index("zero")
    total = 0
    for n in range(count):
        for k in range(shards):
            if (k or n) and (n == 0 or k % 2 == 0):
                there = {"zero": lax.rem(zero + k, shards), "seq": lax.rem(seq + n, count)}
                pl.semaphore_signal(barrier, inc=1, device_id=there, device_id_type=MESH)
                total += 1
    return functools.partial(pl.semaphore_wait, barrier, total)


def push(src, dst, send, recv, axis, peer):
    return pltpu.make_async_remote_copy(
        src_ref=src,
        dst_ref=dst,
        send_sem=send,
        recv_sem=recv,
        device_id={axis: peer},
        device_id_type=MESH,
    )


def split2(x):
    hi = x.astype(BF16)
    return hi, (x - hi.astype(F32)).astype(BF16)


def split3(x):
    hi = x.astype(BF16)
    rest = x - hi.astype(F32)
    mid = rest.astype(BF16)
    return hi, mid, (rest - mid.astype(F32)).astype(BF16)


def exact_left(a, x):
    n = x.shape[1]
    out = mm(a, jnp.concatenate(split3(x), axis=1))
    return out[:, :n] + out[:, n : 2 * n] + out[:, 2 * n :]


def exact_right(x, b):
    n = x.shape[0]
    out = mm(jnp.concatenate(split3(x), axis=0), b)
    return out[:n] + out[n : 2 * n] + out[2 * n :]


def ones_where(keep):
    return jnp.where(keep, 1.0, 0.0).astype(BF16)


def one_hot(at_ref, head):
    at = at_ref[...]
    same = at == head.astype(F32).astype(BF16)
    return jnp.where(same, jnp.ones_like(at), jnp.zeros_like(at))


def strand_swap():
    k, lane = iota(0), iota(1)
    return ones_where((lane >= 32) & (lane < 32 + HEADS) & (k + lane == 31 + HEADS))


def folded(tail, fold):
    size = tail.shape[0] // fold
    out = tail[:size]
    for q in range(1, fold):
        out = out + pltpu.roll(tail[q * size : (q + 1) * size], 24 * q, 1)
    return out


def whole_kernel(
    shards, count, fold,
    hid_hbm, go_hbm, wt_hbm, c_hbm, alog_ref, bias_ref,
    out_ref, gh_ref, full, total2,
    hid_ref, go_ref, wt_in, c_in, wt_pad,
    x_ref, xf_ref, xt_ref, taps_ref, wp_ref, w_out, w_rev, w_slots, c_own, c_slots, before, after,
    vals, slope, u_ref, fu_ref, eg_ref, yoff, duo, e_b, f_b, dt_b,
    own, in_slots, out_slots,
    pick_at, sel_at, sum_at, heads_in, rates, dtx_ref, stack, split, within_t, score, diag, bc_act, bc_t, bc_slope, masks,
    d_score, d_diag, d_bc, acc,
    gi_ref, gf_ref, bcx_ref, g_out, g_before, g_after, parts, pair_in, pair_sum, part_in, gathered,
    small, small_in, small2, small2_in,
    local, sides, w_send, w_recv, f_send, f_recv, t_send, t_recv, c_send, c_recv,
    g_sides, p_send, p_recv, zs, zr, ss, sr, ms, mr,
):
    seq, zero = lax.axis_index("seq"), lax.axis_index("zero")
    core = lax.rem(zero, 2)
    chip = lax.div(zero, 2)
    chips = shards // 2
    sibling = zero + 1 - 2 * core
    rows = WIDTH // shards
    fold_rows = rows // fold
    packed = rows + fold_rows
    greeted = greet_all(shards, count)
    loads = [
        pltpu.make_async_copy(src, dst, local.at[n])
        for n, (src, dst) in enumerate(
            ((c_hbm, c_in), (wt_hbm, wt_in), (hid_hbm, hid_ref), (go_hbm, go_ref))
        )
    ]
    for load in loads:
        load.start()
    c_own[...] = jnp.zeros_like(c_own)
    wt_pad[...] = jnp.zeros_like(wt_pad)
    loads[0].wait()
    c_own[:KERNEL] = c_in[...].astype(F32)
    loads[1].wait()
    wt_pad[: wt_in.shape[0], :rows] = wt_in[...].astype(F32)
    w_own = wt_pad[...].T
    w_slots[zero, :rows] = w_own[:rows, :128].astype(BF16)
    w_slots[zero, rows:] = folded(w_own[:rows, 128:], fold).astype(BF16)
    greeted()
    tap_copies = []
    for k in range(1, shards):
        peer = lax.rem(zero + k, shards)
        copy = push(c_own, c_slots.at[zero], t_send.at[k], t_recv.at[k], "zero", peer)
        copy.start()
        tap_copies.append(copy)
    loads[2].wait()
    up = push(
        hid_ref.at[pl.ds(SPAN - 2 * EDGE, 2 * EDGE)], before, sides.at[0], sides.at[1], "seq",
        lax.rem(seq + 1, count),
    )
    down = push(
        hid_ref.at[pl.ds(0, 2 * EDGE)], after, sides.at[2], sides.at[3], "seq",
        lax.rem(seq + count - 1, count),
    )

    @pl.when(seq < count - 1)
    def _():
        up.start()

    @pl.when(seq > 0)
    def _():
        down.start()

    w_copies = []
    for k in range(chips):
        peer = lax.rem(zero + 2 * k, shards) if k else sibling
        copy = push(w_slots.at[zero], w_slots.at[zero], w_send.at[k], w_recv.at[k], "zero", peer)
        copy.start()
        w_copies.append(copy)
    c_slots[zero] = c_own[...]
    w_out[:, 128:] = jnp.zeros((WIDTH, 128), BF16)
    x_ref[EDGE : EDGE + SPAN] = hid_ref[...]
    flip = mirror()
    swap = strand_swap()
    masks[0] = ones_where(iota(0) > iota(1))
    masks[1] = ones_where(iota(0) < iota(1))
    if parts.shape[1] > packed:
        spare = (shards, parts.shape[1] - packed, 128)
        parts[:, packed:] = jnp.zeros(spare, BF16)
    square = (256, 256)
    line, lane = iota(0, square), iota(1, square)
    pick_at[...] = jnp.where(
        line < 192, lax.rem(line, 64) - jnp.where(lane >= 128, 1, 0), -2
    ).astype(F32).astype(BF16)
    wide_shape = (128, 256 * GROUP)
    line, lane = iota(0, wide_shape), iota(1, wide_shape)
    sel_at[...] = (
        lax.rem(line, 64)
        - 2 * lax.div(lane, 256)
        - jnp.where(lax.rem(lane, 256) >= 128, 32, 0)
        - jnp.where(lax.rem(lane, 128) >= HEAD_DIM, 1, 0)
    ).astype(F32).astype(BF16)
    tall = (512, 128)
    line, lane = iota(0, tall), iota(1, tall)
    sum_at[...] = (
        lane
        - jnp.where(line >= 256, 32, 0)
        - jnp.where(lax.rem(line, 128) >= HEAD_DIM, 1, 0)
    ).astype(F32).astype(BF16)
    d_score[...] = jnp.zeros_like(d_score)
    d_diag[...] = jnp.zeros_like(d_diag)
    d_bc[...] = jnp.zeros_like(d_bc)
    acc[...] = jnp.zeros_like(acc)

    @pl.when(seq == 0)
    def _():
        x_ref[:EDGE] = jnp.zeros((EDGE, WIDTH), BF16)
        in_slots[0] = jnp.zeros(in_slots.shape[1:], BF16)

    @pl.when(seq > 0)
    def _():
        up.wait_recv()
        x_ref[:EDGE] = before[EDGE:]

    @pl.when(seq == count - 1)
    def _():
        x_ref[EDGE + SPAN :] = jnp.zeros((EDGE, WIDTH), BF16)
        in_slots[1] = jnp.zeros(in_slots.shape[1:], BF16)

    @pl.when(seq < count - 1)
    def _():
        down.wait_recv()
        x_ref[EDGE + SPAN :] = after[:EDGE]

    for copy in tap_copies:
        copy.wait()
    part = c_own.shape[1]
    for z in range(shards):
        taps_ref[0, :, z * part : (z + 1) * part] = c_slots[z]
    for b in range(PAIRS):
        taps_ref[1, :, b * 128 : (b + 1) * 128] = mm(
            taps_ref[0, :, (PAIRS - 1 - b) * 128 : (PAIRS - b) * 128].astype(BF16), flip
        )

    def values_of(i):
        rows = shifted(x_ref[:, lanes(i)].astype(F32))
        for s in range(2):
            taps = taps_ref[s, :, lanes(i)]
            for d in range(2):
                mixed = conv(taps, rows[d])
                sig = sigmoid(mixed)
                act = mixed * sig
                vals[2 * i + s, d] = act.astype(BF16)
                slope[2 * i + s, d] = sig + act * (1.0 - sig)

    def values_step(i, carry):
        values_of(i)
        return carry

    for b in range(PAIRS):
        xf_ref[:, (PAIRS - 1 - b) * 128 : (PAIRS - b) * 128] = mm(
            x_ref[:, b * 128 : (b + 1) * 128], flip
        ).astype(BF16)
    lax.fori_loop(0, EARLY, values_step, 0)

    for copy in w_copies:
        copy.wait()
    forwards = []
    for k in range(1, chips):
        slot_of = w_slots.at[lax.rem(zero + shards - 2 * k, shards)]
        copy = push(slot_of, slot_of, f_send.at[k], f_recv.at[k], "zero", sibling)
        copy.start()
        forwards.append(copy)

    def unpack(z):
        at = pl.multiple_of(z * rows, 16)
        w_out[pl.ds(at, rows), :128] = w_slots[z, :rows]
        tail = w_slots[z, rows:].astype(F32)
        for q in range(fold):
            moved = pltpu.roll(tail, 128 - 24 * q, 1) if q else tail
            w_out[pl.ds(at + q * fold_rows, fold_rows), 128:] = jnp.where(
                iota(1, (fold_rows, 128)) < HEADS, moved, 0.0
            ).astype(BF16)

    for k in range(chips):
        unpack(lax.rem(zero + shards - 2 * k, shards))
    unpack(sibling)
    for copy in forwards:
        copy.wait()
    for k in range(1, chips):
        unpack(lax.rem(sibling + shards - 2 * k, shards))
    wp_ref[:, :128] = w_out[:, :128]
    wp_ref[:, 128:] = mm(w_out[:, 128:], swap).astype(BF16)
    proj = (mm(x_ref[...], w_out[...]), mm(xf_ref[...], wp_ref[...]))
    loads[3].wait()
    heads_in[...] = jnp.zeros_like(heads_in)
    heads_in[0:1, :HEADS] = alog_ref[...]
    heads_in[1:2, :HEADS] = bias_ref[...]
    place = heads_in[...] + exact_right(heads_in[...], swap)
    rate = jnp.exp(place[0:1])
    rates[0:1] = rate
    dtx = (proj[0] + proj[1])[EDGE : EDGE + SPAN, 128:] + place[1:2]
    dtx_ref[...] = dtx
    delta = softplus(dtx)
    both = jnp.concatenate(
        [ones_where(iota(0) >= iota(1)), ones_where(iota(0) <= iota(1))], axis=0
    )
    within = exact_left(both, -rate * delta)
    ends = jnp.concatenate(
        [
            jnp.broadcast_to(within[SPAN - 1 : SPAN], (SPAN, 128)),
            jnp.broadcast_to(within[SPAN : SPAN + 1], (SPAN, 128)),
        ],
        axis=0,
    )
    spread = jnp.concatenate([jnp.exp(within), jnp.exp(ends - within), delta], axis=0)
    hi, lo = split2(spread)
    wide_low = iota(1, spread.shape) < 64
    stack[...] = jnp.where(
        wide_low, hi.astype(F32), pltpu.roll(lo.astype(F32), 64, 1)
    ).astype(BF16)
    hi, mid, lo = split3(within)
    low_two = iota(1, (256, 128)) < 64
    split[:, :128] = jnp.where(
        low_two, hi.astype(F32), pltpu.roll(mid.astype(F32), 64, 1)
    ).astype(BF16)
    split[:, 128:] = jnp.where(low_two, lo.astype(F32), 0.0).astype(BF16)
    for d in range(2):
        within_t[d] = within[d * 128 : d * 128 + 128].T
    for s in range(2):
        bcx_ref[s] = proj[s][:, :128].astype(BF16).astype(F32)
        bcx = shifted(bcx_ref[s])
        for d in range(2):
            c = 2 * s + d
            mixed = conv(taps_ref[0, :, WIDTH:], bcx[d])
            sig = sigmoid(mixed)
            wide = mixed * sig
            act = wide.astype(BF16)
            bc_slope[c] = sig + wide * (1.0 - sig)
            bc_act[c, 0] = act[:, :STATE]
            bc_act[c, 1] = act[:, STATE:]
            act_t = act.astype(F32).T.astype(BF16)
            bc_t[c] = act_t

    def make_scores():
        for s in range(2):
            scores = []
            for d in range(2):
                c = 2 * s + d
                scores.append(mm(bc_act[c, 1], bc_t[c, :STATE]))
                own_diag = jnp.sum(
                    jnp.where(iota(0) == iota(1), scores[d], 0.0), axis=1, keepdims=True
                )
                diag[c] = jnp.broadcast_to(own_diag, (128, 128))
            score[s] = jnp.where(
                iota(0) > iota(1), scores[0], jnp.where(iota(0) < iota(1), scores[1], 0.0)
            )

    def produce(t):
        all_wide = mm(stack[...], one_hot(sel_at, 2 * GROUP * t))
        for n in range(GROUP):
            g = go_ref[:, lanes(GROUP * t + n)].astype(F32)
            for s in range(2):
                u = 2 * GROUP * t + 2 * n + s
                at = 256 * n + 128 * s
                wide = all_wide[:, at : at + 128]
                dt = wide[512:]
                dt_b[u] = dt
                for d in range(2):
                    e, f = wide[128 * d : 128 * d + 128], wide[256 + 128 * d : 384 + 128 * d]
                    e_b[u, d] = e
                    f_b[u, d] = f
                    step = (vals[u, d].astype(F32) * dt).astype(BF16)
                    u_ref[u, d] = step
                    fu = (step.astype(F32) * f).astype(BF16)
                    fu_ref[u, d] = fu
                    eg = (e * g).astype(BF16)
                    eg_ref[u, d] = eg
                    own[d, u, 0] = mm(bc_t[2 * s + d, :STATE], fu)
                    own[1 - d, u, 1] = mm(bc_t[2 * s + d, STATE:], eg)

    def decay_of(u, d):
        at = SPAN - 1 if d == 0 else 0
        return e_b[u, d, at : at + 1]

    chains = ((0, seq, seq + 1), (1, count - 1 - seq, seq - 1))

    def copy_of(d, u, peer):
        return push(
            out_slots.at[d, u], in_slots.at[d, u], c_send.at[d, u], c_recv.at[d, u], "seq", peer
        )

    def send_first(t):
        for d, place, peer in chains:

            @pl.when(place == 0)
            def _():
                for n in range(2 * GROUP):
                    u = 2 * GROUP * t + n
                    out_slots[d, u] = own[d, u].astype(BF16)
                    copy_of(d, u, peer).start()

    def forward(n):
        for d, place, peer in chains:
            u = n - OFFSET - HOP * place

            @pl.when((place > 0) & (place < count - 1) & (u >= 0) & (u < UNITS))
            def _():
                copy_of(d, u, seq).wait_recv()
                for q in range(2):
                    dec = decay_of(u, d if q == 0 else 1 - d)
                    out_slots[d, u, q] = (
                        own[d, u, q] + dec * in_slots[d, u, q].astype(F32)
                    ).astype(BF16)
                copy_of(d, u, peer).start()

    def arrive(i):
        for d, place, peer in chains:

            @pl.when(place == count - 1)
            def _():
                for s in range(2):
                    copy_of(d, 2 * i + s, seq).wait_recv()

    def inside(i):
        lower = iota(0) >= iota(1)
        low = iota(1) < HEAD_DIM
        go = go_ref[:, lanes(i)]
        g = go.astype(F32)
        none = jnp.zeros((128, 128), BF16)
        g_two = jnp.concatenate([jnp.where(low, go, none), jnp.where(low, none, go)], axis=0)
        kept_ins = []
        for s in range(2):
            u = 2 * i + s
            head = 32 * s + 2 * i
            cols = mm(split[...], one_hot(pick_at, head))
            steps = jnp.concatenate([u_ref[u, 0], u_ref[u, 1]], axis=0)
            dw = mm_nt(g_two, steps)
            sc = score[s]
            ds = jnp.zeros((128, 128), F32)
            below, above = [], []
            for r in range(2):
                at = slice(128 * r, 128 * r + 128)
                gap = jnp.where(
                    lower,
                    cols[:128, at] - within_t[0, pl.ds(head + r, 1), :],
                    cols[128:, at] - within_t[1, pl.ds(head + r, 1), :],
                )
                decay = jnp.exp(gap)
                w = (sc * decay).astype(BF16)
                below.append(w * masks[0])
                above.append(w * masks[1])
                ds = ds + decay * jnp.where(lower, dw[at, :128], dw[at, 128:])
            for d, ws in enumerate((below, above)):
                step = steps[128 * d : 128 * d + 128]
                y_two = mm(jnp.concatenate(ws, axis=0), step)
                kept_ins.append(
                    (
                        jnp.where(low, y_two[:128], y_two[128:]),
                        jnp.where(low, mm_tn(ws[0], go), mm_tn(ws[1], go)),
                        g * step.astype(F32),
                    )
                )
            kept_ins.append(ds)
        for s in range(2):
            for d in range(2):
                y_two, du, on_diag = kept_ins[3 * s + d]
                yoff[2 * i + s, d] = y_two
                duo[2 * i + s, d] = du
                d_diag[2 * s + d] += on_diag
            d_score[s] += kept_ins[3 * s + 2]

    def back(taps, dms, x):
        zero_rows = jnp.zeros((EDGE, 128), F32)
        wides = [jnp.concatenate([zero_rows, dm, zero_rows], axis=0) for dm in dms]
        both = wides[0] + wides[1]
        out = taps[0:1] * both
        sums = [jnp.sum(both * x, axis=0, keepdims=True)]
        for k in range(1, KERNEL):
            both = pltpu.roll(wides[0], EXT - k, 0) + pltpu.roll(wides[1], k, 0)
            out = out + taps[k : k + 1] * both
            sums.append(jnp.sum(both * x, axis=0, keepdims=True))
        return out, jnp.concatenate(sums + [jnp.zeros((8 - KERNEL, 128), F32)], axis=0)

    def finish(i):
        g = go_ref[:, lanes(i)].astype(F32)
        x = x_ref[:, lanes(i)].astype(F32)
        sel_t = one_hot(sum_at, 2 * i)
        ys, parts_of, adds = [], [], []
        for s in range(2):
            u = 2 * i + s
            taps = taps_ref[s, :, lanes(i)]
            dt = dt_b[u]
            y = jnp.zeros((128, 128), F32)
            dms = []
            qt = jnp.zeros((128, 128), F32)
            qs, ends = [], []
            for d in range(2):
                c = 2 * s + d
                s_in, g_in = in_slots[d, u, 0], in_slots[1 - d, u, 1]
                step = u_ref[u, d].astype(F32)
                across = mm(bc_act[c, 1], s_in) * e_b[u, d] + yoff[u, d]
                y = y + across + diag[c] * step
                du = duo[u, d] + f_b[u, d] * mm(bc_act[c, 0], g_in)
                qs.append(g * across - step * du)
                du = du + diag[c] * g
                qt = qt + vals[u, d].astype(F32) * du
                adds.append((c, mm_nt(fu_ref[u, d], g_in), mm_nt(eg_ref[u, d], s_in)))
                leaving = own[d, u, 0] + decay_of(u, d) * s_in.astype(F32)
                ends.append(jnp.sum(leaving * g_in.astype(F32), axis=0, keepdims=True))
                dms.append((dt * du).astype(BF16).astype(F32) * slope[u, d])
            gi, gf = back(taps, dms, x)
            q = jnp.concatenate(qs + [qt] + ends + [jnp.zeros((6, 128), F32)], axis=0)
            parts_of.extend(split2(q))
            ys.append(y.astype(BF16).astype(F32))
            adds.append((s, gi, gf))
        totals = mm(jnp.concatenate(parts_of, axis=1), sel_t)
        for s in range(2):
            for c, db, dc in adds[3 * s : 3 * s + 2]:
                d_bc[c, 0] += db
                d_bc[c, 1] += dc
            _, gi, gf = adds[3 * s + 2]
            gi_ref[s, :, lanes(i)] = gi
            gf_ref[2 * i + s] = gf
        acc[...] += totals
        out_ref[:, lanes(i)] = (ys[0] + ys[1]).astype(BF16)

    groups = PAIRS // GROUP

    def first_part(t, carry):
        produce(t)
        send_first(t)
        return carry

    early = EARLY // GROUP

    def late_part(t, carry):
        for n in range(GROUP):
            values_of(GROUP * t + n)
        first_part(t, carry)
        for n in range(3):
            forward(3 * (t - early) + 3 + n)
        return carry

    before_second = 3 * (groups - early) + 3

    def second_part(i, carry):
        xt_ref[0, lanes(i)] = x_ref[:, lanes(i)].astype(F32).T.astype(BF16)
        xt_ref[1, lanes(i)] = xf_ref[:, lanes(i)].astype(F32).T.astype(BF16)
        w_rev[lanes(i)] = mm(flip, w_out[lanes(PAIRS - 1 - i)]).astype(BF16)
        inside(i)
        forward(before_second + i)
        return carry

    def idle(n, carry):
        forward(n)
        return carry

    before_third = before_second + PAIRS
    began = max(before_third, 2 + OFFSET + HOP * (count - 2))

    def third_part(i, carry):
        forward(began + 2 * i)
        forward(began + 2 * i + 1)
        arrive(i)
        finish(i)
        return carry

    lax.fori_loop(0, early, first_part, 0)
    lax.fori_loop(early, groups, late_part, 0)
    make_scores()
    lax.fori_loop(0, PAIRS, second_part, 0)
    if began > before_third:
        lax.fori_loop(before_third, began, idle, 0)
    lax.fori_loop(0, PAIRS, third_part, 0)

    halos = []
    for n, at in enumerate((pl.ds(0, WIDTH), pl.ds(WIDTH, 128))):
        halos.append(
            (
                push(
                    g_out.at[0, :, at], g_before.at[:, at],
                    g_sides.at[4 * n], g_sides.at[4 * n + 1], "seq", lax.rem(seq + 1, count),
                ),
                push(
                    g_out.at[1, :, at], g_after.at[:, at],
                    g_sides.at[4 * n + 2], g_sides.at[4 * n + 3], "seq",
                    lax.rem(seq + count - 1, count),
                ),
            )
        )

    def send_edges(at, halo):
        for side, start in ((0, EDGE + SPAN), (1, 0)):
            g_out[side, :, at] = jnp.concatenate(
                [gi_ref[s, start : start + EDGE, at] for s in range(2)], axis=0
            ).astype(BF16)

        @pl.when(seq < count - 1)
        def _():
            halo[0].start()

        @pl.when(seq > 0)
        def _():
            halo[1].start()

    send_edges(slice(0, WIDTH), halos[0])
    end_rows = acc[3 * SPAN : 3 * SPAN + 8]
    dl0 = acc[:SPAN] + jnp.where(iota(0) == SPAN - 1, end_rows[0:1], 0.0)
    dl1 = acc[SPAN : 2 * SPAN] + jnp.where(iota(0) == 0, end_rows[1:2], 0.0)
    both_t = jnp.concatenate(
        [ones_where(iota(0) <= iota(1)), ones_where(iota(0) >= iota(1))], axis=1
    )
    d_log = exact_left(both_t, jnp.concatenate([dl0, dl1], axis=0))
    rate = rates[0:1]
    dtx = dtx_ref[...]
    d_raw = (acc[2 * SPAN : 3 * SPAN] - rate * d_log) * sigmoid(dtx)
    line, lane = iota(0), iota(1)
    unswap = ones_where((line >= 32) & (line < 32 + HEADS) & (line + lane == 31 + HEADS))
    ddt = (
        jnp.where(iota(1) < HEADS, d_raw, 0.0).astype(BF16),
        mm(d_raw.astype(BF16), unswap).astype(BF16),
    )
    wides = []
    for s in range(2):
        taps = taps_ref[0, :, WIDTH:]
        dms = []
        for d in range(2):
            c = 2 * s + d
            on_diag = jnp.sum(d_diag[c], axis=1, keepdims=True)
            off = iota(0) > iota(1) if d == 0 else iota(0) < iota(1)
            ds = jnp.where(
                off, d_score[s], jnp.where(iota(0) == iota(1), on_diag, 0.0)
            ).astype(BF16)
            db = d_bc[c, 0] + mm_tn(ds, bc_act[c, 1])
            dc = d_bc[c, 1] + mm(ds, bc_act[c, 0])
            dms.append(jnp.concatenate([db, dc], axis=1).astype(BF16).astype(F32) * bc_slope[c])
        gi, gf = back(taps, dms, bcx_ref[s])
        gi_ref[s, :, WIDTH:] = gi
        gf_ref[UNITS + s] = gf
        edge = jnp.zeros((EDGE, 128), F32)
        wides.append(
            jnp.concatenate(
                [gi, jnp.concatenate([edge, ddt[s].astype(F32), edge], axis=0)], axis=1
            ).astype(BF16)
        )
    send_edges(slice(WIDTH, CHANNELS), halos[1])

    def weight_parts(zs):
        totals = []
        for z in zs:
            at = pl.ds(pl.multiple_of(z * rows, 16), rows)
            totals.append(mm(xt_ref[0, at], wides[0]) + mm(xt_ref[1, at], wides[1]))
        for z, total in zip(zs, totals):
            parts[z, :rows] = total[:, :128].astype(BF16)
            parts[z, rows:packed] = folded(total[:, 128:], fold).astype(BF16)

    order = list(range(1, chips)) + [0]
    theirs = [2 * lax.rem(chip + k, chips) + 1 - core for k in order]
    weight_parts(theirs)
    pairs = []
    for k, z in zip(order, theirs):
        copy = push(
            parts.at[z], pair_in.at[lax.div(z, 2)], p_send.at[k], p_recv.at[k], "zero", sibling
        )
        copy.start()
        pairs.append(copy)
    weight_parts([2 * lax.rem(chip + k, chips) + core for k in order])

    @pl.when(seq == 0)
    def _():
        g_before[...] = jnp.zeros_like(g_before)

    @pl.when(seq == count - 1)
    def _():
        g_after[...] = jnp.zeros_like(g_after)

    chunk = gathered.shape[0] // count
    here = pl.ds(pl.multiple_of(seq * chunk, 16), chunk)
    scatter = []
    for k in list(range(1, chips)) + [0]:
        there = lax.rem(chip + k, chips)
        pairs[k - 1].wait()
        pair_sum[there] = (
            parts[2 * there + core].astype(F32) + pair_in[there].astype(F32)
        ).astype(BF16)
        for n in range(count):
            if k or n:
                peer = lax.rem(seq + n, count)
                copy = pltpu.make_async_remote_copy(
                    src_ref=pair_sum.at[there, pl.ds(pl.multiple_of(peer * chunk, 16), chunk)],
                    dst_ref=part_in.at[k, n],
                    send_sem=zs.at[k, n],
                    recv_sem=zr.at[k, n],
                    device_id={"zero": 2 * there + core, "seq": peer},
                    device_id_type=MESH,
                )
                copy.start()
                scatter.append(copy)
    sums = jnp.concatenate(
        [
            jnp.sum(d_log * (-rate * softplus(dtx)), axis=0, keepdims=True),
            jnp.sum(d_raw, axis=0, keepdims=True),
            jnp.zeros((6, 128), F32),
        ],
        axis=0,
    )
    heads = jnp.where(iota(1, (8, 128)) < HEADS, sums, 0.0) + exact_right(sums, unswap)
    swapped = exact_right(
        jnp.concatenate([gf_ref[2 * (PAIRS - 1 - i) + 1] for i in range(PAIRS)], axis=0), flip
    )
    blocks = [
        (gf_ref[2 * i] + swapped[8 * i : 8 * i + 8])[:KERNEL] for i in range(PAIRS)
    ] + [(gf_ref[UNITS] + gf_ref[UNITS + 1])[:KERNEL]]
    head_hi = heads[:2].astype(BF16).astype(F32)
    small[...] = jnp.concatenate(blocks + [head_hi, heads[:2] - head_hi], axis=0).astype(BF16)
    first = []
    for k in range(1, shards):
        peer = lax.rem(zero + k, shards)
        copy = push(small, small_in.at[zero], ms.at[0, k], mr.at[0, k], "zero", peer)
        copy.start()
        first.append(copy)
    small_in[zero] = small[...]

    @pl.when(seq > 0)
    def _():
        for halo in halos:
            halo[0].wait_recv()

    @pl.when(seq < count - 1)
    def _():
        for halo in halos:
            halo[1].wait_recv()

    def settled(s, at):
        near = slice(EDGE * s, EDGE * s + EDGE)
        top = gi_ref[s, EDGE : 2 * EDGE, at] + g_before[:, at].astype(F32)[near]
        low = gi_ref[s, SPAN : SPAN + EDGE, at] + g_after[:, at].astype(F32)[near]
        return jnp.concatenate([top, gi_ref[s, 2 * EDGE : SPAN, at], low], axis=0).astype(BF16)

    gps = [
        jnp.concatenate([settled(s, slice(WIDTH, CHANNELS)), ddt[s]], axis=1) for s in range(2)
    ]

    def hidden_part(i):
        at = slice(i * 128, i * 128 + 128)
        a = (settled(0, at).astype(F32) + mm_nt(gps[0], w_out[at])).astype(BF16)
        b = (settled(1, at).astype(F32) + mm_nt(gps[1], w_rev[at])).astype(BF16)
        gh_ref[:, at] = (a.astype(F32) + b.astype(F32)).astype(BF16)

    for i in range(PAIRS // 2):
        hidden_part(i)
    for copy in first:
        copy.wait()
    summed = small_in[0].astype(F32)
    for z in range(1, shards):
        summed = summed + small_in[z].astype(F32)
    last = KERNEL * (PAIRS + 1)
    heads = summed[last : last + 2] + summed[last + 2 : last + 4]
    head_hi = heads.astype(BF16).astype(F32)
    small2[...] = jnp.concatenate([summed[:last], head_hi, heads - head_hi], axis=0).astype(BF16)
    second = []
    for k in range(1, count):
        peer = lax.rem(seq + k, count)
        copy = push(small2, small2_in.at[seq], ms.at[1, shards + k], mr.at[1, shards + k], "seq", peer)
        copy.start()
        second.append(copy)
    small2_in[seq] = small2[...]
    for copy in scatter:
        copy.wait()
    summed = parts[zero, here].astype(F32) + pair_in[chip, here].astype(F32)
    for k in range(chips):
        for n in range(count):
            if k or n:
                summed = summed + part_in[k, n].astype(F32)
    gathered[here] = summed.astype(BF16)
    third = []
    for k in range(1, count):
        peer = lax.rem(seq + k, count)
        copy = push(gathered.at[here], gathered.at[here], ss.at[1, k], sr.at[1, k], "seq", peer)
        copy.start()
        third.append(copy)
    for i in range(PAIRS // 2, PAIRS):
        hidden_part(i)
    for copy in second:
        copy.wait()
    summed = small2_in[0].astype(F32)
    for z in range(1, count):
        summed = summed + small2_in[z].astype(F32)
    total2[...] = summed
    for d, place, peer in chains:

        @pl.when(place < count - 1)
        def _():
            def sent(u, carry):
                copy_of(d, u, peer).wait_send()
                return carry

            lax.fori_loop(0, UNITS, sent, 0)

    @pl.when(seq < count - 1)
    def _():
        up.wait_send()

    @pl.when(seq > 0)
    def _():
        down.wait_send()

    @pl.when(seq < count - 1)
    def _():
        for halo in halos:
            halo[0].wait_send()

    @pl.when(seq > 0)
    def _():
        for halo in halos:
            halo[1].wait_send()

    for copy in third:
        copy.wait()
    full[...] = gathered[...]


def emit_kernel(
    shards, fold, out_ref, gh_ref, full, total, out_hbm, gh_hbm, gw_ref, gc_ref, gd_ref,
    wide, taps, sems,
):
    copies = [
        pltpu.make_async_copy(out_ref, out_hbm, sems.at[0]),
        pltpu.make_async_copy(gh_ref, gh_hbm, sems.at[1]),
    ]
    for copy in copies:
        copy.start()
    rows = WIDTH // shards
    fold_rows = rows // fold
    tail = full[rows : rows + fold_rows].astype(F32)
    wide[...] = jnp.zeros_like(wide)
    wide[:rows, :128] = full[:rows].astype(F32)
    for q in range(fold):
        moved = pltpu.roll(tail, 128 - 24 * q, 1) if q else tail
        wide[q * fold_rows : (q + 1) * fold_rows, 128:] = moved
    gw_ref[...] = wide[...].T[: gw_ref.shape[0], :rows]
    last = KERNEL * (PAIRS + 1)
    gd_ref[...] = total[last : last + 2, :HEADS] + total[last + 2 : last + 4, :HEADS]
    for i in range(PAIRS + 1):
        taps[:, i * 128 : i * 128 + 128] = total[KERNEL * i : KERNEL * i + KERNEL]
    zero = lax.axis_index("zero")
    width = gc_ref.shape[1]
    for z in range(shards):

        @pl.when(zero == z)
        def _():
            gc_ref[...] = taps[:, z * width : (z + 1) * width]

    for copy in copies:
        copy.wait()


def spec(space):
    return pl.BlockSpec(memory_space=space)


SQ4 = (4, 128, 128)
SQ2 = (2, 128, 128)
TILES = (UNITS, 2, 128, 128)


def per_device(hidden, grad_out, w_proj, conv_w, a_log, dt_bias):
    assert hidden.shape[:2] == (1, SPAN)
    count, shards = lax.axis_size("seq"), lax.axis_size("zero")
    chips = shards // 2
    rows, columns = w_proj.shape
    part = CHANNELS // shards
    fold = 5 if rows % 80 == 0 else 1
    packed = rows + rows // fold
    step = 16 * count
    padded = -(-packed // step) * step
    lines = 48
    wide_rows = -(-rows // 128) * 128
    pieces = (2, UNITS, 2, STATE, 128)
    edges = (2 * EDGE, CHANNELS)
    scratch = [
        ((SPAN, WIDTH), BF16), ((SPAN, WIDTH), BF16), ((columns, rows), BF16),
        ((KERNEL, part), BF16), ((256, wide_rows), F32),
        ((EXT, WIDTH), BF16), ((EXT, WIDTH), BF16), ((2, WIDTH, EXT), BF16),
        ((2, 8, CHANNELS), F32), ((WIDTH, 256), BF16), ((WIDTH, 256), BF16), ((WIDTH, 256), BF16),
        ((shards, packed, 128), BF16), ((8, part), F32), ((shards, 8, part), F32),
        ((2 * EDGE, WIDTH), BF16), ((2 * EDGE, WIDTH), BF16),
        (TILES, BF16), (TILES, F32), (TILES, BF16), (TILES, BF16), (TILES, BF16),
        (TILES, F32), (TILES, F32), (TILES, F32), (TILES, F32), ((UNITS, 128, 128), F32),
        (pieces, F32), (pieces, BF16), (pieces, BF16),
        ((256, 256), BF16), ((128, 256 * GROUP), BF16), ((512, 128), BF16),
        ((8, 128), F32), ((8, 128), F32), ((128, 128), F32), ((5 * 128, 128), BF16), ((256, 256), BF16),
        (SQ2, F32), (SQ2, F32), (SQ4, F32), ((4, 2, 128, STATE), BF16), (SQ4, BF16),
        (SQ4, F32), (SQ2, BF16), (SQ2, F32), (SQ4, F32), ((4, 2, 128, STATE), F32),
        ((3 * SPAN + 8, 128), F32),
        ((2, EXT, CHANNELS), F32), ((UNITS + 2, 8, 128), F32), ((2, EXT, 128), F32),
        ((2,) + edges, BF16), (edges, BF16), (edges, BF16),
        ((shards, padded, 128), BF16), ((chips, padded, 128), BF16),
        ((chips, padded, 128), BF16), ((chips, count, padded // count, 128), BF16),
        ((padded, 128), BF16),
        ((lines, 128), BF16), ((shards, lines, 128), BF16),
        ((lines, 128), BF16), ((count, lines, 128), BF16),
    ]
    sems = [
        (4,), (4,), (chips,), (chips,), (chips,), (chips,), (shards,), (shards,),
        (2, UNITS), (2, UNITS), (8,), (chips,), (chips,), (chips, count), (chips, count),
        (2, count), (2, count), (2, shards + count), (2, shards + count),
    ]
    anywhere = spec(pl.ANY)
    outs = pl.pallas_call(
        functools.partial(whole_kernel, shards, count, fold),
        out_shape=[
            jax.ShapeDtypeStruct((SPAN, WIDTH), BF16), jax.ShapeDtypeStruct((SPAN, WIDTH), BF16),
            jax.ShapeDtypeStruct((padded, 128), BF16), jax.ShapeDtypeStruct((lines, 128), F32),
        ],
        in_specs=[spec(pltpu.HBM)] * 4 + [spec(pltpu.VMEM)] * 2,
        scratch_shapes=[pltpu.VMEM(s, t) for s, t in scratch]
        + [pltpu.SemaphoreType.DMA(s) for s in sems],
        compiler_params=pltpu.CompilerParams(
            vmem_limit_bytes=54300 * 1024, collective_id=0, has_side_effects=True
        ),
    )(hidden[0], grad_out[0], w_proj.T, conv_w, a_log[None], dt_bias[None])
    output, grad_hidden, share_w, share_c, grad_heads = pl.pallas_call(
        functools.partial(emit_kernel, shards, fold),
        out_shape=[
            jax.ShapeDtypeStruct((SPAN, WIDTH), BF16), jax.ShapeDtypeStruct((SPAN, WIDTH), BF16),
            jax.ShapeDtypeStruct((columns, rows), F32),
            jax.ShapeDtypeStruct((KERNEL, part), F32), jax.ShapeDtypeStruct((2, HEADS), F32),
        ],
        out_specs=[anywhere] * 2 + [spec(pltpu.VMEM)] * 3,
        scratch_shapes=[
            pltpu.VMEM((wide_rows, 256), F32), pltpu.VMEM((KERNEL, CHANNELS), F32),
            pltpu.SemaphoreType.DMA((2,)),
        ],
        compiler_params=pltpu.CompilerParams(vmem_limit_bytes=8 * 1024 * 1024),
    )(*outs)
    return (output[None], grad_hidden[None], share_w.T, share_c, grad_heads)


def solution(mesh):
    return jax.shard_map(
        per_device,
        mesh=mesh,
        in_specs=(
            P(("grp", "zero"), "seq", None),
            P(("grp", "zero"), "seq", None),
            P("zero", None),
            P(None, "zero"),
            P(),
            P(),
        ),
        out_specs=(
            P(("grp", "zero"), "seq", None),
            P(("grp", "zero"), "seq", None),
            P(("grp", "zero"), None),
            P("grp", "zero"),
            P("grp", None),
        ),
        check_vma=False,
    )
```

```python
import functools
import jax
import jax.numpy as jnp
from jax import lax
from jax.experimental import pallas as pl
from jax.experimental.pallas import tpu as pltpu
from jax.sharding import PartitionSpec as P

WIDTH = 1280
STATE = 64
HEAD_DIM = 64
SPAN = 128
KERNEL = 4
HEADS = 20
PAIRS = WIDTH // 128
CHANNELS = WIDTH + 2 * STATE
EDGE = 8
EXT = SPAN + 2 * EDGE
F32 = jnp.float32
BF16 = jnp.bfloat16
UNITS = 2 * PAIRS
HOP = 6
OFFSET = 3
GROUP = 2
EARLY = 4


def mm(a, b):
    return jnp.dot(a, b, preferred_element_type=F32)


def mm_nt(a, b):
    return lax.dot_general(a, b, (((1,), (1,)), ((), ())), preferred_element_type=F32)


def mm_tn(a, b):
    return lax.dot_general(a, b, (((0,), (0,)), ((), ())), preferred_element_type=F32)


def exact(a, b):
    return jnp.dot(a, b, preferred_element_type=F32, precision=lax.Precision.HIGHEST)


def iota(dim, shape=(128, 128)):
    return lax.broadcasted_iota(jnp.int32, shape, dim)


def mirror(dtype=BF16):
    return jnp.where(iota(0) + iota(1) == 127, 1.0, 0.0).astype(dtype)


def softplus(x):
    return jnp.maximum(x, 0.0) + jnp.log1p(jnp.exp(-jnp.abs(x)))


def sigmoid(x):
    return 0.5 * jnp.tanh(0.5 * x) + 0.5


def shifted(x):
    back = [x[EDGE : EDGE + SPAN]]
    fore = [back[0]]
    for k in range(1, KERNEL):
        back.append(pltpu.roll(x, k, 0)[EDGE : EDGE + SPAN])
        fore.append(pltpu.roll(x, EXT - k, 0)[EDGE : EDGE + SPAN])
    return back, fore


def conv(taps, rows):
    out = taps[0:1] * rows[0]
    for k in range(1, KERNEL):
        out = out + taps[k : k + 1] * rows[k]
    return out


def lanes(i):
    return pl.ds(pl.multiple_of(i * 128, 128), 128)


MESH = pl.DeviceIdType.MESH


def greet_all(shards, count):
    barrier = pltpu.get_barrier_semaphore()
    seq, zero = lax.axis_index("seq"), lax.axis_index("zero")
    total = 0
    for n in range(count):
        for k in range(shards):
            if (k or n) and (n == 0 or k % 2 == 0):
                there = {"zero": lax.rem(zero + k, shards), "seq": lax.rem(seq + n, count)}
                pl.semaphore_signal(barrier, inc=1, device_id=there, device_id_type=MESH)
                total += 1
    return functools.partial(pl.semaphore_wait, barrier, total)


def push(src, dst, send, recv, axis, peer):
    return pltpu.make_async_remote_copy(
        src_ref=src,
        dst_ref=dst,
        send_sem=send,
        recv_sem=recv,
        device_id={axis: peer},
        device_id_type=MESH,
    )


def split2(x):
    hi = x.astype(BF16)
    return hi, (x - hi.astype(F32)).astype(BF16)


def split3(x):
    hi = x.astype(BF16)
    rest = x - hi.astype(F32)
    mid = rest.astype(BF16)
    return hi, mid, (rest - mid.astype(F32)).astype(BF16)


def exact_left(a, x):
    n = x.shape[1]
    out = mm(a, jnp.concatenate(split3(x), axis=1))
    return out[:, :n] + out[:, n : 2 * n] + out[:, 2 * n :]


def exact_right(x, b):
    n = x.shape[0]
    out = mm(jnp.concatenate(split3(x), axis=0), b)
    return out[:n] + out[n : 2 * n] + out[2 * n :]


def ones_where(keep):
    return jnp.where(keep, 1.0, 0.0).astype(BF16)


def one_hot(at_ref, head):
    at = at_ref[...]
    same = at == head.astype(F32).astype(BF16)
    return jnp.where(same, jnp.ones_like(at), jnp.zeros_like(at))


def strand_swap():
    k, lane = iota(0), iota(1)
    return ones_where((lane >= 32) & (lane < 32 + HEADS) & (k + lane == 31 + HEADS))


def folded(tail, fold):
    size = tail.shape[0] // fold
    out = tail[:size]
    for q in range(1, fold):
        out = out + pltpu.roll(tail[q * size : (q + 1) * size], 24 * q, 1)
    return out


def whole_kernel(
    shards, count, fold,
    hid_hbm, go_hbm, wt_hbm, c_hbm, alog_ref, bias_ref,
    out_ref, gh_ref, full, total2,
    hid_ref, go_ref, wt_in, c_in, wt_pad,
    x_ref, xf_ref, xt_ref, taps_ref, wp_ref, w_out, w_rev, w_slots, c_own, c_slots, before, after,
    vals, slope, u_ref, fu_ref, eg_ref, yoff, duo, e_b, f_b, dt_b,
    own, in_slots, out_slots,
    pick_at, sel_at, sum_at, heads_in, rates, dtx_ref, stack, split, within_t, score, diag, bc_act, bc_t, bc_slope, masks,
    d_score, d_diag, d_bc, acc,
    gi_ref, gf_ref, bcx_ref, g_out, g_before, g_after, parts, pair_in, pair_sum, part_in, gathered,
    small, small_in, small2, small2_in,
    local, sides, w_send, w_recv, f_send, f_recv, t_send, t_recv, c_send, c_recv,
    g_sides, p_send, p_recv, zs, zr, ss, sr, ms, mr,
):
    seq, zero = lax.axis_index("seq"), lax.axis_index("zero")
    core = lax.rem(zero, 2)
    chip = lax.div(zero, 2)
    chips = shards // 2
    sibling = zero + 1 - 2 * core
    rows = WIDTH // shards
    fold_rows = rows // fold
    packed = rows + fold_rows
    greeted = greet_all(shards, count)
    loads = [
        pltpu.make_async_copy(src, dst, local.at[n])
        for n, (src, dst) in enumerate(
            ((c_hbm, c_in), (wt_hbm, wt_in), (hid_hbm, hid_ref), (go_hbm, go_ref))
        )
    ]
    for load in loads:
        load.start()
    c_own[...] = jnp.zeros_like(c_own)
    wt_pad[...] = jnp.zeros_like(wt_pad)
    loads[0].wait()
    c_own[:KERNEL] = c_in[...].astype(F32)
    loads[1].wait()
    wt_pad[: wt_in.shape[0], :rows] = wt_in[...].astype(F32)
    w_own = wt_pad[...].T
    w_slots[zero, :rows] = w_own[:rows, :128].astype(BF16)
    w_slots[zero, rows:] = folded(w_own[:rows, 128:], fold).astype(BF16)
    greeted()
    tap_copies = []
    for k in range(1, shards):
        peer = lax.rem(zero + k, shards)
        copy = push(c_own, c_slots.at[zero], t_send.at[k], t_recv.at[k], "zero", peer)
        copy.start()
        tap_copies.append(copy)
    loads[2].wait()
    up = push(
        hid_ref.at[pl.ds(SPAN - 2 * EDGE, 2 * EDGE)], before, sides.at[0], sides.at[1], "seq",
        lax.rem(seq + 1, count),
    )
    down = push(
        hid_ref.at[pl.ds(0, 2 * EDGE)], after, sides.at[2], sides.at[3], "seq",
        lax.rem(seq + count - 1, count),
    )

    @pl.when(seq < count - 1)
    def _():
        up.start()

    @pl.when(seq > 0)
    def _():
        down.start()

    w_copies = []
    for k in range(chips):
        peer = lax.rem(zero + 2 * k, shards) if k else sibling
        copy = push(w_slots.at[zero], w_slots.at[zero], w_send.at[k], w_recv.at[k], "zero", peer)
        copy.start()
        w_copies.append(copy)
    c_slots[zero] = c_own[...]
    w_out[:, 128:] = jnp.zeros((WIDTH, 128), BF16)
    x_ref[EDGE : EDGE + SPAN] = hid_ref[...]
    flip = mirror()
    swap = strand_swap()
    masks[0] = ones_where(iota(0) > iota(1))
    masks[1] = ones_where(iota(0) < iota(1))
    if parts.shape[1] > packed:
        spare = (shards, parts.shape[1] - packed, 128)
        parts[:, packed:] = jnp.zeros(spare, BF16)
    square = (256, 256)
    line, lane = iota(0, square), iota(1, square)
    pick_at[...] = jnp.where(
        line < 192, lax.rem(line, 64) - jnp.where(lane >= 128, 1, 0), -2
    ).astype(F32).astype(BF16)
    wide_shape = (128, 256 * GROUP)
    line, lane = iota(0, wide_shape), iota(1, wide_shape)
    sel_at[...] = (
        lax.rem(line, 64)
        - 2 * lax.div(lane, 256)
        - jnp.where(lax.rem(lane, 256) >= 128, 32, 0)
        - jnp.where(lax.rem(lane, 128) >= HEAD_DIM, 1, 0)
    ).astype(F32).astype(BF16)
    tall = (512, 128)
    line, lane = iota(0, tall), iota(1, tall)
    sum_at[...] = (
        lane
        - jnp.where(line >= 256, 32, 0)
        - jnp.where(lax.rem(line, 128) >= HEAD_DIM, 1, 0)
    ).astype(F32).astype(BF16)
    d_score[...] = jnp.zeros_like(d_score)
    d_diag[...] = jnp.zeros_like(d_diag)
    d_bc[...] = jnp.zeros_like(d_bc)
    acc[...] = jnp.zeros_like(acc)

    @pl.when(seq == 0)
    def _():
        x_ref[:EDGE] = jnp.zeros((EDGE, WIDTH), BF16)
        in_slots[0] = jnp.zeros(in_slots.shape[1:], BF16)

    @pl.when(seq > 0)
    def _():
        up.wait_recv()
        x_ref[:EDGE] = before[EDGE:]

    @pl.when(seq == count - 1)
    def _():
        x_ref[EDGE + SPAN :] = jnp.zeros((EDGE, WIDTH), BF16)
        in_slots[1] = jnp.zeros(in_slots.shape[1:], BF16)

    @pl.when(seq < count - 1)
    def _():
        down.wait_recv()
        x_ref[EDGE + SPAN :] = after[:EDGE]

    for copy in tap_copies:
        copy.wait()
    part = c_own.shape[1]
    for z in range(shards):
        taps_ref[0, :, z * part : (z + 1) * part] = c_slots[z]
    for b in range(PAIRS):
        taps_ref[1, :, b * 128 : (b + 1) * 128] = mm(
            taps_ref[0, :, (PAIRS - 1 - b) * 128 : (PAIRS - b) * 128].astype(BF16), flip
        )

    def values_of(i):
        rows = shifted(x_ref[:, lanes(i)].astype(F32))
        for s in range(2):
            taps = taps_ref[s, :, lanes(i)]
            for d in range(2):
                mixed = conv(taps, rows[d])
                sig = sigmoid(mixed)
                act = mixed * sig
                vals[2 * i + s, d] = act.astype(BF16)
                slope[2 * i + s, d] = sig + act * (1.0 - sig)

    def values_step(i, carry):
        values_of(i)
        return carry

    for b in range(PAIRS):
        xf_ref[:, (PAIRS - 1 - b) * 128 : (PAIRS - b) * 128] = mm(
            x_ref[:, b * 128 : (b + 1) * 128], flip
        ).astype(BF16)
    lax.fori_loop(0, EARLY, values_step, 0)

    for copy in w_copies:
        copy.wait()
    forwards = []
    for k in range(1, chips):
        slot_of = w_slots.at[lax.rem(zero + shards - 2 * k, shards)]
        copy = push(slot_of, slot_of, f_send.at[k], f_recv.at[k], "zero", sibling)
        copy.start()
        forwards.append(copy)

    def unpack(z):
        at = pl.multiple_of(z * rows, 16)
        w_out[pl.ds(at, rows), :128] = w_slots[z, :rows]
        tail = w_slots[z, rows:].astype(F32)
        for q in range(fold):
            moved = pltpu.roll(tail, 128 - 24 * q, 1) if q else tail
            w_out[pl.ds(at + q * fold_rows, fold_rows), 128:] = jnp.where(
                iota(1, (fold_rows, 128)) < HEADS, moved, 0.0
            ).astype(BF16)

    for k in range(chips):
        unpack(lax.rem(zero + shards - 2 * k, shards))
    unpack(sibling)
    for copy in forwards:
        copy.wait()
    for k in range(1, chips):
        unpack(lax.rem(sibling + shards - 2 * k, shards))
    wp_ref[:, :128] = w_out[:, :128]
    wp_ref[:, 128:] = mm(w_out[:, 128:], swap).astype(BF16)
    proj = (mm(x_ref[...], w_out[...]), mm(xf_ref[...], wp_ref[...]))
    loads[3].wait()
    heads_in[...] = jnp.zeros_like(heads_in)
    heads_in[0:1, :HEADS] = alog_ref[...]
    heads_in[1:2, :HEADS] = bias_ref[...]
    place = heads_in[...] + exact_right(heads_in[...], swap)
    rate = jnp.exp(place[0:1])
    rates[0:1] = rate
    dtx = (proj[0] + proj[1])[EDGE : EDGE + SPAN, 128:] + place[1:2]
    dtx_ref[...] = dtx
    delta = softplus(dtx)
    both = jnp.concatenate(
        [ones_where(iota(0) >= iota(1)), ones_where(iota(0) <= iota(1))], axis=0
    )
    within = exact_left(both, -rate * delta)
    ends = jnp.concatenate(
        [
            jnp.broadcast_to(within[SPAN - 1 : SPAN], (SPAN, 128)),
            jnp.broadcast_to(within[SPAN : SPAN + 1], (SPAN, 128)),
        ],
        axis=0,
    )
    spread = jnp.concatenate([jnp.exp(within), jnp.exp(ends - within), delta], axis=0)
    hi, lo = split2(spread)
    wide_low = iota(1, spread.shape) < 64
    stack[...] = jnp.where(
        wide_low, hi.astype(F32), pltpu.roll(lo.astype(F32), 64, 1)
    ).astype(BF16)
    hi, mid, lo = split3(within)
    low_two = iota(1, (256, 128)) < 64
    split[:, :128] = jnp.where(
        low_two, hi.astype(F32), pltpu.roll(mid.astype(F32), 64, 1)
    ).astype(BF16)
    split[:, 128:] = jnp.where(low_two, lo.astype(F32), 0.0).astype(BF16)
    for d in range(2):
        within_t[d] = within[d * 128 : d * 128 + 128].T
    for s in range(2):
        bcx_ref[s] = proj[s][:, :128].astype(BF16).astype(F32)
        bcx = shifted(bcx_ref[s])
        for d in range(2):
            c = 2 * s + d
            mixed = conv(taps_ref[0, :, WIDTH:], bcx[d])
            sig = sigmoid(mixed)
            wide = mixed * sig
            act = wide.astype(BF16)
            bc_slope[c] = sig + wide * (1.0 - sig)
            bc_act[c, 0] = act[:, :STATE]
            bc_act[c, 1] = act[:, STATE:]
            act_t = act.astype(F32).T.astype(BF16)
            bc_t[c] = act_t

    def make_scores():
        for s in range(2):
            scores = []
            for d in range(2):
                c = 2 * s + d
                scores.append(mm(bc_act[c, 1], bc_t[c, :STATE]))
                own_diag = jnp.sum(
                    jnp.where(iota(0) == iota(1), scores[d], 0.0), axis=1, keepdims=True
                )
                diag[c] = jnp.broadcast_to(own_diag, (128, 128))
            score[s] = jnp.where(
                iota(0) > iota(1), scores[0], jnp.where(iota(0) < iota(1), scores[1], 0.0)
            )

    def produce(t):
        all_wide = mm(stack[...], one_hot(sel_at, 2 * GROUP * t))
        for n in range(GROUP):
            g = go_ref[:, lanes(GROUP * t + n)].astype(F32)
            for s in range(2):
                u = 2 * GROUP * t + 2 * n + s
                at = 256 * n + 128 * s
                wide = all_wide[:, at : at + 128]
                dt = wide[512:]
                dt_b[u] = dt
                for d in range(2):
                    e, f = wide[128 * d : 128 * d + 128], wide[256 + 128 * d : 384 + 128 * d]
                    e_b[u, d] = e
                    f_b[u, d] = f
                    step = (vals[u, d].astype(F32) * dt).astype(BF16)
                    u_ref[u, d] = step
                    fu = (step.astype(F32) * f).astype(BF16)
                    fu_ref[u, d] = fu
                    eg = (e * g).astype(BF16)
                    eg_ref[u, d] = eg
                    own[d, u, 0] = mm(bc_t[2 * s + d, :STATE], fu)
                    own[1 - d, u, 1] = mm(bc_t[2 * s + d, STATE:], eg)

    def decay_of(u, d):
        at = SPAN - 1 if d == 0 else 0
        return e_b[u, d, at : at + 1]

    chains = ((0, seq, seq + 1), (1, count - 1 - seq, seq - 1))

    def copy_of(d, u, peer):
        return push(
            out_slots.at[d, u], in_slots.at[d, u], c_send.at[d, u], c_recv.at[d, u], "seq", peer
        )

    def send_first(t):
        for d, place, peer in chains:

            @pl.when(place == 0)
            def _():
                for n in range(2 * GROUP):
                    u = 2 * GROUP * t + n
                    out_slots[d, u] = own[d, u].astype(BF16)
                    copy_of(d, u, peer).start()

    def forward(n):
        for d, place, peer in chains:
            u = n - OFFSET - HOP * place

            @pl.when((place > 0) & (place < count - 1) & (u >= 0) & (u < UNITS))
            def _():
                copy_of(d, u, seq).wait_recv()
                for q in range(2):
                    dec = decay_of(u, d if q == 0 else 1 - d)
                    out_slots[d, u, q] = (
                        own[d, u, q] + dec * in_slots[d, u, q].astype(F32)
                    ).astype(BF16)
                copy_of(d, u, peer).start()

    def arrive(i):
        for d, place, peer in chains:

            @pl.when(place == count - 1)
            def _():
                for s in range(2):
                    copy_of(d, 2 * i + s, seq).wait_recv()

    def inside(i):
        lower = iota(0) >= iota(1)
        low = iota(1) < HEAD_DIM
        go = go_ref[:, lanes(i)]
        g = go.astype(F32)
        none = jnp.zeros((128, 128), BF16)
        g_two = jnp.concatenate([jnp.where(low, go, none), jnp.where(low, none, go)], axis=0)
        kept_ins = []
        for s in range(2):
            u = 2 * i + s
            head = 32 * s + 2 * i
            cols = mm(split[...], one_hot(pick_at, head))
            steps = jnp.concatenate([u_ref[u, 0], u_ref[u, 1]], axis=0)
            dw = mm_nt(g_two, steps)
            sc = score[s]
            ds = jnp.zeros((128, 128), F32)
            below, above = [], []
            for r in range(2):
                at = slice(128 * r, 128 * r + 128)
                gap = jnp.where(
                    lower,
                    cols[:128, at] - within_t[0, pl.ds(head + r, 1), :],
                    cols[128:, at] - within_t[1, pl.ds(head + r, 1), :],
                )
                decay = jnp.exp(gap)
                w = (sc * decay).astype(BF16)
                below.append(w * masks[0])
                above.append(w * masks[1])
                ds = ds + decay * jnp.where(lower, dw[at, :128], dw[at, 128:])
            for d, ws in enumerate((below, above)):
                step = steps[128 * d : 128 * d + 128]
                y_two = mm(jnp.concatenate(ws, axis=0), step)
                kept_ins.append(
                    (
                        jnp.where(low, y_two[:128], y_two[128:]),
                        jnp.where(low, mm_tn(ws[0], go), mm_tn(ws[1], go)),
                        g * step.astype(F32),
                    )
                )
            kept_ins.append(ds)
        for s in range(2):
            for d in range(2):
                y_two, du, on_diag = kept_ins[3 * s + d]
                yoff[2 * i + s, d] = y_two
                duo[2 * i + s, d] = du
                d_diag[2 * s + d] += on_diag
            d_score[s] += kept_ins[3 * s + 2]

    def back(taps, dms, x):
        zero_rows = jnp.zeros((EDGE, 128), F32)
        wides = [jnp.concatenate([zero_rows, dm, zero_rows], axis=0) for dm in dms]
        both = wides[0] + wides[1]
        out = taps[0:1] * both
        sums = [jnp.sum(both * x, axis=0, keepdims=True)]
        for k in range(1, KERNEL):
            both = pltpu.roll(wides[0], EXT - k, 0) + pltpu.roll(wides[1], k, 0)
            out = out + taps[k : k + 1] * both
            sums.append(jnp.sum(both * x, axis=0, keepdims=True))
        return out, jnp.concatenate(sums + [jnp.zeros((8 - KERNEL, 128), F32)], axis=0)

    def finish(i):
        g = go_ref[:, lanes(i)].astype(F32)
        x = x_ref[:, lanes(i)].astype(F32)
        sel_t = one_hot(sum_at, 2 * i)
        ys, parts_of, adds = [], [], []
        for s in range(2):
            u = 2 * i + s
            taps = taps_ref[s, :, lanes(i)]
            dt = dt_b[u]
            y = jnp.zeros((128, 128), F32)
            dms = []
            qt = jnp.zeros((128, 128), F32)
            qs, ends = [], []
            for d in range(2):
                c = 2 * s + d
                s_in, g_in = in_slots[d, u, 0], in_slots[1 - d, u, 1]
                step = u_ref[u, d].astype(F32)
                across = mm(bc_act[c, 1], s_in) * e_b[u, d] + yoff[u, d]
                y = y + across + diag[c] * step
                du = duo[u, d] + f_b[u, d] * mm(bc_act[c, 0], g_in)
                qs.append(g * across - step * du)
                du = du + diag[c] * g
                qt = qt + vals[u, d].astype(F32) * du
                adds.append((c, mm_nt(fu_ref[u, d], g_in), mm_nt(eg_ref[u, d], s_in)))
                leaving = own[d, u, 0] + decay_of(u, d) * s_in.astype(F32)
                ends.append(jnp.sum(leaving * g_in.astype(F32), axis=0, keepdims=True))
                dms.append((dt * du).astype(BF16).astype(F32) * slope[u, d])
            gi, gf = back(taps, dms, x)
            q = jnp.concatenate(qs + [qt] + ends + [jnp.zeros((6, 128), F32)], axis=0)
            parts_of.extend(split2(q))
            ys.append(y.astype(BF16).astype(F32))
            adds.append((s, gi, gf))
        totals = mm(jnp.concatenate(parts_of, axis=1), sel_t)
        for s in range(2):
            for c, db, dc in adds[3 * s : 3 * s + 2]:
                d_bc[c, 0] += db
                d_bc[c, 1] += dc
            _, gi, gf = adds[3 * s + 2]
            gi_ref[s, :, lanes(i)] = gi
            gf_ref[2 * i + s] = gf
        acc[...] += totals
        out_ref[:, lanes(i)] = (ys[0] + ys[1]).astype(BF16)

    groups = PAIRS // GROUP

    def first_part(t, carry):
        produce(t)
        send_first(t)
        return carry

    early = EARLY // GROUP

    def late_part(t, carry):
        for n in range(GROUP):
            values_of(GROUP * t + n)
        first_part(t, carry)
        for n in range(3):
            forward(3 * (t - early) + 3 + n)
        return carry

    before_second = 3 * (groups - early) + 3

    def second_part(i, carry):
        for n in range(GROUP):
            b = GROUP * i + n
            xt_ref[0, lanes(b)] = x_ref[:, lanes(b)].astype(F32).T.astype(BF16)
            xt_ref[1, lanes(b)] = xf_ref[:, lanes(b)].astype(F32).T.astype(BF16)
            w_rev[lanes(b)] = mm(flip, w_out[lanes(PAIRS - 1 - b)]).astype(BF16)
            inside(b)
        for n in range(GROUP):
            forward(before_second + GROUP * i + n)
        return carry

    def idle(n, carry):
        forward(n)
        return carry

    before_third = before_second + PAIRS
    began = max(before_third, 2 + OFFSET + HOP * (count - 2))

    def third_part(i, carry):
        forward(began + 2 * i)
        forward(began + 2 * i + 1)
        arrive(i)
        finish(i)
        return carry

    lax.fori_loop(0, early, first_part, 0)
    lax.fori_loop(early, groups, late_part, 0)
    make_scores()
    lax.fori_loop(0, groups, second_part, 0)
    if began > before_third:
        lax.fori_loop(before_third, began, idle, 0)
    lax.fori_loop(0, PAIRS, third_part, 0)

    halos = []
    for n, at in enumerate((pl.ds(0, WIDTH), pl.ds(WIDTH, 128))):
        halos.append(
            (
                push(
                    g_out.at[0, :, at], g_before.at[:, at],
                    g_sides.at[4 * n], g_sides.at[4 * n + 1], "seq", lax.rem(seq + 1, count),
                ),
                push(
                    g_out.at[1, :, at], g_after.at[:, at],
                    g_sides.at[4 * n + 2], g_sides.at[4 * n + 3], "seq",
                    lax.rem(seq + count - 1, count),
                ),
            )
        )

    def send_edges(at, halo):
        for side, start in ((0, EDGE + SPAN), (1, 0)):
            g_out[side, :, at] = jnp.concatenate(
                [gi_ref[s, start : start + EDGE, at] for s in range(2)], axis=0
            ).astype(BF16)

        @pl.when(seq < count - 1)
        def _():
            halo[0].start()

        @pl.when(seq > 0)
        def _():
            halo[1].start()

    send_edges(slice(0, WIDTH), halos[0])
    end_rows = acc[3 * SPAN : 3 * SPAN + 8]
    dl0 = acc[:SPAN] + jnp.where(iota(0) == SPAN - 1, end_rows[0:1], 0.0)
    dl1 = acc[SPAN : 2 * SPAN] + jnp.where(iota(0) == 0, end_rows[1:2], 0.0)
    both_t = jnp.concatenate(
        [ones_where(iota(0) <= iota(1)), ones_where(iota(0) >= iota(1))], axis=1
    )
    d_log = exact_left(both_t, jnp.concatenate([dl0, dl1], axis=0))
    rate = rates[0:1]
    dtx = dtx_ref[...]
    d_raw = (acc[2 * SPAN : 3 * SPAN] - rate * d_log) * sigmoid(dtx)
    line, lane = iota(0), iota(1)
    unswap = ones_where((line >= 32) & (line < 32 + HEADS) & (line + lane == 31 + HEADS))
    ddt = (
        jnp.where(iota(1) < HEADS, d_raw, 0.0).astype(BF16),
        mm(d_raw.astype(BF16), unswap).astype(BF16),
    )
    wides = []
    for s in range(2):
        taps = taps_ref[0, :, WIDTH:]
        dms = []
        for d in range(2):
            c = 2 * s + d
            on_diag = jnp.sum(d_diag[c], axis=1, keepdims=True)
            off = iota(0) > iota(1) if d == 0 else iota(0) < iota(1)
            ds = jnp.where(
                off, d_score[s], jnp.where(iota(0) == iota(1), on_diag, 0.0)
            ).astype(BF16)
            db = d_bc[c, 0] + mm_tn(ds, bc_act[c, 1])
            dc = d_bc[c, 1] + mm(ds, bc_act[c, 0])
            dms.append(jnp.concatenate([db, dc], axis=1).astype(BF16).astype(F32) * bc_slope[c])
        gi, gf = back(taps, dms, bcx_ref[s])
        gi_ref[s, :, WIDTH:] = gi
        gf_ref[UNITS + s] = gf
        edge = jnp.zeros((EDGE, 128), F32)
        wides.append(
            jnp.concatenate(
                [gi, jnp.concatenate([edge, ddt[s].astype(F32), edge], axis=0)], axis=1
            ).astype(BF16)
        )
    send_edges(slice(WIDTH, CHANNELS), halos[1])

    def weight_parts(zs):
        totals = []
        for z in zs:
            at = pl.ds(pl.multiple_of(z * rows, 16), rows)
            totals.append(mm(xt_ref[0, at], wides[0]) + mm(xt_ref[1, at], wides[1]))
        for z, total in zip(zs, totals):
            parts[z, :rows] = total[:, :128].astype(BF16)
            parts[z, rows:packed] = folded(total[:, 128:], fold).astype(BF16)

    order = list(range(1, chips)) + [0]
    theirs = [2 * lax.rem(chip + k, chips) + 1 - core for k in order]
    weight_parts(theirs)
    pairs = []
    for k, z in zip(order, theirs):
        copy = push(
            parts.at[z], pair_in.at[lax.div(z, 2)], p_send.at[k], p_recv.at[k], "zero", sibling
        )
        copy.start()
        pairs.append(copy)
    weight_parts([2 * lax.rem(chip + k, chips) + core for k in order])

    @pl.when(seq == 0)
    def _():
        g_before[...] = jnp.zeros_like(g_before)

    @pl.when(seq == count - 1)
    def _():
        g_after[...] = jnp.zeros_like(g_after)

    chunk = gathered.shape[0] // count
    here = pl.ds(pl.multiple_of(seq * chunk, 16), chunk)
    scatter = []
    for k in list(range(1, chips)) + [0]:
        there = lax.rem(chip + k, chips)
        pairs[k - 1].wait()
        pair_sum[there] = (
            parts[2 * there + core].astype(F32) + pair_in[there].astype(F32)
        ).astype(BF16)
        for n in range(count):
            if k or n:
                peer = lax.rem(seq + n, count)
                copy = pltpu.make_async_remote_copy(
                    src_ref=pair_sum.at[there, pl.ds(pl.multiple_of(peer * chunk, 16), chunk)],
                    dst_ref=part_in.at[k, n],
                    send_sem=zs.at[k, n],
                    recv_sem=zr.at[k, n],
                    device_id={"zero": 2 * there + core, "seq": peer},
                    device_id_type=MESH,
                )
                copy.start()
                scatter.append(copy)
    sums = jnp.concatenate(
        [
            jnp.sum(d_log * (-rate * softplus(dtx)), axis=0, keepdims=True),
            jnp.sum(d_raw, axis=0, keepdims=True),
            jnp.zeros((6, 128), F32),
        ],
        axis=0,
    )
    heads = jnp.where(iota(1, (8, 128)) < HEADS, sums, 0.0) + exact_right(sums, unswap)
    swapped = exact_right(
        jnp.concatenate([gf_ref[2 * (PAIRS - 1 - i) + 1] for i in range(PAIRS)], axis=0), flip
    )
    blocks = [
        (gf_ref[2 * i] + swapped[8 * i : 8 * i + 8])[:KERNEL] for i in range(PAIRS)
    ] + [(gf_ref[UNITS] + gf_ref[UNITS + 1])[:KERNEL]]
    head_hi = heads[:2].astype(BF16).astype(F32)
    small[...] = jnp.concatenate(blocks + [head_hi, heads[:2] - head_hi], axis=0).astype(BF16)
    first = []
    for k in range(1, shards):
        peer = lax.rem(zero + k, shards)
        copy = push(small, small_in.at[zero], ms.at[0, k], mr.at[0, k], "zero", peer)
        copy.start()
        first.append(copy)
    small_in[zero] = small[...]

    @pl.when(seq > 0)
    def _():
        for halo in halos:
            halo[0].wait_recv()

    @pl.when(seq < count - 1)
    def _():
        for halo in halos:
            halo[1].wait_recv()

    def settled(s, at):
        near = slice(EDGE * s, EDGE * s + EDGE)
        top = gi_ref[s, EDGE : 2 * EDGE, at] + g_before[:, at].astype(F32)[near]
        low = gi_ref[s, SPAN : SPAN + EDGE, at] + g_after[:, at].astype(F32)[near]
        return jnp.concatenate([top, gi_ref[s, 2 * EDGE : SPAN, at], low], axis=0).astype(BF16)

    gps = [
        jnp.concatenate([settled(s, slice(WIDTH, CHANNELS)), ddt[s]], axis=1) for s in range(2)
    ]

    def hidden_part(i):
        at = slice(i * 128, i * 128 + 128)
        a = (settled(0, at).astype(F32) + mm_nt(gps[0], w_out[at])).astype(BF16)
        b = (settled(1, at).astype(F32) + mm_nt(gps[1], w_rev[at])).astype(BF16)
        gh_ref[:, at] = (a.astype(F32) + b.astype(F32)).astype(BF16)

    for i in range(PAIRS // 2):
        hidden_part(i)
    for copy in first:
        copy.wait()
    summed = small_in[0].astype(F32)
    for z in range(1, shards):
        summed = summed + small_in[z].astype(F32)
    last = KERNEL * (PAIRS + 1)
    heads = summed[last : last + 2] + summed[last + 2 : last + 4]
    head_hi = heads.astype(BF16).astype(F32)
    small2[...] = jnp.concatenate([summed[:last], head_hi, heads - head_hi], axis=0).astype(BF16)
    second = []
    for k in range(1, count):
        peer = lax.rem(seq + k, count)
        copy = push(small2, small2_in.at[seq], ms.at[1, shards + k], mr.at[1, shards + k], "seq", peer)
        copy.start()
        second.append(copy)
    small2_in[seq] = small2[...]
    for copy in scatter:
        copy.wait()
    summed = parts[zero, here].astype(F32) + pair_in[chip, here].astype(F32)
    for k in range(chips):
        for n in range(count):
            if k or n:
                summed = summed + part_in[k, n].astype(F32)
    gathered[here] = summed.astype(BF16)
    third = []
    for k in range(1, count):
        peer = lax.rem(seq + k, count)
        copy = push(gathered.at[here], gathered.at[here], ss.at[1, k], sr.at[1, k], "seq", peer)
        copy.start()
        third.append(copy)
    for i in range(PAIRS // 2, PAIRS):
        hidden_part(i)
    for copy in second:
        copy.wait()
    summed = small2_in[0].astype(F32)
    for z in range(1, count):
        summed = summed + small2_in[z].astype(F32)
    total2[...] = summed
    for d, place, peer in chains:

        @pl.when(place < count - 1)
        def _():
            def sent(u, carry):
                copy_of(d, u, peer).wait_send()
                return carry

            lax.fori_loop(0, UNITS, sent, 0)

    @pl.when(seq < count - 1)
    def _():
        up.wait_send()

    @pl.when(seq > 0)
    def _():
        down.wait_send()

    @pl.when(seq < count - 1)
    def _():
        for halo in halos:
            halo[0].wait_send()

    @pl.when(seq > 0)
    def _():
        for halo in halos:
            halo[1].wait_send()

    for copy in third:
        copy.wait()
    full[...] = gathered[...]


def emit_kernel(
    shards, fold, out_ref, gh_ref, full, total, out_hbm, gh_hbm, gw_ref, gc_ref, gd_ref,
    wide, taps, sems,
):
    copies = [
        pltpu.make_async_copy(out_ref, out_hbm, sems.at[0]),
        pltpu.make_async_copy(gh_ref, gh_hbm, sems.at[1]),
    ]
    for copy in copies:
        copy.start()
    rows = WIDTH // shards
    fold_rows = rows // fold
    tail = full[rows : rows + fold_rows].astype(F32)
    wide[...] = jnp.zeros_like(wide)
    wide[:rows, :128] = full[:rows].astype(F32)
    for q in range(fold):
        moved = pltpu.roll(tail, 128 - 24 * q, 1) if q else tail
        wide[q * fold_rows : (q + 1) * fold_rows, 128:] = moved
    gw_ref[...] = wide[...].T[: gw_ref.shape[0], :rows]
    last = KERNEL * (PAIRS + 1)
    gd_ref[...] = total[last : last + 2, :HEADS] + total[last + 2 : last + 4, :HEADS]
    for i in range(PAIRS + 1):
        taps[:, i * 128 : i * 128 + 128] = total[KERNEL * i : KERNEL * i + KERNEL]
    zero = lax.axis_index("zero")
    width = gc_ref.shape[1]
    for z in range(shards):

        @pl.when(zero == z)
        def _():
            gc_ref[...] = taps[:, z * width : (z + 1) * width]

    for copy in copies:
        copy.wait()


def spec(space):
    return pl.BlockSpec(memory_space=space)


SQ4 = (4, 128, 128)
SQ2 = (2, 128, 128)
TILES = (UNITS, 2, 128, 128)


def per_device(hidden, grad_out, w_proj, conv_w, a_log, dt_bias):
    assert hidden.shape[:2] == (1, SPAN)
    count, shards = lax.axis_size("seq"), lax.axis_size("zero")
    chips = shards // 2
    rows, columns = w_proj.shape
    part = CHANNELS // shards
    fold = 5 if rows % 80 == 0 else 1
    packed = rows + rows // fold
    step = 16 * count
    padded = -(-packed // step) * step
    lines = 48
    wide_rows = -(-rows // 128) * 128
    pieces = (2, UNITS, 2, STATE, 128)
    edges = (2 * EDGE, CHANNELS)
    scratch = [
        ((SPAN, WIDTH), BF16), ((SPAN, WIDTH), BF16), ((columns, rows), BF16),
        ((KERNEL, part), BF16), ((256, wide_rows), F32),
        ((EXT, WIDTH), BF16), ((EXT, WIDTH), BF16), ((2, WIDTH, EXT), BF16),
        ((2, 8, CHANNELS), F32), ((WIDTH, 256), BF16), ((WIDTH, 256), BF16), ((WIDTH, 256), BF16),
        ((shards, packed, 128), BF16), ((8, part), F32), ((shards, 8, part), F32),
        ((2 * EDGE, WIDTH), BF16), ((2 * EDGE, WIDTH), BF16),
        (TILES, BF16), (TILES, F32), (TILES, BF16), (TILES, BF16), (TILES, BF16),
        (TILES, F32), (TILES, F32), (TILES, F32), (TILES, F32), ((UNITS, 128, 128), F32),
        (pieces, F32), (pieces, BF16), (pieces, BF16),
        ((256, 256), BF16), ((128, 256 * GROUP), BF16), ((512, 128), BF16),
        ((8, 128), F32), ((8, 128), F32), ((128, 128), F32), ((5 * 128, 128), BF16), ((256, 256), BF16),
        (SQ2, F32), (SQ2, F32), (SQ4, F32), ((4, 2, 128, STATE), BF16), (SQ4, BF16),
        (SQ4, F32), (SQ2, BF16), (SQ2, F32), (SQ4, F32), ((4, 2, 128, STATE), F32),
        ((3 * SPAN + 8, 128), F32),
        ((2, EXT, CHANNELS), F32), ((UNITS + 2, 8, 128), F32), ((2, EXT, 128), F32),
        ((2,) + edges, BF16), (edges, BF16), (edges, BF16),
        ((shards, padded, 128), BF16), ((chips, padded, 128), BF16),
        ((chips, padded, 128), BF16), ((chips, count, padded // count, 128), BF16),
        ((padded, 128), BF16),
        ((lines, 128), BF16), ((shards, lines, 128), BF16),
        ((lines, 128), BF16), ((count, lines, 128), BF16),
    ]
    sems = [
        (4,), (4,), (chips,), (chips,), (chips,), (chips,), (shards,), (shards,),
        (2, UNITS), (2, UNITS), (8,), (chips,), (chips,), (chips, count), (chips, count),
        (2, count), (2, count), (2, shards + count), (2, shards + count),
    ]
    anywhere = spec(pl.ANY)
    outs = pl.pallas_call(
        functools.partial(whole_kernel, shards, count, fold),
        out_shape=[
            jax.ShapeDtypeStruct((SPAN, WIDTH), BF16), jax.ShapeDtypeStruct((SPAN, WIDTH), BF16),
            jax.ShapeDtypeStruct((padded, 128), BF16), jax.ShapeDtypeStruct((lines, 128), F32),
        ],
        in_specs=[spec(pltpu.HBM)] * 4 + [spec(pltpu.VMEM)] * 2,
        scratch_shapes=[pltpu.VMEM(s, t) for s, t in scratch]
        + [pltpu.SemaphoreType.DMA(s) for s in sems],
        compiler_params=pltpu.CompilerParams(
            vmem_limit_bytes=54300 * 1024, collective_id=0, has_side_effects=True
        ),
    )(hidden[0], grad_out[0], w_proj.T, conv_w, a_log[None], dt_bias[None])
    output, grad_hidden, share_w, share_c, grad_heads = pl.pallas_call(
        functools.partial(emit_kernel, shards, fold),
        out_shape=[
            jax.ShapeDtypeStruct((SPAN, WIDTH), BF16), jax.ShapeDtypeStruct((SPAN, WIDTH), BF16),
            jax.ShapeDtypeStruct((columns, rows), F32),
            jax.ShapeDtypeStruct((KERNEL, part), F32), jax.ShapeDtypeStruct((2, HEADS), F32),
        ],
        out_specs=[anywhere] * 2 + [spec(pltpu.VMEM)] * 3,
        scratch_shapes=[
            pltpu.VMEM((wide_rows, 256), F32), pltpu.VMEM((KERNEL, CHANNELS), F32),
            pltpu.SemaphoreType.DMA((2,)),
        ],
        compiler_params=pltpu.CompilerParams(vmem_limit_bytes=8 * 1024 * 1024),
    )(*outs)
    return (output[None], grad_hidden[None], share_w.T, share_c, grad_heads)


def solution(mesh):
    return jax.shard_map(
        per_device,
        mesh=mesh,
        in_specs=(
            P(("grp", "zero"), "seq", None),
            P(("grp", "zero"), "seq", None),
            P("zero", None),
            P(None, "zero"),
            P(),
            P(),
        ),
        out_specs=(
            P(("grp", "zero"), "seq", None),
            P(("grp", "zero"), "seq", None),
            P(("grp", "zero"), None),
            P("grp", "zero"),
            P("grp", None),
        ),
        check_vma=False,
    )
```

```python
import functools
import jax
import jax.numpy as jnp
from jax import lax
from jax.experimental import pallas as pl
from jax.experimental.pallas import tpu as pltpu
from jax.sharding import PartitionSpec as P

WIDTH = 1280
STATE = 64
HEAD_DIM = 64
SPAN = 128
KERNEL = 4
HEADS = 20
PAIRS = WIDTH // 128
CHANNELS = WIDTH + 2 * STATE
EDGE = 8
EXT = SPAN + 2 * EDGE
F32 = jnp.float32
BF16 = jnp.bfloat16
UNITS = 2 * PAIRS
HOP = 6
OFFSET = 5
GROUP = 2
EARLY = 2


def mm(a, b):
    return jnp.dot(a, b, preferred_element_type=F32)


def mm_nt(a, b):
    return lax.dot_general(a, b, (((1,), (1,)), ((), ())), preferred_element_type=F32)


def mm_tn(a, b):
    return lax.dot_general(a, b, (((0,), (0,)), ((), ())), preferred_element_type=F32)


def exact(a, b):
    return jnp.dot(a, b, preferred_element_type=F32, precision=lax.Precision.HIGHEST)


def iota(dim, shape=(128, 128)):
    return lax.broadcasted_iota(jnp.int32, shape, dim)


def mirror(dtype=BF16):
    return jnp.where(iota(0) + iota(1) == 127, 1.0, 0.0).astype(dtype)


def softplus(x):
    return jnp.maximum(x, 0.0) + jnp.log1p(jnp.exp(-jnp.abs(x)))


def sigmoid(x):
    return 0.5 * jnp.tanh(0.5 * x) + 0.5


def shifted(x):
    back = [x[EDGE : EDGE + SPAN]]
    fore = [back[0]]
    for k in range(1, KERNEL):
        back.append(pltpu.roll(x, k, 0)[EDGE : EDGE + SPAN])
        fore.append(pltpu.roll(x, EXT - k, 0)[EDGE : EDGE + SPAN])
    return back, fore


def conv(taps, rows):
    out = taps[0:1] * rows[0]
    for k in range(1, KERNEL):
        out = out + taps[k : k + 1] * rows[k]
    return out


def lanes(i):
    return pl.ds(pl.multiple_of(i * 128, 128), 128)


MESH = pl.DeviceIdType.MESH


def greet_all(shards, count):
    barrier = pltpu.get_barrier_semaphore()
    seq, zero = lax.axis_index("seq"), lax.axis_index("zero")
    total = 0
    for n in range(count):
        for k in range(shards):
            if (k or n) and (n == 0 or k % 2 == 0):
                there = {"zero": lax.rem(zero + k, shards), "seq": lax.rem(seq + n, count)}
                pl.semaphore_signal(barrier, inc=1, device_id=there, device_id_type=MESH)
                total += 1
    return functools.partial(pl.semaphore_wait, barrier, total)


def push(src, dst, send, recv, axis, peer):
    return pltpu.make_async_remote_copy(
        src_ref=src,
        dst_ref=dst,
        send_sem=send,
        recv_sem=recv,
        device_id={axis: peer},
        device_id_type=MESH,
    )


def split2(x):
    hi = x.astype(BF16)
    return hi, (x - hi.astype(F32)).astype(BF16)


def split3(x):
    hi = x.astype(BF16)
    rest = x - hi.astype(F32)
    mid = rest.astype(BF16)
    return hi, mid, (rest - mid.astype(F32)).astype(BF16)


def exact_left(a, x):
    n = x.shape[1]
    out = mm(a, jnp.concatenate(split3(x), axis=1))
    return out[:, :n] + out[:, n : 2 * n] + out[:, 2 * n :]


def exact_right(x, b):
    n = x.shape[0]
    out = mm(jnp.concatenate(split3(x), axis=0), b)
    return out[:n] + out[n : 2 * n] + out[2 * n :]


def ones_where(keep):
    return jnp.where(keep, 1.0, 0.0).astype(BF16)


def one_hot(at_ref, head):
    at = at_ref[...]
    same = at == head.astype(F32).astype(BF16)
    return jnp.where(same, jnp.ones_like(at), jnp.zeros_like(at))


def strand_swap():
    k, lane = iota(0), iota(1)
    return ones_where((lane >= 32) & (lane < 32 + HEADS) & (k + lane == 31 + HEADS))


def folded(tail, fold):
    size = tail.shape[0] // fold
    out = tail[:size]
    for q in range(1, fold):
        out = out + pltpu.roll(tail[q * size : (q + 1) * size], 24 * q, 1)
    return out


def whole_kernel(
    shards, count, fold,
    hid_hbm, go_hbm, wt_hbm, c_hbm, alog_ref, bias_ref,
    out_ref, gh_ref, full, total2,
    hid_ref, go_ref, wt_in, c_in, wt_pad,
    x_ref, xf_ref, xt_ref, taps_ref, wp_ref, w_out, w_rev, w_slots, c_own, c_slots, before, after,
    vals, slope, u_ref, fu_ref, eg_ref, yoff, duo, e_b, f_b, dt_b,
    own, in_slots, out_slots,
    pick_at, sel_at, sum_at, heads_in, rates, dtx_ref, stack, split, within_t, score, diag, bc_act, bc_t, bc_slope, masks,
    d_score, d_diag, d_bc, acc,
    gi_ref, gf_ref, bcx_ref, g_out, g_before, g_after, parts, pair_in, pair_sum, part_in, gathered,
    small, small_in, small2, small2_in,
    local, sides, w_send, w_recv, f_send, f_recv, t_send, t_recv, c_send, c_recv,
    g_sides, p_send, p_recv, zs, zr, ss, sr, ms, mr,
):
    seq, zero = lax.axis_index("seq"), lax.axis_index("zero")
    core = lax.rem(zero, 2)
    chip = lax.div(zero, 2)
    chips = shards // 2
    sibling = zero + 1 - 2 * core
    rows = WIDTH // shards
    fold_rows = rows // fold
    packed = rows + fold_rows
    greeted = greet_all(shards, count)
    loads = [
        pltpu.make_async_copy(src, dst, local.at[n])
        for n, (src, dst) in enumerate(
            ((c_hbm, c_in), (wt_hbm, wt_in), (hid_hbm, hid_ref), (go_hbm, go_ref))
        )
    ]
    for load in loads:
        load.start()
    c_own[...] = jnp.zeros_like(c_own)
    wt_pad[...] = jnp.zeros_like(wt_pad)
    loads[0].wait()
    c_own[:KERNEL] = c_in[...].astype(F32)
    loads[1].wait()
    wt_pad[: wt_in.shape[0], :rows] = wt_in[...].astype(F32)
    w_own = wt_pad[...].T
    w_slots[zero, :rows] = w_own[:rows, :128].astype(BF16)
    w_slots[zero, rows:] = folded(w_own[:rows, 128:], fold).astype(BF16)
    greeted()
    tap_copies = []
    for k in range(1, shards):
        peer = lax.rem(zero + k, shards)
        copy = push(c_own, c_slots.at[zero], t_send.at[k], t_recv.at[k], "zero", peer)
        copy.start()
        tap_copies.append(copy)
    loads[2].wait()
    up = push(
        hid_ref.at[pl.ds(SPAN - 2 * EDGE, 2 * EDGE)], before, sides.at[0], sides.at[1], "seq",
        lax.rem(seq + 1, count),
    )
    down = push(
        hid_ref.at[pl.ds(0, 2 * EDGE)], after, sides.at[2], sides.at[3], "seq",
        lax.rem(seq + count - 1, count),
    )

    @pl.when(seq < count - 1)
    def _():
        up.start()

    @pl.when(seq > 0)
    def _():
        down.start()

    w_copies = []
    for k in range(chips):
        peer = lax.rem(zero + 2 * k, shards) if k else sibling
        copy = push(w_slots.at[zero], w_slots.at[zero], w_send.at[k], w_recv.at[k], "zero", peer)
        copy.start()
        w_copies.append(copy)
    c_slots[zero] = c_own[...]
    w_out[:, 128:] = jnp.zeros((WIDTH, 128), BF16)
    x_ref[EDGE : EDGE + SPAN] = hid_ref[...]
    flip = mirror()
    swap = strand_swap()
    masks[0] = ones_where(iota(0) > iota(1))
    masks[1] = ones_where(iota(0) < iota(1))
    if parts.shape[1] > packed:
        spare = (shards, parts.shape[1] - packed, 128)
        parts[:, packed:] = jnp.zeros(spare, BF16)
    square = (256, 256)
    line, lane = iota(0, square), iota(1, square)
    pick_at[...] = jnp.where(
        line < 192, lax.rem(line, 64) - jnp.where(lane >= 128, 1, 0), -2
    ).astype(F32).astype(BF16)
    wide_shape = (128, 256 * GROUP)
    line, lane = iota(0, wide_shape), iota(1, wide_shape)
    sel_at[...] = (
        lax.rem(line, 64)
        - 2 * lax.div(lane, 256)
        - jnp.where(lax.rem(lane, 256) >= 128, 32, 0)
        - jnp.where(lax.rem(lane, 128) >= HEAD_DIM, 1, 0)
    ).astype(F32).astype(BF16)
    tall = (512, 128)
    line, lane = iota(0, tall), iota(1, tall)
    sum_at[...] = (
        lane
        - jnp.where(line >= 256, 32, 0)
        - jnp.where(lax.rem(line, 128) >= HEAD_DIM, 1, 0)
    ).astype(F32).astype(BF16)
    d_score[...] = jnp.zeros_like(d_score)
    d_diag[...] = jnp.zeros_like(d_diag)
    d_bc[...] = jnp.zeros_like(d_bc)
    acc[...] = jnp.zeros_like(acc)

    @pl.when(seq == 0)
    def _():
        x_ref[:EDGE] = jnp.zeros((EDGE, WIDTH), BF16)
        in_slots[0] = jnp.zeros(in_slots.shape[1:], BF16)

    @pl.when(seq > 0)
    def _():
        up.wait_recv()
        x_ref[:EDGE] = before[EDGE:]

    @pl.when(seq == count - 1)
    def _():
        x_ref[EDGE + SPAN :] = jnp.zeros((EDGE, WIDTH), BF16)
        in_slots[1] = jnp.zeros(in_slots.shape[1:], BF16)

    @pl.when(seq < count - 1)
    def _():
        down.wait_recv()
        x_ref[EDGE + SPAN :] = after[:EDGE]

    for copy in tap_copies:
        copy.wait()
    part = c_own.shape[1]
    for z in range(shards):
        taps_ref[0, :, z * part : (z + 1) * part] = c_slots[z]
    for b in range(PAIRS):
        taps_ref[1, :, b * 128 : (b + 1) * 128] = mm(
            taps_ref[0, :, (PAIRS - 1 - b) * 128 : (PAIRS - b) * 128].astype(BF16), flip
        )

    def values_of(i):
        rows = shifted(x_ref[:, lanes(i)].astype(F32))
        for s in range(2):
            taps = taps_ref[s, :, lanes(i)]
            for d in range(2):
                mixed = conv(taps, rows[d])
                sig = sigmoid(mixed)
                act = mixed * sig
                vals[2 * i + s, d] = act.astype(BF16)
                slope[2 * i + s, d] = sig + act * (1.0 - sig)

    def values_step(i, carry):
        values_of(i)
        return carry

    for b in range(PAIRS):
        xf_ref[:, (PAIRS - 1 - b) * 128 : (PAIRS - b) * 128] = mm(
            x_ref[:, b * 128 : (b + 1) * 128], flip
        ).astype(BF16)
    lax.fori_loop(0, EARLY, values_step, 0)

    for copy in w_copies:
        copy.wait()
    forwards = []
    for k in range(1, chips):
        slot_of = w_slots.at[lax.rem(zero + shards - 2 * k, shards)]
        copy = push(slot_of, slot_of, f_send.at[k], f_recv.at[k], "zero", sibling)
        copy.start()
        forwards.append(copy)

    def unpack(z):
        at = pl.multiple_of(z * rows, 16)
        w_out[pl.ds(at, rows), :128] = w_slots[z, :rows]
        tail = w_slots[z, rows:].astype(F32)
        for q in range(fold):
            moved = pltpu.roll(tail, 128 - 24 * q, 1) if q else tail
            w_out[pl.ds(at + q * fold_rows, fold_rows), 128:] = jnp.where(
                iota(1, (fold_rows, 128)) < HEADS, moved, 0.0
            ).astype(BF16)

    for k in range(chips):
        unpack(lax.rem(zero + shards - 2 * k, shards))
    unpack(sibling)
    for copy in forwards:
        copy.wait()
    for k in range(1, chips):
        unpack(lax.rem(sibling + shards - 2 * k, shards))
    wp_ref[:, :128] = w_out[:, :128]
    wp_ref[:, 128:] = mm(w_out[:, 128:], swap).astype(BF16)
    proj = (mm(x_ref[...], w_out[...]), mm(xf_ref[...], wp_ref[...]))
    loads[3].wait()
    heads_in[...] = jnp.zeros_like(heads_in)
    heads_in[0:1, :HEADS] = alog_ref[...]
    heads_in[1:2, :HEADS] = bias_ref[...]
    place = heads_in[...] + exact_right(heads_in[...], swap)
    rate = jnp.exp(place[0:1])
    rates[0:1] = rate
    dtx = (proj[0] + proj[1])[EDGE : EDGE + SPAN, 128:] + place[1:2]
    dtx_ref[...] = dtx
    delta = softplus(dtx)
    both = jnp.concatenate(
        [ones_where(iota(0) >= iota(1)), ones_where(iota(0) <= iota(1))], axis=0
    )
    within = exact_left(both, -rate * delta)
    ends = jnp.concatenate(
        [
            jnp.broadcast_to(within[SPAN - 1 : SPAN], (SPAN, 128)),
            jnp.broadcast_to(within[SPAN : SPAN + 1], (SPAN, 128)),
        ],
        axis=0,
    )
    spread = jnp.concatenate([jnp.exp(within), jnp.exp(ends - within), delta], axis=0)
    hi, lo = split2(spread)
    wide_low = iota(1, spread.shape) < 64
    stack[...] = jnp.where(
        wide_low, hi.astype(F32), pltpu.roll(lo.astype(F32), 64, 1)
    ).astype(BF16)
    hi, mid, lo = split3(within)
    low_two = iota(1, (256, 128)) < 64
    split[:, :128] = jnp.where(
        low_two, hi.astype(F32), pltpu.roll(mid.astype(F32), 64, 1)
    ).astype(BF16)
    split[:, 128:] = jnp.where(low_two, lo.astype(F32), 0.0).astype(BF16)
    for d in range(2):
        within_t[d] = within[d * 128 : d * 128 + 128].T
    for s in range(2):
        bcx_ref[s] = proj[s][:, :128].astype(BF16).astype(F32)
        bcx = shifted(bcx_ref[s])
        for d in range(2):
            c = 2 * s + d
            mixed = conv(taps_ref[0, :, WIDTH:], bcx[d])
            sig = sigmoid(mixed)
            wide = mixed * sig
            act = wide.astype(BF16)
            bc_slope[c] = sig + wide * (1.0 - sig)
            bc_act[c, 0] = act[:, :STATE]
            bc_act[c, 1] = act[:, STATE:]
            act_t = act.astype(F32).T.astype(BF16)
            bc_t[c] = act_t

    def make_scores():
        for s in range(2):
            scores = []
            for d in range(2):
                c = 2 * s + d
                scores.append(mm(bc_act[c, 1], bc_t[c, :STATE]))
                own_diag = jnp.sum(
                    jnp.where(iota(0) == iota(1), scores[d], 0.0), axis=1, keepdims=True
                )
                diag[c] = jnp.broadcast_to(own_diag, (128, 128))
            score[s] = jnp.where(
                iota(0) > iota(1), scores[0], jnp.where(iota(0) < iota(1), scores[1], 0.0)
            )

    def produce(t):
        all_wide = mm(stack[...], one_hot(sel_at, 2 * GROUP * t))
        for n in range(GROUP):
            g = go_ref[:, lanes(GROUP * t + n)].astype(F32)
            for s in range(2):
                u = 2 * GROUP * t + 2 * n + s
                at = 256 * n + 128 * s
                wide = all_wide[:, at : at + 128]
                dt = wide[512:]
                dt_b[u] = dt
                for d in range(2):
                    e, f = wide[128 * d : 128 * d + 128], wide[256 + 128 * d : 384 + 128 * d]
                    e_b[u, d] = e
                    f_b[u, d] = f
                    step = (vals[u, d].astype(F32) * dt).astype(BF16)
                    u_ref[u, d] = step
                    fu = (step.astype(F32) * f).astype(BF16)
                    fu_ref[u, d] = fu
                    eg = (e * g).astype(BF16)
                    eg_ref[u, d] = eg
                    own[d, u, 0] = mm(bc_t[2 * s + d, :STATE], fu)
                    own[1 - d, u, 1] = mm(bc_t[2 * s + d, STATE:], eg)

    def decay_of(u, d):
        at = SPAN - 1 if d == 0 else 0
        return e_b[u, d, at : at + 1]

    chains = ((0, seq, seq + 1), (1, count - 1 - seq, seq - 1))

    def copy_of(d, u, peer):
        return push(
            out_slots.at[d, u], in_slots.at[d, u], c_send.at[d, u], c_recv.at[d, u], "seq", peer
        )

    def send_first(t):
        for d, place, peer in chains:

            @pl.when(place == 0)
            def _():
                for n in range(2 * GROUP):
                    u = 2 * GROUP * t + n
                    out_slots[d, u] = own[d, u].astype(BF16)
                    copy_of(d, u, peer).start()

    def forward(n):
        for d, place, peer in chains:
            u = n - OFFSET - HOP * place

            @pl.when((place > 0) & (place < count - 1) & (u >= 0) & (u < UNITS))
            def _():
                copy_of(d, u, seq).wait_recv()
                for q in range(2):
                    dec = decay_of(u, d if q == 0 else 1 - d)
                    out_slots[d, u, q] = (
                        own[d, u, q] + dec * in_slots[d, u, q].astype(F32)
                    ).astype(BF16)
                copy_of(d, u, peer).start()

    def arrive(i):
        for d, place, peer in chains:

            @pl.when(place == count - 1)
            def _():
                for s in range(2):
                    copy_of(d, 2 * i + s, seq).wait_recv()

    def inside(i):
        lower = iota(0) >= iota(1)
        low = iota(1) < HEAD_DIM
        go = go_ref[:, lanes(i)]
        g = go.astype(F32)
        none = jnp.zeros((128, 128), BF16)
        g_two = jnp.concatenate([jnp.where(low, go, none), jnp.where(low, none, go)], axis=0)
        kept_ins = []
        for s in range(2):
            u = 2 * i + s
            head = 32 * s + 2 * i
            cols = mm(split[...], one_hot(pick_at, head))
            steps = jnp.concatenate([u_ref[u, 0], u_ref[u, 1]], axis=0)
            dw = mm_nt(g_two, steps)
            sc = score[s]
            ds = jnp.zeros((128, 128), F32)
            below, above = [], []
            for r in range(2):
                at = slice(128 * r, 128 * r + 128)
                gap = jnp.where(
                    lower,
                    cols[:128, at] - within_t[0, pl.ds(head + r, 1), :],
                    cols[128:, at] - within_t[1, pl.ds(head + r, 1), :],
                )
                decay = jnp.exp(gap)
                w = (sc * decay).astype(BF16)
                below.append(w * masks[0])
                above.append(w * masks[1])
                ds = ds + decay * jnp.where(lower, dw[at, :128], dw[at, 128:])
            for d, ws in enumerate((below, above)):
                step = steps[128 * d : 128 * d + 128]
                y_two = mm(jnp.concatenate(ws, axis=0), step)
                kept_ins.append(
                    (
                        jnp.where(low, y_two[:128], y_two[128:]),
                        jnp.where(low, mm_tn(ws[0], go), mm_tn(ws[1], go)),
                        g * step.astype(F32),
                    )
                )
            kept_ins.append(ds)
        for s in range(2):
            for d in range(2):
                y_two, du, on_diag = kept_ins[3 * s + d]
                yoff[2 * i + s, d] = y_two
                duo[2 * i + s, d] = du
                d_diag[2 * s + d] += on_diag
            d_score[s] += kept_ins[3 * s + 2]

    def back(taps, dms, x):
        zero_rows = jnp.zeros((EDGE, 128), F32)
        wides = [jnp.concatenate([zero_rows, dm, zero_rows], axis=0) for dm in dms]
        both = wides[0] + wides[1]
        out = taps[0:1] * both
        sums = [jnp.sum(both * x, axis=0, keepdims=True)]
        for k in range(1, KERNEL):
            both = pltpu.roll(wides[0], EXT - k, 0) + pltpu.roll(wides[1], k, 0)
            out = out + taps[k : k + 1] * both
            sums.append(jnp.sum(both * x, axis=0, keepdims=True))
        return out, jnp.concatenate(sums + [jnp.zeros((8 - KERNEL, 128), F32)], axis=0)

    def finish(i):
        g = go_ref[:, lanes(i)].astype(F32)
        x = x_ref[:, lanes(i)].astype(F32)
        sel_t = one_hot(sum_at, 2 * i)
        ys, parts_of, adds = [], [], []
        for s in range(2):
            u = 2 * i + s
            taps = taps_ref[s, :, lanes(i)]
            dt = dt_b[u]
            y = jnp.zeros((128, 128), F32)
            dms = []
            qt = jnp.zeros((128, 128), F32)
            qs, ends = [], []
            for d in range(2):
                c = 2 * s + d
                s_in, g_in = in_slots[d, u, 0], in_slots[1 - d, u, 1]
                step = u_ref[u, d].astype(F32)
                across = mm(bc_act[c, 1], s_in) * e_b[u, d] + yoff[u, d]
                y = y + across + diag[c] * step
                du = duo[u, d] + f_b[u, d] * mm(bc_act[c, 0], g_in)
                qs.append(g * across - step * du)
                du = du + diag[c] * g
                qt = qt + vals[u, d].astype(F32) * du
                adds.append((c, mm_nt(fu_ref[u, d], g_in), mm_nt(eg_ref[u, d], s_in)))
                leaving = own[d, u, 0] + decay_of(u, d) * s_in.astype(F32)
                ends.append(jnp.sum(leaving * g_in.astype(F32), axis=0, keepdims=True))
                dms.append((dt * du).astype(BF16).astype(F32) * slope[u, d])
            gi, gf = back(taps, dms, x)
            q = jnp.concatenate(qs + [qt] + ends + [jnp.zeros((6, 128), F32)], axis=0)
            parts_of.extend(split2(q))
            ys.append(y.astype(BF16).astype(F32))
            adds.append((s, gi, gf))
        totals = mm(jnp.concatenate(parts_of, axis=1), sel_t)
        for s in range(2):
            for c, db, dc in adds[3 * s : 3 * s + 2]:
                d_bc[c, 0] += db
                d_bc[c, 1] += dc
            _, gi, gf = adds[3 * s + 2]
            gi_ref[s, :, lanes(i)] = gi
            gf_ref[2 * i + s] = gf
        acc[...] += totals
        out_ref[:, lanes(i)] = (ys[0] + ys[1]).astype(BF16)

    groups = PAIRS // GROUP

    def first_part(t, carry):
        produce(t)
        send_first(t)
        return carry

    early = EARLY // GROUP

    def late_part(t, carry):
        for n in range(GROUP):
            values_of(GROUP * t + n)
        first_part(t, carry)
        for n in range(3):
            forward(3 * (t - early) + 3 + n)
        return carry

    before_second = 3 * (groups - early) + 3

    def second_part(i, carry):
        for n in range(GROUP):
            b = GROUP * i + n
            xt_ref[0, lanes(b)] = x_ref[:, lanes(b)].astype(F32).T.astype(BF16)
            xt_ref[1, lanes(b)] = xf_ref[:, lanes(b)].astype(F32).T.astype(BF16)
            w_rev[lanes(b)] = mm(flip, w_out[lanes(PAIRS - 1 - b)]).astype(BF16)
            inside(b)
        for n in range(GROUP):
            forward(before_second + GROUP * i + n)
        return carry

    def idle(n, carry):
        forward(n)
        return carry

    before_third = before_second + PAIRS
    began = max(before_third, 2 + OFFSET + HOP * (count - 2))

    def third_part(i, carry):
        forward(began + 2 * i)
        forward(began + 2 * i + 1)
        arrive(i)
        finish(i)
        return carry

    lax.fori_loop(0, early, first_part, 0)
    lax.fori_loop(early, groups, late_part, 0)
    make_scores()
    lax.fori_loop(0, groups, second_part, 0)
    if began > before_third:
        lax.fori_loop(before_third, began, idle, 0)
    lax.fori_loop(0, PAIRS, third_part, 0)

    halos = []
    for n, at in enumerate((pl.ds(0, WIDTH), pl.ds(WIDTH, 128))):
        halos.append(
            (
                push(
                    g_out.at[0, :, at], g_before.at[:, at],
                    g_sides.at[4 * n], g_sides.at[4 * n + 1], "seq", lax.rem(seq + 1, count),
                ),
                push(
                    g_out.at[1, :, at], g_after.at[:, at],
                    g_sides.at[4 * n + 2], g_sides.at[4 * n + 3], "seq",
                    lax.rem(seq + count - 1, count),
                ),
            )
        )

    def send_edges(at, halo):
        for side, start in ((0, EDGE + SPAN), (1, 0)):
            g_out[side, :, at] = jnp.concatenate(
                [gi_ref[s, start : start + EDGE, at] for s in range(2)], axis=0
            ).astype(BF16)

        @pl.when(seq < count - 1)
        def _():
            halo[0].start()

        @pl.when(seq > 0)
        def _():
            halo[1].start()

    send_edges(slice(0, WIDTH), halos[0])
    end_rows = acc[3 * SPAN : 3 * SPAN + 8]
    dl0 = acc[:SPAN] + jnp.where(iota(0) == SPAN - 1, end_rows[0:1], 0.0)
    dl1 = acc[SPAN : 2 * SPAN] + jnp.where(iota(0) == 0, end_rows[1:2], 0.0)
    both_t = jnp.concatenate(
        [ones_where(iota(0) <= iota(1)), ones_where(iota(0) >= iota(1))], axis=1
    )
    d_log = exact_left(both_t, jnp.concatenate([dl0, dl1], axis=0))
    rate = rates[0:1]
    dtx = dtx_ref[...]
    d_raw = (acc[2 * SPAN : 3 * SPAN] - rate * d_log) * sigmoid(dtx)
    line, lane = iota(0), iota(1)
    unswap = ones_where((line >= 32) & (line < 32 + HEADS) & (line + lane == 31 + HEADS))
    ddt = (
        jnp.where(iota(1) < HEADS, d_raw, 0.0).astype(BF16),
        mm(d_raw.astype(BF16), unswap).astype(BF16),
    )
    wides = []
    for s in range(2):
        taps = taps_ref[0, :, WIDTH:]
        dms = []
        for d in range(2):
            c = 2 * s + d
            on_diag = jnp.sum(d_diag[c], axis=1, keepdims=True)
            off = iota(0) > iota(1) if d == 0 else iota(0) < iota(1)
            ds = jnp.where(
                off, d_score[s], jnp.where(iota(0) == iota(1), on_diag, 0.0)
            ).astype(BF16)
            db = d_bc[c, 0] + mm_tn(ds, bc_act[c, 1])
            dc = d_bc[c, 1] + mm(ds, bc_act[c, 0])
            dms.append(jnp.concatenate([db, dc], axis=1).astype(BF16).astype(F32) * bc_slope[c])
        gi, gf = back(taps, dms, bcx_ref[s])
        gi_ref[s, :, WIDTH:] = gi
        gf_ref[UNITS + s] = gf
        edge = jnp.zeros((EDGE, 128), F32)
        wides.append(
            jnp.concatenate(
                [gi, jnp.concatenate([edge, ddt[s].astype(F32), edge], axis=0)], axis=1
            ).astype(BF16)
        )
    send_edges(slice(WIDTH, CHANNELS), halos[1])

    def weight_parts(zs):
        totals = []
        for z in zs:
            at = pl.ds(pl.multiple_of(z * rows, 16), rows)
            totals.append(mm(xt_ref[0, at], wides[0]) + mm(xt_ref[1, at], wides[1]))
        for z, total in zip(zs, totals):
            parts[z, :rows] = total[:, :128].astype(BF16)
            parts[z, rows:packed] = folded(total[:, 128:], fold).astype(BF16)

    order = list(range(1, chips)) + [0]
    theirs = [2 * lax.rem(chip + k, chips) + 1 - core for k in order]
    weight_parts(theirs)
    pairs = []
    for k, z in zip(order, theirs):
        copy = push(
            parts.at[z], pair_in.at[lax.div(z, 2)], p_send.at[k], p_recv.at[k], "zero", sibling
        )
        copy.start()
        pairs.append(copy)
    weight_parts([2 * lax.rem(chip + k, chips) + core for k in order])

    @pl.when(seq == 0)
    def _():
        g_before[...] = jnp.zeros_like(g_before)

    @pl.when(seq == count - 1)
    def _():
        g_after[...] = jnp.zeros_like(g_after)

    chunk = gathered.shape[0] // count
    here = pl.ds(pl.multiple_of(seq * chunk, 16), chunk)
    scatter = []
    for k in list(range(1, chips)) + [0]:
        there = lax.rem(chip + k, chips)
        pairs[k - 1].wait()
        pair_sum[there] = (
            parts[2 * there + core].astype(F32) + pair_in[there].astype(F32)
        ).astype(BF16)
        for n in range(count):
            if k or n:
                peer = lax.rem(seq + n, count)
                copy = pltpu.make_async_remote_copy(
                    src_ref=pair_sum.at[there, pl.ds(pl.multiple_of(peer * chunk, 16), chunk)],
                    dst_ref=part_in.at[k, n],
                    send_sem=zs.at[k, n],
                    recv_sem=zr.at[k, n],
                    device_id={"zero": 2 * there + core, "seq": peer},
                    device_id_type=MESH,
                )
                copy.start()
                scatter.append(copy)
    sums = jnp.concatenate(
        [
            jnp.sum(d_log * (-rate * softplus(dtx)), axis=0, keepdims=True),
            jnp.sum(d_raw, axis=0, keepdims=True),
            jnp.zeros((6, 128), F32),
        ],
        axis=0,
    )
    heads = jnp.where(iota(1, (8, 128)) < HEADS, sums, 0.0) + exact_right(sums, unswap)
    swapped = exact_right(
        jnp.concatenate([gf_ref[2 * (PAIRS - 1 - i) + 1] for i in range(PAIRS)], axis=0), flip
    )
    blocks = [
        (gf_ref[2 * i] + swapped[8 * i : 8 * i + 8])[:KERNEL] for i in range(PAIRS)
    ] + [(gf_ref[UNITS] + gf_ref[UNITS + 1])[:KERNEL]]
    head_hi = heads[:2].astype(BF16).astype(F32)
    small[...] = jnp.concatenate(blocks + [head_hi, heads[:2] - head_hi], axis=0).astype(BF16)
    first = []
    for k in range(1, shards):
        peer = lax.rem(zero + k, shards)
        copy = push(small, small_in.at[zero], ms.at[0, k], mr.at[0, k], "zero", peer)
        copy.start()
        first.append(copy)
    small_in[zero] = small[...]

    @pl.when(seq > 0)
    def _():
        for halo in halos:
            halo[0].wait_recv()

    @pl.when(seq < count - 1)
    def _():
        for halo in halos:
            halo[1].wait_recv()

    def settled(s, at):
        near = slice(EDGE * s, EDGE * s + EDGE)
        top = gi_ref[s, EDGE : 2 * EDGE, at] + g_before[:, at].astype(F32)[near]
        low = gi_ref[s, SPAN : SPAN + EDGE, at] + g_after[:, at].astype(F32)[near]
        return jnp.concatenate([top, gi_ref[s, 2 * EDGE : SPAN, at], low], axis=0).astype(BF16)

    gps = [
        jnp.concatenate([settled(s, slice(WIDTH, CHANNELS)), ddt[s]], axis=1) for s in range(2)
    ]

    def hidden_part(i):
        at = slice(i * 128, i * 128 + 128)
        a = (settled(0, at).astype(F32) + mm_nt(gps[0], w_out[at])).astype(BF16)
        b = (settled(1, at).astype(F32) + mm_nt(gps[1], w_rev[at])).astype(BF16)
        gh_ref[:, at] = (a.astype(F32) + b.astype(F32)).astype(BF16)

    for i in range(PAIRS // 2):
        hidden_part(i)
    for copy in first:
        copy.wait()
    summed = small_in[0].astype(F32)
    for z in range(1, shards):
        summed = summed + small_in[z].astype(F32)
    last = KERNEL * (PAIRS + 1)
    heads = summed[last : last + 2] + summed[last + 2 : last + 4]
    head_hi = heads.astype(BF16).astype(F32)
    small2[...] = jnp.concatenate([summed[:last], head_hi, heads - head_hi], axis=0).astype(BF16)
    second = []
    for k in range(1, count):
        peer = lax.rem(seq + k, count)
        copy = push(small2, small2_in.at[seq], ms.at[1, shards + k], mr.at[1, shards + k], "seq", peer)
        copy.start()
        second.append(copy)
    small2_in[seq] = small2[...]
    for copy in scatter:
        copy.wait()
    summed = parts[zero, here].astype(F32) + pair_in[chip, here].astype(F32)
    for k in range(chips):
        for n in range(count):
            if k or n:
                summed = summed + part_in[k, n].astype(F32)
    gathered[here] = summed.astype(BF16)
    third = []
    for k in range(1, count):
        peer = lax.rem(seq + k, count)
        copy = push(gathered.at[here], gathered.at[here], ss.at[1, k], sr.at[1, k], "seq", peer)
        copy.start()
        third.append(copy)
    for i in range(PAIRS // 2, PAIRS):
        hidden_part(i)
    for copy in second:
        copy.wait()
    summed = small2_in[0].astype(F32)
    for z in range(1, count):
        summed = summed + small2_in[z].astype(F32)
    total2[...] = summed
    for d, place, peer in chains:

        @pl.when(place < count - 1)
        def _():
            def sent(u, carry):
                copy_of(d, u, peer).wait_send()
                return carry

            lax.fori_loop(0, UNITS, sent, 0)

    @pl.when(seq < count - 1)
    def _():
        up.wait_send()

    @pl.when(seq > 0)
    def _():
        down.wait_send()

    @pl.when(seq < count - 1)
    def _():
        for halo in halos:
            halo[0].wait_send()

    @pl.when(seq > 0)
    def _():
        for halo in halos:
            halo[1].wait_send()

    for copy in third:
        copy.wait()
    full[...] = gathered[...]


def emit_kernel(
    shards, fold, out_ref, gh_ref, full, total, out_hbm, gh_hbm, gw_ref, gc_ref, gd_ref,
    wide, taps, sems,
):
    copies = [
        pltpu.make_async_copy(out_ref, out_hbm, sems.at[0]),
        pltpu.make_async_copy(gh_ref, gh_hbm, sems.at[1]),
    ]
    for copy in copies:
        copy.start()
    rows = WIDTH // shards
    fold_rows = rows // fold
    tail = full[rows : rows + fold_rows].astype(F32)
    wide[...] = jnp.zeros_like(wide)
    wide[:rows, :128] = full[:rows].astype(F32)
    for q in range(fold):
        moved = pltpu.roll(tail, 128 - 24 * q, 1) if q else tail
        wide[q * fold_rows : (q + 1) * fold_rows, 128:] = moved
    gw_ref[...] = wide[...].T[: gw_ref.shape[0], :rows]
    last = KERNEL * (PAIRS + 1)
    gd_ref[...] = total[last : last + 2, :HEADS] + total[last + 2 : last + 4, :HEADS]
    for i in range(PAIRS + 1):
        taps[:, i * 128 : i * 128 + 128] = total[KERNEL * i : KERNEL * i + KERNEL]
    zero = lax.axis_index("zero")
    width = gc_ref.shape[1]
    for z in range(shards):

        @pl.when(zero == z)
        def _():
            gc_ref[...] = taps[:, z * width : (z + 1) * width]

    for copy in copies:
        copy.wait()


def spec(space):
    return pl.BlockSpec(memory_space=space)


SQ4 = (4, 128, 128)
SQ2 = (2, 128, 128)
TILES = (UNITS, 2, 128, 128)


def per_device(hidden, grad_out, w_proj, conv_w, a_log, dt_bias):
    assert hidden.shape[:2] == (1, SPAN)
    count, shards = lax.axis_size("seq"), lax.axis_size("zero")
    chips = shards // 2
    rows, columns = w_proj.shape
    part = CHANNELS // shards
    fold = 5 if rows % 80 == 0 else 1
    packed = rows + rows // fold
    step = 16 * count
    padded = -(-packed // step) * step
    lines = 48
    wide_rows = -(-rows // 128) * 128
    pieces = (2, UNITS, 2, STATE, 128)
    edges = (2 * EDGE, CHANNELS)
    scratch = [
        ((SPAN, WIDTH), BF16), ((SPAN, WIDTH), BF16), ((columns, rows), BF16),
        ((KERNEL, part), BF16), ((256, wide_rows), F32),
        ((EXT, WIDTH), BF16), ((EXT, WIDTH), BF16), ((2, WIDTH, EXT), BF16),
        ((2, 8, CHANNELS), F32), ((WIDTH, 256), BF16), ((WIDTH, 256), BF16), ((WIDTH, 256), BF16),
        ((shards, packed, 128), BF16), ((8, part), F32), ((shards, 8, part), F32),
        ((2 * EDGE, WIDTH), BF16), ((2 * EDGE, WIDTH), BF16),
        (TILES, BF16), (TILES, F32), (TILES, BF16), (TILES, BF16), (TILES, BF16),
        (TILES, F32), (TILES, F32), (TILES, F32), (TILES, F32), ((UNITS, 128, 128), F32),
        (pieces, F32), (pieces, BF16), (pieces, BF16),
        ((256, 256), BF16), ((128, 256 * GROUP), BF16), ((512, 128), BF16),
        ((8, 128), F32), ((8, 128), F32), ((128, 128), F32), ((5 * 128, 128), BF16), ((256, 256), BF16),
        (SQ2, F32), (SQ2, F32), (SQ4, F32), ((4, 2, 128, STATE), BF16), (SQ4, BF16),
        (SQ4, F32), (SQ2, BF16), (SQ2, F32), (SQ4, F32), ((4, 2, 128, STATE), F32),
        ((3 * SPAN + 8, 128), F32),
        ((2, EXT, CHANNELS), F32), ((UNITS + 2, 8, 128), F32), ((2, EXT, 128), F32),
        ((2,) + edges, BF16), (edges, BF16), (edges, BF16),
        ((shards, padded, 128), BF16), ((chips, padded, 128), BF16),
        ((chips, padded, 128), BF16), ((chips, count, padded // count, 128), BF16),
        ((padded, 128), BF16),
        ((lines, 128), BF16), ((shards, lines, 128), BF16),
        ((lines, 128), BF16), ((count, lines, 128), BF16),
    ]
    sems = [
        (4,), (4,), (chips,), (chips,), (chips,), (chips,), (shards,), (shards,),
        (2, UNITS), (2, UNITS), (8,), (chips,), (chips,), (chips, count), (chips, count),
        (2, count), (2, count), (2, shards + count), (2, shards + count),
    ]
    anywhere = spec(pl.ANY)
    outs = pl.pallas_call(
        functools.partial(whole_kernel, shards, count, fold),
        out_shape=[
            jax.ShapeDtypeStruct((SPAN, WIDTH), BF16), jax.ShapeDtypeStruct((SPAN, WIDTH), BF16),
            jax.ShapeDtypeStruct((padded, 128), BF16), jax.ShapeDtypeStruct((lines, 128), F32),
        ],
        in_specs=[spec(pltpu.HBM)] * 4 + [spec(pltpu.VMEM)] * 2,
        scratch_shapes=[pltpu.VMEM(s, t) for s, t in scratch]
        + [pltpu.SemaphoreType.DMA(s) for s in sems],
        compiler_params=pltpu.CompilerParams(
            vmem_limit_bytes=54300 * 1024, collective_id=0, has_side_effects=True
        ),
    )(hidden[0], grad_out[0], w_proj.T, conv_w, a_log[None], dt_bias[None])
    output, grad_hidden, share_w, share_c, grad_heads = pl.pallas_call(
        functools.partial(emit_kernel, shards, fold),
        out_shape=[
            jax.ShapeDtypeStruct((SPAN, WIDTH), BF16), jax.ShapeDtypeStruct((SPAN, WIDTH), BF16),
            jax.ShapeDtypeStruct((columns, rows), F32),
            jax.ShapeDtypeStruct((KERNEL, part), F32), jax.ShapeDtypeStruct((2, HEADS), F32),
        ],
        out_specs=[anywhere] * 2 + [spec(pltpu.VMEM)] * 3,
        scratch_shapes=[
            pltpu.VMEM((wide_rows, 256), F32), pltpu.VMEM((KERNEL, CHANNELS), F32),
            pltpu.SemaphoreType.DMA((2,)),
        ],
        compiler_params=pltpu.CompilerParams(vmem_limit_bytes=8 * 1024 * 1024),
    )(*outs)
    return (output[None], grad_hidden[None], share_w.T, share_c, grad_heads)


def solution(mesh):
    return jax.shard_map(
        per_device,
        mesh=mesh,
        in_specs=(
            P(("grp", "zero"), "seq", None),
            P(("grp", "zero"), "seq", None),
            P("zero", None),
            P(None, "zero"),
            P(),
            P(),
        ),
        out_specs=(
            P(("grp", "zero"), "seq", None),
            P(("grp", "zero"), "seq", None),
            P(("grp", "zero"), None),
            P("grp", "zero"),
            P("grp", None),
        ),
        check_vma=False,
    )
```
